256 devices in a mesh: ctx: 64 (over x_lo, z, y), head: 4 (over x_hi, core).
Axes of the slice: x: 4 (x_hi: 2, x_lo: 2; x = x_hi * 2 + x_lo), y: 4, z: 8, core: 2. Of those that a mesh axis runs over, the one named last changes fastest.
Arguments:
- frozen_queries: bfloat16 [16384, 2048], P('ctx', 'head'), may hold values from -70 to 70
- key_value_rows: bfloat16 [16384, 512], P('ctx'), may hold values from -4.5 to 4.5
- output_gradient: bfloat16 [16384, 2048], P('ctx', 'head'), may hold values from -6 to 6
- inputs: bfloat16 [16384, 8192], P('ctx', 'head'), may hold values from -6 to 6
- adapter_down: float32 [64, 8192], P('ctx', 'head'), may hold values from -0.0625 to 0.0625
- down_first_moment: float32 [64, 8192], P('ctx', 'head'), may hold values from -6 to 6
- down_second_moment: float32 [64, 8192], P('ctx', 'head'), may hold values from 0.5 to 8
- adapter_up: float32 [64, 2048], P('ctx', 'head'), may hold values from -0.75 to 0.75
- up_first_moment: float32 [64, 2048], P('ctx', 'head'), may hold values from -6 to 6
- up_second_moment: float32 [64, 2048], P('ctx', 'head'), may hold values from 0.5 to 8
- rank_keep_mask: int32 [2, 64], replicated, may hold values 0 or 1
- group_length: int32 [2], replicated, may hold values from 512 to 2048, as said below
- group_shift: int32 [2], replicated, may hold values from 1 to 2047
Outputs:
- attention_out: bfloat16 [16384, 2048], P('ctx', 'head')
- query_gradient: bfloat16 [16384, 2048], P('ctx', 'head')
- kv_grad: float32 [16384, 512], P('ctx', 'head')
- updated_down: float32 [64, 8192], P('ctx', 'head')
- updated_down_first: float32 [64, 8192], P('ctx', 'head')
- updated_down_second: float32 [64, 8192], P('ctx', 'head')
- updated_up: float32 [64, 2048], P('ctx', 'head')
- updated_up_first: float32 [64, 2048], P('ctx', 'head')
- updated_up_second: float32 [64, 2048], P('ctx', 'head')
The draws below stay inside these ranges and needn't reach their ends.
Inputs may be any that keep to these rules, and one draw needn't show every extreme that they name: `group_length`: each key-value head's group holds 2048 rolled positions or fewer, and in every draw some head's group holds exactly 2048.
All inputs are finite; a program needn't handle non-finite values.
Results may differ from the reference program's by a relative error of at most 0.012.
Values may be sent and summed in bfloat16 or wider, within the bound.
No kernel may reach another device: no remote copies, remote signals or barrier semaphores. Data moves between devices by JAX's collectives and lax.ppermute only.
A program may use at most 64 MiB of HBM per device.

```python
import math
import jax
import jax.numpy as jnp
from jax import lax

MODEL_WIDTH = 8192
LOCAL_HEADS = 16
KVH = 2
HEAD_SIZE = 128
ADAPTER_RANK = 64
TOK_DEV = 256
TOKENS = 16384
REACH = 8
GROUP = 2048
N_CTX = 64


def pair_table(key):
    shape_all = (TOKENS, 2 * KVH * HEAD_SIZE)
    table = jax.random.truncated_normal(jax.random.fold_in(key, 7003), -4.0, 4.0, shape_all, jnp.float32)
    return table


def draw_key_value_rows(key, part):
    return pair_table(key).astype(jnp.bfloat16)


def draw_frozen_queries(key, part):
    shape_all = (TOKENS, LOCAL_HEADS * HEAD_SIZE)
    base = jax.random.truncated_normal(jax.random.fold_in(key, 7005), -4.0, 4.0, shape_all, jnp.float32)
    return base.astype(jnp.bfloat16)


def draw_group_length(key, part):
    lengths = jax.random.randint(jax.random.fold_in(key, 7011), (KVH,), GROUP // 4, GROUP + 1)
    chosen = jax.random.randint(jax.random.fold_in(key, 7012), (), 0, KVH)
    return jnp.where(jnp.arange(KVH) == chosen, GROUP, lengths).astype(jnp.int32)


def with_ends(drawn, rng, least, top_value):
    spot = [jax.random.randint(jax.random.fold_in(rng, axis), (), 0, length) for axis, length in enumerate(drawn.shape)]
    main_axis = drawn.shape.index(max(drawn.shape))
    beside = spot[:main_axis] + [(spot[main_axis] + 1) % drawn.shape[main_axis]] + spot[main_axis + 1:]
    return drawn.at[tuple(spot)].set(least).at[tuple(beside)].set(top_value)


def block_levels(own_key, shape, split, smallest, largest):
    gain = 1.0
    for dim, blocks in split:
        steps = jax.random.uniform(jax.random.fold_in(jax.random.fold_in(own_key, 6), dim), (blocks,), jnp.float32, smallest / len(split), largest / len(split))
        gain = gain * jnp.repeat(jnp.exp(steps), shape[dim] // blocks).reshape((-1,) + (1,) * (len(shape) - 1 - dim))
    return gain


def normal_values(rng, dims, width, most, split=(), kind=jnp.bfloat16):
    factor_of = block_levels(rng, dims, split, -0.22, 0.18) if split else 1.0
    result = jax.random.normal(rng, dims, jnp.float32) * width * factor_of
    return jnp.minimum(jnp.maximum(result, -most), most).astype(kind)


def setup_inputs(seed: int = 0) -> dict:
    seeds = jax.random.split(jax.random.key(seed), 14)
    frozen_queries = draw_frozen_queries(jax.random.fold_in(seeds[13], 71), 0)
    key_value_rows = draw_key_value_rows(jax.random.fold_in(seeds[13], 71), 0)
    output_gradient = normal_values(seeds[2], (TOKENS, LOCAL_HEADS * HEAD_SIZE), 1.0, 6.0, ((0, 64), (1, 4)))
    inputs = normal_values(seeds[3], (TOKENS, MODEL_WIDTH), 1.0, 6.0, ((0, 64), (1, 4)))
    adapter_down = normal_values(seeds[4], (ADAPTER_RANK, MODEL_WIDTH), MODEL_WIDTH ** -0.5, 0.0625, ((0, 64), (1, 4)), jnp.float32)
    down_first_moment = normal_values(seeds[5], (ADAPTER_RANK, MODEL_WIDTH), 1.0, 6.0, ((0, 64), (1, 4)), jnp.float32)
    down_second_moment = jnp.clip(jnp.exp(math.log(8.0) - 2.7725887 * jax.random.uniform(seeds[6], (ADAPTER_RANK, MODEL_WIDTH), jnp.float32) ** block_levels(seeds[6], (ADAPTER_RANK, MODEL_WIDTH), ((0, 64), (1, 4)), -0.2, 0.2)), 0.5, 8.0)
    adapter_up = normal_values(seeds[7], (ADAPTER_RANK, LOCAL_HEADS * HEAD_SIZE), ADAPTER_RANK ** -0.5, 0.75, ((0, 64), (1, 4)), jnp.float32)
    up_first_moment = normal_values(seeds[8], (ADAPTER_RANK, LOCAL_HEADS * HEAD_SIZE), 1.0, 6.0, ((0, 64), (1, 4)), jnp.float32)
    up_second_moment = jnp.clip(jnp.exp(math.log(8.0) - 2.7725887 * jax.random.uniform(seeds[9], (ADAPTER_RANK, LOCAL_HEADS * HEAD_SIZE), jnp.float32) ** block_levels(seeds[9], (ADAPTER_RANK, LOCAL_HEADS * HEAD_SIZE), ((0, 64), (1, 4)), -0.2, 0.2)), 0.5, 8.0)
    rank_keep_mask = with_ends((jax.random.randint(seeds[10], (2, ADAPTER_RANK), 0, 2) < 1).astype(jnp.int32), jax.random.fold_in(seeds[10], 1), 0, 1)
    group_length = draw_group_length(jax.random.fold_in(seeds[13], 71), 0)
    group_shift = jax.random.randint(seeds[12], (KVH,), 1, GROUP).astype(jnp.int32)
    return dict(frozen_queries=frozen_queries, key_value_rows=key_value_rows, output_gradient=output_gradient, inputs=inputs, adapter_down=adapter_down, down_first_moment=down_first_moment, down_second_moment=down_second_moment, adapter_up=adapter_up, up_first_moment=up_first_moment, up_second_moment=up_second_moment, rank_keep_mask=rank_keep_mask, group_length=group_length, group_shift=group_shift)


adapter_scale = 0.25
beta_one = 0.9
beta_two = 0.999
learn_rate = 0.01
adam_epsilon = 1e-08

def adam_update(current, moment_one, moment_two, gradient):
    moment_one_new = beta_one * moment_one + (1.0 - beta_one) * gradient
    moment_two_new = beta_two * moment_two + (1.0 - beta_two) * gradient * gradient
    updated = current - learn_rate * moment_one_new / (jnp.sqrt(moment_two_new) + adam_epsilon)
    return (updated, moment_one_new, moment_two_new)

def reference(frozen_queries, key_value_rows, output_gradient, inputs, adapter_down, down_first_moment, down_second_moment, adapter_up, up_first_moment, up_second_moment, rank_keep_mask, group_length, group_shift):
    group_heads = LOCAL_HEADS // KVH
    seq_total = TOK_DEV * N_CTX
    span = (REACH + 1) * TOK_DEV
    down_keep_mask = rank_keep_mask[0].astype(jnp.float32)
    up_keep_mask = rank_keep_mask[1].astype(jnp.float32)
    half_down_factor = adapter_down.astype(jnp.bfloat16)
    masked_up_factor = adapter_up.astype(jnp.bfloat16) * rank_keep_mask[1][:, None].astype(jnp.bfloat16)
    projected = jnp.dot(inputs, half_down_factor.T, preferred_element_type=jnp.float32)
    masked_projection = (projected * down_keep_mask[None, :]).astype(jnp.bfloat16)
    query_values = (frozen_queries.astype(jnp.float32) + adapter_scale * jnp.dot(masked_projection, masked_up_factor, preferred_element_type=jnp.float32)).astype(jnp.bfloat16)
    score_scale = 1.0 / math.sqrt(HEAD_SIZE)
    query_blocks = query_values.reshape(N_CTX, TOK_DEV, KVH, group_heads, HEAD_SIZE)
    grad_blocks = output_gradient.reshape(N_CTX, TOK_DEV, KVH, group_heads, HEAD_SIZE)
    key_blocks = key_value_rows[:, :KVH * HEAD_SIZE].reshape(N_CTX, TOK_DEV, KVH, HEAD_SIZE)
    value_blocks = key_value_rows[:, KVH * HEAD_SIZE:].reshape(N_CTX, TOK_DEV, KVH, HEAD_SIZE)
    within = jnp.arange(TOK_DEV, dtype=jnp.int32)
    offsets = jnp.arange(REACH + 1, dtype=jnp.int32)

    def one_block(shard_index):
        sources = (shard_index - REACH + offsets + N_CTX) % N_CTX
        query_rows = query_blocks[shard_index].astype(jnp.float32)
        grad_rows = grad_blocks[shard_index].astype(jnp.float32)
        key_rows = key_blocks[sources].reshape(span, KVH, HEAD_SIZE).astype(jnp.float32)
        value_rows = value_blocks[sources].reshape(span, KVH, HEAD_SIZE).astype(jnp.float32)
        query_place = shard_index * TOK_DEV + within
        key_place = (sources[:, None] * TOK_DEV + within[None, :]).reshape(span)
        query_rolled = ((query_place[:, None] - group_shift[None, :]) % seq_total).T
        key_rolled = ((key_place[:, None] - group_shift[None, :]) % seq_total).T
        same_group = query_rolled[:, :, None] // group_length[:, None, None] == key_rolled[:, None, :] // group_length[:, None, None]
        allowed = same_group & (key_rolled[:, None, :] <= query_rolled[:, :, None])
        scores = jnp.einsum('qjhd,kjd->jhqk', query_rows, key_rows) * score_scale
        scores = jnp.where(allowed[:, None], scores, -1e+30)
        row_max = lax.optimization_barrier(jnp.max(scores, -1, keepdims=True))
        powers = jnp.exp(scores - row_max)
        weights = powers / lax.optimization_barrier(jnp.sum(powers, -1, keepdims=True))
        weights_half = lax.optimization_barrier(weights.astype(jnp.bfloat16)).astype(jnp.float32)
        attended = jnp.einsum('jhqk,kjd->qjhd', weights_half, value_rows).astype(jnp.bfloat16)
        grad_weights = jnp.einsum('qjhd,kjd->jhqk', grad_rows, value_rows)
        row_dots = lax.optimization_barrier(jnp.sum(weights * grad_weights, -1, keepdims=True))
        grad_scores = lax.optimization_barrier((weights * (grad_weights - row_dots)).astype(jnp.bfloat16)).astype(jnp.float32)
        grad_query = (score_scale * jnp.einsum('jhqk,kjd->qjhd', grad_scores, key_rows)).astype(jnp.bfloat16)
        grad_keys = score_scale * jnp.einsum('jhqk,qjhd->kjd', grad_scores, query_rows)
        grad_values = jnp.einsum('jhqk,qjhd->kjd', weights_half, grad_rows)
        return (attended, grad_query, grad_keys.reshape(REACH + 1, TOK_DEV, KVH, HEAD_SIZE), grad_values.reshape(REACH + 1, TOK_DEV, KVH, HEAD_SIZE))
    attended_all, grad_query_all, grad_keys_all, grad_values_all = lax.map(one_block, jnp.arange(N_CTX, dtype=jnp.int32))
    attention_out = attended_all.reshape(seq_total, LOCAL_HEADS * HEAD_SIZE)
    query_gradient = grad_query_all.reshape(seq_total, LOCAL_HEADS * HEAD_SIZE)
    key_total = grad_keys_all[:, REACH]
    value_total = grad_values_all[:, REACH]
    for back in range(REACH):
        key_total = key_total + jnp.roll(grad_keys_all[:, back], -(REACH - back), axis=0)
        value_total = value_total + jnp.roll(grad_values_all[:, back], -(REACH - back), axis=0)
    kv_grad = jnp.concatenate([key_total.reshape(seq_total, KVH * HEAD_SIZE), value_total.reshape(seq_total, KVH * HEAD_SIZE)], 1)
    up_gradient = up_keep_mask[:, None] * (adapter_scale * jnp.dot(masked_projection.T, query_gradient, preferred_element_type=jnp.float32))
    projection_backward = jnp.dot(query_gradient, masked_up_factor.T, preferred_element_type=jnp.float32)
    rank_product = (projection_backward * down_keep_mask[None, :] * adapter_scale).astype(jnp.bfloat16)
    down_gradient = jnp.dot(rank_product.T, inputs, preferred_element_type=jnp.float32)
    updated_down, updated_down_first, updated_down_second = adam_update(adapter_down, down_first_moment, down_second_moment, down_gradient)
    updated_up, updated_up_first, updated_up_second = adam_update(adapter_up, up_first_moment, up_second_moment, up_gradient)
    return (attention_out, query_gradient, kv_grad, updated_down, updated_down_first, updated_down_second, updated_up, updated_up_first, updated_up_second)
```

```python
import functools
import math

import jax
import jax.numpy as jnp
from jax import lax
from jax.experimental import pallas as pl
from jax.experimental.pallas import tpu as pltpu
from jax.sharding import PartitionSpec as P

HEAD_SIZE = 128
KVH = 2
REACH = 8
CORES = 2

adapter_scale = 0.25
beta_one = 0.9
beta_two = 0.999
learn_rate = 0.01
adam_epsilon = 1e-08


NN = (((1,), (0,)), ((), ()))
NT = (((1,), (1,)), ((), ()))


def dot32(a, b, dims):
    return lax.dot_general(a, b, dims, preferred_element_type=jnp.float32)


def attention_kernel(*refs, tokens, ranks, heads, score_scale):
    tiles = REACH + 1
    (core_ref, fq_ref, go_ref, up_ref, keep0_ref, keep1_ref, low_ref, own_k_ref, own_v_ref) = refs[:9]
    direct = refs[9 : 9 + REACH]
    swapped = refs[9 + REACH : 9 + 2 * REACH]
    parts = refs[9 + 2 * REACH : 13 + 2 * REACH]
    out_ref, gq_ref, keep_ref, send_ref, low_rank_ref, grad_up_ref = refs[13 + 2 * REACH : 19 + 2 * REACH]
    (k_s, v_s, kt_s, vt_s, gk_s, gv_s, s_s, p_s, mpt_s, mp_s, lr_s) = refs[19 + 2 * REACH :]
    head = pl.program_id(0)
    core = core_ref[0]

    def rows(d):
        return pl.ds(d * tokens, tokens)

    @pl.when(head == 0)
    def _():
        k_s[rows(0), :] = own_k_ref[...]
        v_s[rows(0), :] = own_v_ref[...]

        @pl.when(core == 0)
        def _():
            for d in range(1, tiles):
                k_s[rows(d), :] = direct[d - 1][...]
                v_s[rows(d), :] = swapped[d - 1][...]

        @pl.when(core != 0)
        def _():
            for d in range(1, tiles):
                k_s[rows(d), :] = swapped[d - 1][...]
                v_s[rows(d), :] = direct[d - 1][...]

        for d in range(tiles):
            kt_s[:, rows(d)] = k_s[rows(d), :].T
            vt_s[:, rows(d)] = v_s[rows(d), :].T
        gk_s[...] = jnp.zeros_like(gk_s)
        gv_s[...] = jnp.zeros_like(gv_s)
        lr_s[...] = jnp.zeros_like(lr_s)
        total = (parts[0][...].astype(jnp.float32) + parts[1][...].astype(jnp.float32)) + (
            parts[2][...].astype(jnp.float32) + parts[3][...].astype(jnp.float32)
        )
        mpt = (total * keep0_ref[...]).astype(jnp.bfloat16)
        mpt_s[...] = mpt
        mp_s[...] = mpt.astype(jnp.float32).T.astype(jnp.bfloat16)

    up = (up_ref[...].astype(jnp.float32) * keep1_ref[...]).astype(jnp.bfloat16)
    query = (
        fq_ref[...].astype(jnp.float32) + adapter_scale * dot32(mp_s[...], up, NN)
    ).astype(jnp.bfloat16)
    grad_out = go_ref[...]
    low = low_ref[...]

    top = jnp.full((1, tokens), -1e30, jnp.float32)
    for d in range(tiles):
        s = dot32(k_s[rows(d), :], query, NT)
        ki = lax.broadcasted_iota(jnp.int32, (tokens, tokens), 0)
        allowed = ki >= low + d * tokens
        if d == 0:
            qi = lax.broadcasted_iota(jnp.int32, (tokens, tokens), 1)
            allowed = allowed & (ki <= qi)
        s = jnp.where(allowed, s, -1e30)
        s_s[rows(d), :] = s
        top = jnp.maximum(top, jnp.max(s, axis=0, keepdims=True))
    total = jnp.zeros((1, tokens), jnp.float32)
    for d in range(tiles):
        p = jnp.exp((s_s[rows(d), :] - top) * score_scale)
        s_s[rows(d), :] = p
        total = total + jnp.sum(p, axis=0, keepdims=True)
    inverse = 1.0 / total
    row_dots = jnp.zeros((1, tokens), jnp.float32)
    out_t = jnp.zeros((HEAD_SIZE, tokens), jnp.float32)
    for d in range(tiles):
        w = s_s[rows(d), :] * inverse
        s_s[rows(d), :] = w
        gw = dot32(v_s[rows(d), :], grad_out, NT)
        p_s[rows(d), :] = gw
        row_dots = row_dots + jnp.sum(w * gw, axis=0, keepdims=True)
        w_half = w.astype(jnp.bfloat16)
        out_t = out_t + dot32(vt_s[:, rows(d)], w_half, NN)
        gv_s[rows(d), :] += dot32(w_half, grad_out, NN)
    out_ref[...] = out_t.T.astype(jnp.bfloat16)
    gq_t = jnp.zeros((HEAD_SIZE, tokens), jnp.float32)
    for d in range(tiles):
        gs = (s_s[rows(d), :] * (p_s[rows(d), :] - row_dots)).astype(jnp.bfloat16)
        gq_t = gq_t + dot32(kt_s[:, rows(d)], gs, NN)
        gk_s[rows(d), :] += dot32(gs, query, NN)
    gq_t = (score_scale * gq_t).astype(jnp.bfloat16)
    gq = (gq_t.astype(jnp.float32).T).astype(jnp.bfloat16)
    gq_ref[...] = gq
    lr_s[...] += dot32(up, gq_t, NN)
    grad_up_ref[...] = (adapter_scale * dot32(mpt_s[...], gq, NN)).astype(jnp.bfloat16)

    @pl.when(head == heads - 1)
    def _():
        low_rank_ref[...] = lr_s[...].astype(jnp.bfloat16)

        @pl.when(core == 0)
        def _():
            keep_ref[...] = gk_s[...] * score_scale
            send_ref[...] = gv_s[...].astype(jnp.bfloat16)

        @pl.when(core != 0)
        def _():
            keep_ref[...] = gv_s[...]
            send_ref[...] = (gk_s[...] * score_scale).astype(jnp.bfloat16)


def attention(core, fq, go, up, keep0, keep1, low, own_k, own_v, direct, swapped, parts):
    tokens, width = fq.shape
    heads = width // HEAD_SIZE
    ranks = up.shape[0]
    tiles = REACH + 1
    span = tiles * tokens

    def whole(a):
        return pl.BlockSpec(a.shape, lambda h, c, n=a.ndim: (0,) * n)

    def by_head(rows):
        return pl.BlockSpec((rows, HEAD_SIZE), lambda h, c: (0, h))

    rest = [keep0, keep1, low, own_k, own_v, *direct, *swapped, *parts]
    out_shape = [
        jax.ShapeDtypeStruct((tokens, width), jnp.bfloat16),
        jax.ShapeDtypeStruct((tokens, width), jnp.bfloat16),
        jax.ShapeDtypeStruct((span, HEAD_SIZE), jnp.float32),
        jax.ShapeDtypeStruct((span, HEAD_SIZE), jnp.bfloat16),
        jax.ShapeDtypeStruct((ranks, tokens), jnp.bfloat16),
        jax.ShapeDtypeStruct((ranks, width), jnp.bfloat16),
    ]
    return pl.pallas_call(
        functools.partial(
            attention_kernel,
            tokens=tokens,
            ranks=ranks,
            heads=heads,
            score_scale=1.0 / math.sqrt(HEAD_SIZE),
        ),
        grid_spec=pltpu.PrefetchScalarGridSpec(
            num_scalar_prefetch=1,
            grid=(heads,),
            in_specs=[by_head(tokens), by_head(tokens), by_head(ranks)] + [whole(a) for a in rest],
            out_specs=[
                by_head(tokens),
                by_head(tokens),
                whole(out_shape[2]),
                whole(out_shape[3]),
                whole(out_shape[4]),
                by_head(ranks),
            ],
            scratch_shapes=[
                pltpu.VMEM((span, HEAD_SIZE), jnp.bfloat16),
                pltpu.VMEM((span, HEAD_SIZE), jnp.bfloat16),
                pltpu.VMEM((HEAD_SIZE, span), jnp.bfloat16),
                pltpu.VMEM((HEAD_SIZE, span), jnp.bfloat16),
                pltpu.VMEM((span, HEAD_SIZE), jnp.float32),
                pltpu.VMEM((span, HEAD_SIZE), jnp.float32),
                pltpu.VMEM((span, tokens), jnp.float32),
                pltpu.VMEM((span, tokens), jnp.float32),
                pltpu.VMEM((ranks, tokens), jnp.bfloat16),
                pltpu.VMEM((tokens, ranks), jnp.bfloat16),
                pltpu.VMEM((ranks, tokens), jnp.float32),
            ],
        ),
        out_shape=out_shape,
        compiler_params=pltpu.CompilerParams(vmem_limit_bytes=48 << 20),
        cost_estimate=pl.CostEstimate(
            flops=12 * heads * tokens * span * HEAD_SIZE,
            bytes_accessed=8 << 20,
            transcendentals=heads * tokens * span,
        ),
        name="attention",
    )(core, fq, go, up, *rest)


def pair_sum_kernel(keep_ref, got_ref, *outs):
    tokens = outs[0].shape[0]
    for d, out in enumerate(outs):
        rows = pl.ds(d * tokens, tokens)
        out[...] = (keep_ref[rows, :] + got_ref[rows, :].astype(jnp.float32)).astype(jnp.bfloat16)


def pair_sum(keep, got, tokens):
    tiles = keep.shape[0] // tokens
    return pl.pallas_call(
        pair_sum_kernel,
        out_shape=[jax.ShapeDtypeStruct((tokens, HEAD_SIZE), jnp.bfloat16)] * tiles,
        name="pair_sum",
    )(keep, got)


def adam_kernel(got_ref, pd, md, vd, pu, mu, vu, keep_ref, opd, omd, ovd, opu, omu, ovu):
    down_rows = pd.shape[0]
    total = jnp.sum(got_ref[...].astype(jnp.float32), axis=0)
    grads = (total[:down_rows], total[down_rows:] * keep_ref[0, 0])
    for grad, p, m, v, op, om, ov in (
        (grads[0], pd, md, vd, opd, omd, ovd),
        (grads[1], pu, mu, vu, opu, omu, ovu),
    ):
        first = beta_one * m[...] + (1.0 - beta_one) * grad
        second = beta_two * v[...] + (1.0 - beta_two) * grad * grad
        op[...] = p[...] - learn_rate * first / (jnp.sqrt(second) + adam_epsilon)
        om[...] = first
        ov[...] = second


def on_device(
    frozen_queries,
    key_value_rows,
    output_gradient,
    inputs,
    adapter_down,
    down_first_moment,
    down_second_moment,
    adapter_up,
    up_first_moment,
    up_second_moment,
    rank_keep_mask,
    group_length,
    group_shift,
):
    tokens = frozen_queries.shape[0]
    width = frozen_queries.shape[1]
    model = inputs.shape[1]
    ctx = lax.axis_size("ctx")
    head_count = lax.axis_size("head")
    ctx_place = lax.axis_index("ctx")
    head_place = lax.axis_index("head")
    core = head_place % CORES
    kv_head = head_place // CORES
    key_width = KVH * HEAD_SIZE
    ranks = rank_keep_mask.shape[1]

    own_k = lax.dynamic_slice_in_dim(key_value_rows, kv_head * HEAD_SIZE, HEAD_SIZE, 1)
    own_v = lax.dynamic_slice_in_dim(key_value_rows, key_width + kv_head * HEAD_SIZE, HEAD_SIZE, 1)
    mine = lax.dynamic_slice_in_dim(
        key_value_rows, core * key_width + kv_head * HEAD_SIZE, HEAD_SIZE, 1
    )
    swap = [(h, h ^ 1) for h in range(head_count)]
    direct = [
        lax.ppermute(mine, "ctx", [(i, (i + d) % ctx) for i in range(ctx)])
        for d in range(1, REACH + 1)
    ]
    swapped = [lax.ppermute(piece, "head", swap) for piece in direct]

    down_rows, up_rows = model // 128, width // 128
    row = jnp.concatenate([adapter_down.reshape(down_rows, 128), adapter_up.reshape(up_rows, 128)], 0)
    row = row.astype(jnp.bfloat16)
    gathered = lax.all_to_all(
        jnp.broadcast_to(row[None], (ctx,) + row.shape), "ctx", split_axis=0, concat_axis=0
    )
    down = gathered[:, :down_rows].reshape(ranks, model)
    up = gathered[:, down_rows:].reshape(ranks, width)

    part = dot32(down, inputs, NT).astype(jnp.bfloat16)
    others = [[(h, h ^ k) for h in range(head_count)] for k in range(1, head_count)]
    parts = [part] + [lax.ppermute(part, "head", pairs) for pairs in others]

    length = group_length[kv_head]
    within = jnp.arange(tokens, dtype=jnp.int32)
    rolled = (ctx_place * tokens + within - group_shift[kv_head]) % (tokens * ctx)
    low = (within - rolled % length).reshape(1, tokens)
    keep_masks = rank_keep_mask.astype(jnp.float32)[:, :, None]
    out, query_gradient, keep, send, low_rank_part, grad_up_part = attention(
        core.reshape(1).astype(jnp.int32),
        frozen_queries,
        output_gradient,
        up,
        keep_masks[0],
        keep_masks[1],
        low,
        own_k,
        own_v,
        direct,
        swapped,
        parts,
    )

    low_parts = [low_rank_part] + [lax.ppermute(low_rank_part, "head", pairs) for pairs in others]
    low_total = sum(p.astype(jnp.float32) for p in low_parts)
    low_rank = (low_total * keep_masks[0] * adapter_scale).astype(jnp.bfloat16)
    grad_down_part = dot32(low_rank, inputs, NN).astype(jnp.bfloat16)
    packed = jnp.concatenate(
        [
            grad_down_part.reshape(ranks, down_rows, 128),
            grad_up_part.reshape(ranks, up_rows, 128),
        ],
        1,
    )
    received = lax.all_to_all(packed, "ctx", split_axis=0, concat_axis=0)

    got = lax.ppermute(send, "head", swap)
    pieces = pair_sum(keep, got, tokens)
    back = []
    for d, piece in enumerate(pieces):
        pairs = [
            (i * head_count + h, ((i - d) % ctx) * head_count + (h % CORES) * CORES + h // CORES)
            for i in range(ctx)
            for h in range(head_count)
        ]
        back.append(lax.ppermute(piece, ("ctx", "head"), pairs).astype(jnp.float32))
    kv_grad = functools.reduce(jnp.add, back)

    keep_row = lax.dynamic_slice_in_dim(keep_masks[1], ctx_place, 1, 0)
    small = [
        a.reshape(-1, 128)
        for a in (
            adapter_down,
            down_first_moment,
            down_second_moment,
            adapter_up,
            up_first_moment,
            up_second_moment,
        )
    ]
    news = pl.pallas_call(
        adam_kernel,
        out_shape=[jax.ShapeDtypeStruct(a.shape, jnp.float32) for a in small],
        name="adam",
    )(received, *small, keep_row)
    news = [n.reshape(1, -1) for n in news]
    return (out, query_gradient, kv_grad, *news)


def solution(mesh):
    both = P("ctx", "head")
    return jax.shard_map(
        on_device,
        mesh=mesh,
        in_specs=(both, P("ctx", None)) + (both,) * 8 + (P(), P(), P()),
        out_specs=(both,) * 9,
        check_vma=False,
    )
```

```python
import functools
import math

import jax
import jax.numpy as jnp
from jax import lax
from jax.experimental import pallas as pl
from jax.experimental.pallas import tpu as pltpu
from jax.sharding import PartitionSpec as P

HEAD_SIZE = 128
KVH = 2
REACH = 8
CORES = 2
COLUMNS = 4

adapter_scale = 0.25
beta_one = 0.9
beta_two = 0.999
learn_rate = 0.01
adam_epsilon = 1e-08


NN = (((1,), (0,)), ((), ()))
NT = (((1,), (1,)), ((), ()))


def dot32(a, b, dims):
    return lax.dot_general(a, b, dims, preferred_element_type=jnp.float32)


def distance(slot, column):
    if slot < 3:
        return (0, COLUMNS, 2 * COLUMNS)[slot]
    step, late = divmod(slot - 1, 2)
    near = column >= step
    return jnp.where(near, step + (0 if late else COLUMNS), step + (COLUMNS if late else 0))


def pack_kernel(spot_ref, own_ref, one_ref, two_ref, *outs):
    column = spot_ref[1]
    for n, out in enumerate(outs):
        step = n + 1
        out[0] = one_ref[...]

        @pl.when(column + step < COLUMNS)
        def _():
            out[1] = own_ref[...]

        @pl.when(column + step >= COLUMNS)
        def _():
            out[1] = two_ref[...]


def pack(spot, own, one, two):
    vmem = pl.BlockSpec(memory_space=pltpu.VMEM)
    return pl.pallas_call(
        pack_kernel,
        in_specs=[pl.BlockSpec(memory_space=pltpu.SMEM), vmem, vmem, vmem],
        out_shape=[jax.ShapeDtypeStruct((2,) + own.shape, own.dtype)] * (COLUMNS - 1),
        compiler_params=pltpu.CompilerParams(vmem_limit_bytes=8 << 20),
        name="pack",
    )(spot, own, one, two)


def column_of(row):
    n = row.shape[1]
    eye = lax.broadcasted_iota(jnp.int32, (n, n), 0) == lax.broadcasted_iota(jnp.int32, (n, n), 1)
    return jnp.sum(jnp.where(eye, jnp.broadcast_to(row, (n, n)), 0.0), axis=1, keepdims=True)


def attention_kernel(*refs, tokens, heads, score_scale):
    tiles = REACH + 1
    (spot_ref, fq_ref, go_ref, up_ref, mask_ref, low_ref, own_k_ref, own_v_ref) = refs[:8]
    direct, swapped = refs[8:13], refs[13:18]
    parts = refs[18:22]
    out_ref, gq_ref, low_rank_ref, grad_up_ref, q_ref, w_ref, gs_ref = refs[22:29]
    (k_s, v_s, kt_s, vt_s, s_s, a_s, lr_s) = refs[29:]
    core = spot_ref[0]
    column = spot_ref[1]
    exponent = score_scale * math.log2(math.e)

    def rows(d):
        return pl.ds(d * tokens, tokens)

    k_s[rows(0), :] = own_k_ref[...]
    v_s[rows(0), :] = own_v_ref[...]

    def fill(store, pieces):
        store[rows(1), :] = pieces[0][...]
        store[rows(2), :] = pieces[1][...]
        for n in range(1, COLUMNS):
            store[rows(2 * n + 1), :] = pieces[n + 1][0]
            store[rows(2 * n + 2), :] = pieces[n + 1][1]

    @pl.when(core == 0)
    def _():
        fill(k_s, direct)
        fill(v_s, swapped)

    @pl.when(core != 0)
    def _():
        fill(k_s, swapped)
        fill(v_s, direct)

    for d in range(tiles):
        kt_s[:, rows(d)] = k_s[rows(d), :].T
        vt_s[:, rows(d)] = v_s[rows(d), :].T
    lr_s[...] = jnp.zeros_like(lr_s)
    masks = mask_ref[...].astype(jnp.float32)
    keep0, keep1 = column_of(masks[0:1]), column_of(masks[1:2])
    total = (parts[0][...].astype(jnp.float32) + parts[1][...].astype(jnp.float32)) + (
        parts[2][...].astype(jnp.float32) + parts[3][...].astype(jnp.float32)
    )
    mpt = (total * keep0).astype(jnp.bfloat16)
    mp = mpt.astype(jnp.float32).T.astype(jnp.bfloat16)
    low = low_ref[...]

    def one_head(head, carry):
        lanes = pl.ds(pl.multiple_of(head * HEAD_SIZE, HEAD_SIZE), HEAD_SIZE)
        wide = pl.ds(pl.multiple_of(head * tokens, tokens), tokens)
        up = (up_ref[:, lanes].astype(jnp.float32) * keep1).astype(jnp.bfloat16)
        query = (
            fq_ref[:, lanes].astype(jnp.float32) + adapter_scale * dot32(mp, up, NN)
        ).astype(jnp.bfloat16)
        q_ref[wide, :] = query
        grad_out = go_ref[:, lanes]

        top = jnp.full((1, tokens), -1e30, jnp.float32)
        for d in range(tiles):
            s = dot32(k_s[rows(d), :], query, NT)
            ki = lax.broadcasted_iota(jnp.int32, (tokens, tokens), 0)
            allowed = ki >= low + distance(d, column) * tokens
            if d == 0:
                allowed = allowed & (ki <= lax.broadcasted_iota(jnp.int32, (tokens, tokens), 1))
            s = jnp.where(allowed, s, -1e30)
            s_s[rows(d), :] = s
            top = jnp.maximum(top, jnp.max(s, axis=0, keepdims=True))
        total = jnp.zeros((1, tokens), jnp.float32)
        for d in range(tiles):
            p = jnp.exp2((s_s[rows(d), :] - top) * exponent)
            s_s[rows(d), :] = p
            total = total + jnp.sum(p, axis=0, keepdims=True)
        inverse = 1.0 / total
        row_dots = jnp.zeros((1, tokens), jnp.float32)
        out_t = jnp.zeros((HEAD_SIZE, tokens), jnp.float32)
        for d in range(tiles):
            w = s_s[rows(d), :] * inverse
            w_half = w.astype(jnp.bfloat16)
            w_ref[rows(d), wide] = w_half
            out_t = out_t + dot32(vt_s[:, rows(d)], w_half, NN)
            a = w * dot32(v_s[rows(d), :], grad_out, NT)
            a_s[rows(d), :] = a
            row_dots = row_dots + jnp.sum(a, axis=0, keepdims=True)
        out_ref[:, lanes] = out_t.T.astype(jnp.bfloat16)
        row_dots = row_dots * inverse
        gq_t = jnp.zeros((HEAD_SIZE, tokens), jnp.float32)
        for d in range(tiles):
            gs = (a_s[rows(d), :] - s_s[rows(d), :] * row_dots).astype(jnp.bfloat16)
            gs_ref[rows(d), wide] = gs
            gq_t = gq_t + dot32(kt_s[:, rows(d)], gs, NN)
        gq_t = (score_scale * gq_t).astype(jnp.bfloat16)
        gq = (gq_t.astype(jnp.float32).T).astype(jnp.bfloat16)
        gq_ref[:, lanes] = gq
        lr_s[...] += dot32(up, gq_t, NN)
        grad_up_ref[:, lanes] = (adapter_scale * dot32(mpt, gq, NN)).astype(jnp.bfloat16)
        return carry

    lax.fori_loop(0, heads, one_head, 0)
    low_rank_ref[...] = lr_s[...].astype(jnp.bfloat16)


def attention(spot, fq, go, up, rest):
    tokens, width = fq.shape
    heads = width // HEAD_SIZE
    ranks = up.shape[0]
    span = (REACH + 1) * tokens
    vmem = pl.BlockSpec(memory_space=pltpu.VMEM)
    return pl.pallas_call(
        functools.partial(
            attention_kernel, tokens=tokens, heads=heads, score_scale=1.0 / math.sqrt(HEAD_SIZE)
        ),
        in_specs=[pl.BlockSpec(memory_space=pltpu.SMEM)] + [vmem] * (3 + len(rest)),
        out_specs=[vmem] * 7,
        scratch_shapes=[
            pltpu.VMEM((span, HEAD_SIZE), jnp.bfloat16),
            pltpu.VMEM((span, HEAD_SIZE), jnp.bfloat16),
            pltpu.VMEM((HEAD_SIZE, span), jnp.bfloat16),
            pltpu.VMEM((HEAD_SIZE, span), jnp.bfloat16),
            pltpu.VMEM((span, tokens), jnp.float32),
            pltpu.VMEM((span, tokens), jnp.float32),
            pltpu.VMEM((ranks, tokens), jnp.float32),
        ],
        out_shape=[
            jax.ShapeDtypeStruct((tokens, width), jnp.bfloat16),
            jax.ShapeDtypeStruct((tokens, width), jnp.bfloat16),
            jax.ShapeDtypeStruct((ranks, tokens), jnp.bfloat16),
            jax.ShapeDtypeStruct((ranks, width), jnp.bfloat16),
            jax.ShapeDtypeStruct((heads * tokens, HEAD_SIZE), jnp.bfloat16),
            jax.ShapeDtypeStruct((span, heads * tokens), jnp.bfloat16),
            jax.ShapeDtypeStruct((span, heads * tokens), jnp.bfloat16),
        ],
        compiler_params=pltpu.CompilerParams(vmem_limit_bytes=12 << 20),
        cost_estimate=pl.CostEstimate(
            flops=8 * heads * tokens * span * HEAD_SIZE,
            bytes_accessed=8 << 20,
            transcendentals=heads * tokens * span,
        ),
        name="attention",
    )(spot, fq, go, up, *rest)


def kv_half_kernel(spot_ref, w_ref, gs_ref, go_ref, q_ref, half_ref, go_s, *, keep, score_scale):
    tokens = go_ref.shape[0]
    span = w_ref.shape[0]
    heads = go_ref.shape[1] // HEAD_SIZE
    values = (spot_ref[0] == 0) != keep

    @pl.when(values)
    def _():
        for h in range(heads):
            go_s[pl.ds(h * tokens, tokens), :] = go_ref[:, pl.ds(h * HEAD_SIZE, HEAD_SIZE)]
        for d in range(span // tokens):
            rows = pl.ds(d * tokens, tokens)
            half_ref[rows, :] = dot32(w_ref[rows, :], go_s[...], NN).astype(half_ref.dtype)

    @pl.when(jnp.logical_not(values))
    def _():
        for d in range(span // tokens):
            rows = pl.ds(d * tokens, tokens)
            half = score_scale * dot32(gs_ref[rows, :], q_ref[...], NN)
            half_ref[rows, :] = half.astype(half_ref.dtype)


def kv_half(spot, weights, grad_scores, go, queries, keep):
    span = weights.shape[0]
    vmem = pl.BlockSpec(memory_space=pltpu.VMEM)
    return pl.pallas_call(
        functools.partial(kv_half_kernel, keep=keep, score_scale=1.0 / math.sqrt(HEAD_SIZE)),
        in_specs=[pl.BlockSpec(memory_space=pltpu.SMEM)] + [vmem] * 4,
        out_specs=vmem,
        scratch_shapes=[pltpu.VMEM(queries.shape, jnp.bfloat16)],
        out_shape=jax.ShapeDtypeStruct((span, HEAD_SIZE), jnp.float32 if keep else jnp.bfloat16),
        compiler_params=pltpu.CompilerParams(vmem_limit_bytes=6 << 20),
        cost_estimate=pl.CostEstimate(
            flops=2 * span * queries.size, bytes_accessed=2 << 20, transcendentals=0
        ),
        name="kv_keep" if keep else "kv_send",
    )(spot, weights, grad_scores, go, queries)


def pair_sum_kernel(keep_ref, got_ref, own_ref, one_ref, two_ref, *packs):
    tokens = own_ref.shape[0]

    def total(d):
        rows = pl.ds(d * tokens, tokens)
        return keep_ref[rows, :] + got_ref[rows, :].astype(jnp.float32)

    own_ref[...] = total(0)
    one_ref[...] = total(1)
    two_ref[...] = total(2)
    for n, pack_ref in enumerate(packs):
        pack_ref[0] = total(2 * n + 3).astype(jnp.bfloat16)
        pack_ref[1] = total(2 * n + 4).astype(jnp.bfloat16)


def pair_sum(keep, got, tokens):
    tile = (tokens, HEAD_SIZE)
    return pl.pallas_call(
        pair_sum_kernel,
        out_shape=[jax.ShapeDtypeStruct(tile, jnp.float32)] * 3
        + [jax.ShapeDtypeStruct((2,) + tile, jnp.bfloat16)] * (COLUMNS - 1),
        compiler_params=pltpu.CompilerParams(vmem_limit_bytes=12 << 20),
        name="pair_sum",
    )(keep, got)


def row_sum_kernel(spot_ref, own_ref, one_ref, two_ref, *rest):
    column = spot_ref[1]
    packs, (own_out, one_out, two_out) = rest[: COLUMNS - 1], rest[COLUMNS - 1 :]
    own, one, two = own_ref[...], one_ref[...], two_ref[...]
    for n, pack_ref in enumerate(packs):
        one = one + pack_ref[0].astype(jnp.float32)
        piece = pack_ref[1].astype(jnp.float32)
        near = jnp.full(piece.shape, n + 1, jnp.int32) + column < COLUMNS
        own = own + jnp.where(near, piece, 0.0)
        two = two + jnp.where(near, 0.0, piece)
    own_out[...] = own.astype(jnp.bfloat16)
    one_out[...] = one.astype(jnp.bfloat16)
    two_out[...] = two.astype(jnp.bfloat16)


def row_sum(spot, own, one, two, packs):
    vmem = pl.BlockSpec(memory_space=pltpu.VMEM)
    return pl.pallas_call(
        row_sum_kernel,
        in_specs=[pl.BlockSpec(memory_space=pltpu.SMEM)] + [vmem] * (2 + COLUMNS),
        out_shape=[jax.ShapeDtypeStruct(own.shape, jnp.bfloat16)] * 3,
        compiler_params=pltpu.CompilerParams(vmem_limit_bytes=8 << 20),
        name="row_sum",
    )(spot, own, one, two, *packs)


def adam_kernel(got_ref, pd, md, vd, pu, mu, vu, keep_ref, opd, omd, ovd, opu, omu, ovu):
    down_rows = pd.shape[0]
    total = jnp.sum(got_ref[...].astype(jnp.float32), axis=0)
    grads = (total[:down_rows], total[down_rows:] * keep_ref[0, 0])
    for grad, p, m, v, op, om, ov in (
        (grads[0], pd, md, vd, opd, omd, ovd),
        (grads[1], pu, mu, vu, opu, omu, ovu),
    ):
        first = beta_one * m[...] + (1.0 - beta_one) * grad
        second = beta_two * v[...] + (1.0 - beta_two) * grad * grad
        op[...] = p[...] - learn_rate * first / (jnp.sqrt(second) + adam_epsilon)
        om[...] = first
        ov[...] = second


def on_device(
    frozen_queries,
    key_value_rows,
    output_gradient,
    inputs,
    adapter_down,
    down_first_moment,
    down_second_moment,
    adapter_up,
    up_first_moment,
    up_second_moment,
    rank_keep_mask,
    group_length,
    group_shift,
):
    tokens = frozen_queries.shape[0]
    width = frozen_queries.shape[1]
    model = inputs.shape[1]
    ctx = lax.axis_size("ctx")
    head_count = lax.axis_size("head")
    ctx_place = lax.axis_index("ctx")
    head_place = lax.axis_index("head")
    core = head_place % CORES
    kv_head = head_place // CORES
    key_width = KVH * HEAD_SIZE
    ranks = rank_keep_mask.shape[1]

    column = ctx_place % COLUMNS
    spot = jnp.concatenate([core.reshape(1), column.reshape(1)]).astype(jnp.int32)
    own_k = lax.dynamic_slice_in_dim(key_value_rows, kv_head * HEAD_SIZE, HEAD_SIZE, 1)
    own_v = lax.dynamic_slice_in_dim(key_value_rows, key_width + kv_head * HEAD_SIZE, HEAD_SIZE, 1)
    mine = lax.dynamic_slice_in_dim(
        key_value_rows, core * key_width + kv_head * HEAD_SIZE, HEAD_SIZE, 1
    )
    swap = [(h, h ^ 1) for h in range(head_count)]

    def along(piece, step):
        return lax.ppermute(piece, "ctx", [(i, (i + step) % ctx) for i in range(ctx)])

    def across(piece, step):
        pairs = [(i, i // COLUMNS * COLUMNS + (i + step) % COLUMNS) for i in range(ctx)]
        return lax.ppermute(piece, "ctx", pairs)

    one, two = along(mine, COLUMNS), along(mine, 2 * COLUMNS)

    down_rows, up_rows = model // 128, width // 128
    row = jnp.concatenate([adapter_down.reshape(down_rows, 128), adapter_up.reshape(up_rows, 128)], 0)
    row = row.astype(jnp.bfloat16)
    gathered = lax.all_to_all(
        jnp.broadcast_to(row[None], (ctx,) + row.shape), "ctx", split_axis=0, concat_axis=0
    )
    packs = pack(spot, mine, one, two)
    direct = [one, two] + [across(p, n + 1) for n, p in enumerate(packs)]
    swapped = [lax.ppermute(piece, "head", swap) for piece in direct]

    down = gathered[:, :down_rows].reshape(ranks, model)
    up = gathered[:, down_rows:].reshape(ranks, width)

    part = dot32(down, inputs, NT).astype(jnp.bfloat16)
    others = [[(h, h ^ k) for h in range(head_count)] for k in range(1, head_count)]
    parts = [part] + [lax.ppermute(part, "head", pairs) for pairs in others]

    length = group_length[kv_head]
    within = jnp.arange(tokens, dtype=jnp.int32)
    rolled = (ctx_place * tokens + within - group_shift[kv_head]) % (tokens * ctx)
    low = (within - rolled % length).reshape(1, tokens)
    keep_masks = rank_keep_mask.astype(jnp.float32)[:, :, None]
    out, query_gradient, low_rank_part, grad_up_part, queries, weights, grad_scores = attention(
        spot,
        frozen_queries,
        output_gradient,
        up,
        [
            rank_keep_mask,
            low,
            own_k,
            own_v,
            *direct,
            *swapped,
            *parts,
        ],
    )

    low_parts = [low_rank_part] + [lax.ppermute(low_rank_part, "head", pairs) for pairs in others]
    send = kv_half(spot, weights, grad_scores, output_gradient, queries, keep=False)
    got = lax.ppermute(send, "head", swap)
    keep = kv_half(spot, weights, grad_scores, output_gradient, queries, keep=True)
    low_parts, grad_up_part, keep = lax.optimization_barrier((low_parts, grad_up_part, keep))
    low_total = sum(p.astype(jnp.float32) for p in low_parts)
    low_rank = (low_total * keep_masks[0] * adapter_scale).astype(jnp.bfloat16)
    grad_down_part = dot32(low_rank, inputs, NN).astype(jnp.bfloat16)
    packed = jnp.concatenate(
        [
            grad_down_part.reshape(ranks, down_rows, 128),
            grad_up_part.reshape(ranks, up_rows, 128),
        ],
        1,
    )
    received = lax.all_to_all(packed, "ctx", split_axis=0, concat_axis=0)

    own_sum, one_sum, two_sum, *packs = pair_sum(keep, got, tokens)
    packs = [across(p, -(n + 1)) for n, p in enumerate(packs)]
    own_sum, one_sum, two_sum = row_sum(spot, own_sum, one_sum, two_sum, packs)

    def home(piece, back):
        pairs = [
            (
                i * head_count + h,
                (i - back) % ctx * head_count + (h % CORES) * CORES + h // CORES,
            )
            for i in range(ctx)
            for h in range(head_count)
        ]
        return lax.ppermute(piece, ("ctx", "head"), pairs).astype(jnp.float32)

    kv_grad = home(own_sum, 0) + home(one_sum, COLUMNS) + home(two_sum, 2 * COLUMNS)

    keep_row = lax.dynamic_slice_in_dim(keep_masks[1], ctx_place, 1, 0)
    small = [
        a.reshape(-1, 128)
        for a in (
            adapter_down,
            down_first_moment,
            down_second_moment,
            adapter_up,
            up_first_moment,
            up_second_moment,
        )
    ]
    news = pl.pallas_call(
        adam_kernel,
        out_shape=[jax.ShapeDtypeStruct(a.shape, jnp.float32) for a in small],
        compiler_params=pltpu.CompilerParams(vmem_limit_bytes=8 << 20),
        name="adam",
    )(received, *small, keep_row)
    news = [n.reshape(1, -1) for n in news]
    return (out, query_gradient, kv_grad, *news)


def solution(mesh):
    both = P("ctx", "head")
    return jax.shard_map(
        on_device,
        mesh=mesh,
        in_specs=(both, P("ctx", None)) + (both,) * 8 + (P(), P(), P()),
        out_specs=(both,) * 9,
        check_vma=False,
    )
```

```python
import functools
import math

import jax
import jax.numpy as jnp
from jax import lax
from jax.experimental import pallas as pl
from jax.experimental.pallas import tpu as pltpu
from jax.sharding import PartitionSpec as P


HEAD_SIZE = 128
KVH = 2
REACH = 8
CORES = 2
COLUMNS = 4

adapter_scale = 0.25
beta_one = 0.9
beta_two = 0.999
learn_rate = 0.01
adam_epsilon = 1e-08


NN = (((1,), (0,)), ((), ()))
NT = (((1,), (1,)), ((), ()))


def dot32(a, b, dims):
    return lax.dot_general(a, b, dims, preferred_element_type=jnp.float32)


def distance(slot, column):
    if slot < 3:
        return (0, COLUMNS, 2 * COLUMNS)[slot]
    step, late = divmod(slot - 1, 2)
    near = column >= step
    return jnp.where(near, step + (0 if late else COLUMNS), step + (COLUMNS if late else 0))


def pack_kernel(spot_ref, own_ref, one_ref, two_ref, *outs):
    column = spot_ref[1]
    for n, out in enumerate(outs):
        step = n + 1
        out[0] = one_ref[...]

        @pl.when(column + step < COLUMNS)
        def _():
            out[1] = own_ref[...]

        @pl.when(column + step >= COLUMNS)
        def _():
            out[1] = two_ref[...]


def pack(spot, own, one, two):
    vmem = pl.BlockSpec(memory_space=pltpu.VMEM)
    return pl.pallas_call(
        pack_kernel,
        in_specs=[pl.BlockSpec(memory_space=pltpu.SMEM), vmem, vmem, vmem],
        out_shape=[jax.ShapeDtypeStruct((2,) + own.shape, own.dtype)] * (COLUMNS - 1),
        compiler_params=pltpu.CompilerParams(vmem_limit_bytes=8 << 20),
        name="pack",
    )(spot, own, one, two)


def column_of(row):
    n = row.shape[1]
    eye = lax.broadcasted_iota(jnp.int32, (n, n), 0) == lax.broadcasted_iota(jnp.int32, (n, n), 1)
    return jnp.sum(jnp.where(eye, jnp.broadcast_to(row, (n, n)), 0.0), axis=1, keepdims=True)


def fold(combine, start, x):
    for r in range(0, x.shape[0], 8):
        start = combine(start, x[r : r + 8])
    return start


UNROLL = (9, 9, 9, 9)


def loop(count, body, carry, unroll):
    def several(n, carry):
        for u in range(unroll):
            carry = body(n * unroll + u, carry)
        return carry

    if unroll == count:
        return several(0, carry)
    return lax.fori_loop(0, count // unroll, several, carry)


def attention_kernel(*refs, tokens, heads, score_scale):
    tiles = REACH + 1
    (spot_ref, fq_ref, go_ref, up_ref, mask_ref, low_ref, own_k_ref, own_v_ref) = refs[:8]
    direct, swapped = refs[8:13], refs[13:18]
    parts = refs[18:22]
    out_ref, gq_ref, low_rank_ref, grad_up_ref, q_ref, w_ref, gs_ref = refs[22:29]
    (k_s, v_s, kt_s, vt_s, bias_s, s_s, gw_s, a_s, acc_s, lr_s, fq_s, go_s, mask_s, sems) = refs[29:]
    core = spot_ref[0]
    column = spot_ref[1]
    exponent = score_scale * math.log2(math.e)
    loads = [
        pltpu.make_async_copy(fq_ref, fq_s, sems.at[0]),
        pltpu.make_async_copy(go_ref, go_s, sems.at[1]),
        pltpu.make_async_copy(mask_ref, mask_s, sems.at[2]),
    ]
    for load in loads:
        load.start()

    def rows(d):
        return pl.ds(d * tokens, tokens)

    k_s[rows(0), :] = own_k_ref[...]
    v_s[rows(0), :] = own_v_ref[...]

    def fill(store, pieces):
        store[rows(1), :] = pieces[0][...]
        store[rows(2), :] = pieces[1][...]
        for n in range(1, COLUMNS):
            store[rows(2 * n + 1), :] = pieces[n + 1][0]
            store[rows(2 * n + 2), :] = pieces[n + 1][1]

    @pl.when(core == 0)
    def _():
        fill(k_s, direct)
        fill(v_s, swapped)

    @pl.when(core != 0)
    def _():
        fill(k_s, swapped)
        fill(v_s, direct)

    low = low_ref[...]
    for d in range(tiles):
        kt_s[:, rows(d)] = k_s[rows(d), :].T
        vt_s[:, rows(d)] = v_s[rows(d), :].T
        ki = lax.broadcasted_iota(jnp.int32, (tokens, tokens), 0)
        allowed = ki >= low + distance(d, column) * tokens
        if d == 0:
            allowed = allowed & (ki <= lax.broadcasted_iota(jnp.int32, (tokens, tokens), 1))
        bias_s[rows(d), :] = jnp.where(allowed, 0.0, -1e30)
    lr_s[...] = jnp.zeros_like(lr_s)
    for load in loads:
        load.wait()
    masks = mask_s[...].astype(jnp.float32)
    keep0, keep1 = column_of(masks[0:1]), column_of(masks[1:2])
    total = (parts[0][...].astype(jnp.float32) + parts[1][...].astype(jnp.float32)) + (
        parts[2][...].astype(jnp.float32) + parts[3][...].astype(jnp.float32)
    )
    mpt = (total * keep0).astype(jnp.bfloat16)
    mp = mpt.astype(jnp.float32).T.astype(jnp.bfloat16)

    def lanes(head):
        return pl.ds(pl.multiple_of(head * HEAD_SIZE, HEAD_SIZE), HEAD_SIZE)

    def wide(head):
        return pl.ds(pl.multiple_of(head * tokens, tokens), tokens)

    def up_of(head):
        return (up_ref[:, lanes(head)].astype(jnp.float32) * keep1).astype(jnp.bfloat16)

    def make_query(head):
        q_ref[wide(head), :] = (
            fq_s[:, lanes(head)].astype(jnp.float32) + adapter_scale * dot32(mp, up_of(head), NN)
        ).astype(jnp.bfloat16)

    def tile(d):
        if isinstance(d, int):
            return rows(d)
        return pl.ds(pl.multiple_of(d * tokens, tokens), tokens)

    def products(head, slot, d, top):
        s = dot32(k_s[tile(d), :], q_ref[wide(head), :], NT) + bias_s[tile(d), :]
        s_s[slot, tile(d), :] = s
        gw_s[slot, tile(d), :] = dot32(v_s[tile(d), :], go_s[:, lanes(head)], NT)
        return fold(jnp.maximum, top, s)

    lowest = jnp.full((8, tokens), -1e30, jnp.float32)
    zero = jnp.zeros((8, tokens), jnp.float32)
    make_query(0)
    top = loop(tiles, lambda d, top: products(0, 0, d, top), lowest, UNROLL[0])

    def one_head(head, top, last):
        slot = lax.rem(head, 2)
        top = jnp.max(top, axis=0, keepdims=True)
        if not last:
            make_query(head + 1)

        def exponentials(d, carry):
            total, next_top = carry
            p = jnp.exp2((s_s[slot, tile(d), :] - top) * exponent)
            a_s[tile(d), :] = p
            total = fold(jnp.add, total, p)
            if not last:
                next_top = products(head + 1, 1 - slot, d, next_top)
            return total, next_top

        total, next_top = loop(tiles, exponentials, (zero, lowest), UNROLL[1])
        inverse = 1.0 / jnp.sum(total, axis=0, keepdims=True)
        acc_s[...] = jnp.zeros_like(acc_s)

        def weigh(d, dots):
            w = a_s[tile(d), :] * inverse
            w_half = w.astype(jnp.bfloat16)
            w_ref[tile(d), wide(head)] = w_half
            a = w * gw_s[slot, tile(d), :]
            gw_s[slot, tile(d), :] = a
            acc_s[...] += dot32(vt_s[:, tile(d)], w_half, NN)
            return fold(jnp.add, dots, a)

        dots = loop(tiles, weigh, zero, UNROLL[2])
        out_ref[:, lanes(head)] = acc_s[...].T.astype(jnp.bfloat16)
        dots = jnp.sum(dots, axis=0, keepdims=True) * inverse
        acc_s[...] = jnp.zeros_like(acc_s)

        def score_grads(d, carry):
            gs = (gw_s[slot, tile(d), :] - a_s[tile(d), :] * dots).astype(jnp.bfloat16)
            gs_ref[tile(d), wide(head)] = gs
            acc_s[...] += dot32(kt_s[:, tile(d)], gs, NN)
            return carry

        loop(tiles, score_grads, 0, UNROLL[3])
        gq_t = (score_scale * acc_s[...]).astype(jnp.bfloat16)
        gq = (gq_t.astype(jnp.float32).T).astype(jnp.bfloat16)
        gq_ref[:, lanes(head)] = gq
        lr_s[...] += dot32(up_of(head), gq_t, NN)
        grad_up_ref[:, lanes(head)] = (adapter_scale * dot32(mpt, gq, NN)).astype(jnp.bfloat16)
        return next_top

    top = lax.fori_loop(0, heads - 1, lambda h, t: one_head(h, t, False), top)
    one_head(heads - 1, top, True)
    low_rank_ref[...] = lr_s[...].astype(jnp.bfloat16)


def attention(spot, fq, go, up, rest):
    tokens, width = fq.shape
    heads = width // HEAD_SIZE
    ranks = up.shape[0]
    span = (REACH + 1) * tokens
    vmem = pl.BlockSpec(memory_space=pltpu.VMEM)
    hbm = pl.BlockSpec(memory_space=pltpu.HBM)
    return pl.pallas_call(
        functools.partial(
            attention_kernel, tokens=tokens, heads=heads, score_scale=1.0 / math.sqrt(HEAD_SIZE)
        ),
        in_specs=[pl.BlockSpec(memory_space=pltpu.SMEM), hbm, hbm, vmem, hbm] + [vmem] * (len(rest) - 1),
        out_specs=[vmem] * 7,
        scratch_shapes=[
            pltpu.VMEM((span, HEAD_SIZE), jnp.bfloat16),
            pltpu.VMEM((span, HEAD_SIZE), jnp.bfloat16),
            pltpu.VMEM((HEAD_SIZE, span), jnp.bfloat16),
            pltpu.VMEM((HEAD_SIZE, span), jnp.bfloat16),
            pltpu.VMEM((span, tokens), jnp.float32),
            pltpu.VMEM((2, span, tokens), jnp.float32),
            pltpu.VMEM((2, span, tokens), jnp.float32),
            pltpu.VMEM((span, tokens), jnp.float32),
            pltpu.VMEM((HEAD_SIZE, tokens), jnp.float32),
            pltpu.VMEM((ranks, tokens), jnp.float32),
            pltpu.VMEM((tokens, width), jnp.bfloat16),
            pltpu.VMEM((tokens, width), jnp.bfloat16),
            pltpu.VMEM((2, ranks), jnp.int32),
            pltpu.SemaphoreType.DMA((3,)),
        ],
        out_shape=[
            jax.ShapeDtypeStruct((tokens, width), jnp.bfloat16),
            jax.ShapeDtypeStruct((tokens, width), jnp.bfloat16),
            jax.ShapeDtypeStruct((ranks, tokens), jnp.bfloat16),
            jax.ShapeDtypeStruct((ranks, width), jnp.bfloat16),
            jax.ShapeDtypeStruct((heads * tokens, HEAD_SIZE), jnp.bfloat16),
            jax.ShapeDtypeStruct((span, heads * tokens), jnp.bfloat16),
            jax.ShapeDtypeStruct((span, heads * tokens), jnp.bfloat16),
        ],
        compiler_params=pltpu.CompilerParams(vmem_limit_bytes=24 << 20),
        cost_estimate=pl.CostEstimate(
            flops=8 * heads * tokens * span * HEAD_SIZE,
            bytes_accessed=8 << 20,
            transcendentals=heads * tokens * span,
        ),
        name="attention",
    )(spot, fq, go, up, *rest)


def kv_half_kernel(spot_ref, w_ref, gs_ref, go_ref, q_ref, half_ref, go_s, *, keep, score_scale):
    tokens = go_ref.shape[0]
    span = w_ref.shape[0]
    heads = go_ref.shape[1] // HEAD_SIZE
    values = (spot_ref[0] == 0) != keep

    @pl.when(values)
    def _():
        for h in range(heads):
            go_s[pl.ds(h * tokens, tokens), :] = go_ref[:, pl.ds(h * HEAD_SIZE, HEAD_SIZE)]
        for d in range(span // tokens):
            rows = pl.ds(d * tokens, tokens)
            half_ref[rows, :] = dot32(w_ref[rows, :], go_s[...], NN).astype(half_ref.dtype)

    @pl.when(jnp.logical_not(values))
    def _():
        for d in range(span // tokens):
            rows = pl.ds(d * tokens, tokens)
            half = score_scale * dot32(gs_ref[rows, :], q_ref[...], NN)
            half_ref[rows, :] = half.astype(half_ref.dtype)


def kv_half(spot, weights, grad_scores, go, queries, keep):
    span = weights.shape[0]
    vmem = pl.BlockSpec(memory_space=pltpu.VMEM)
    return pl.pallas_call(
        functools.partial(kv_half_kernel, keep=keep, score_scale=1.0 / math.sqrt(HEAD_SIZE)),
        in_specs=[pl.BlockSpec(memory_space=pltpu.SMEM)] + [vmem] * 4,
        out_specs=vmem,
        scratch_shapes=[pltpu.VMEM(queries.shape, jnp.bfloat16)],
        out_shape=jax.ShapeDtypeStruct((span, HEAD_SIZE), jnp.float32 if keep else jnp.bfloat16),
        compiler_params=pltpu.CompilerParams(vmem_limit_bytes=6 << 20),
        cost_estimate=pl.CostEstimate(
            flops=2 * span * queries.size, bytes_accessed=2 << 20, transcendentals=0
        ),
        name="kv_keep" if keep else "kv_send",
    )(spot, weights, grad_scores, go, queries)


def pair_sum_kernel(keep_ref, got_ref, own_ref, one_ref, two_ref, *packs):
    tokens = own_ref.shape[0]

    def total(d):
        rows = pl.ds(d * tokens, tokens)
        return keep_ref[rows, :] + got_ref[rows, :].astype(jnp.float32)

    own_ref[...] = total(0)
    one_ref[...] = total(1)
    two_ref[...] = total(2)
    for n, pack_ref in enumerate(packs):
        pack_ref[0] = total(2 * n + 3).astype(jnp.bfloat16)
        pack_ref[1] = total(2 * n + 4).astype(jnp.bfloat16)


def pair_sum(keep, got, tokens):
    tile = (tokens, HEAD_SIZE)
    return pl.pallas_call(
        pair_sum_kernel,
        out_shape=[jax.ShapeDtypeStruct(tile, jnp.float32)] * 3
        + [jax.ShapeDtypeStruct((2,) + tile, jnp.bfloat16)] * (COLUMNS - 1),
        compiler_params=pltpu.CompilerParams(vmem_limit_bytes=12 << 20),
        name="pair_sum",
    )(keep, got)


def row_sum_kernel(spot_ref, own_ref, one_ref, two_ref, *rest):
    column = spot_ref[1]
    packs, (own_out, one_out, two_out) = rest[: COLUMNS - 1], rest[COLUMNS - 1 :]
    own, one, two = own_ref[...], one_ref[...], two_ref[...]
    for n, pack_ref in enumerate(packs):
        one = one + pack_ref[0].astype(jnp.float32)
        piece = pack_ref[1].astype(jnp.float32)
        near = jnp.full(piece.shape, n + 1, jnp.int32) + column < COLUMNS
        own = own + jnp.where(near, piece, 0.0)
        two = two + jnp.where(near, 0.0, piece)
    own_out[...] = own.astype(jnp.bfloat16)
    one_out[...] = one.astype(jnp.bfloat16)
    two_out[...] = two.astype(jnp.bfloat16)


def row_sum(spot, own, one, two, packs):
    vmem = pl.BlockSpec(memory_space=pltpu.VMEM)
    return pl.pallas_call(
        row_sum_kernel,
        in_specs=[pl.BlockSpec(memory_space=pltpu.SMEM)] + [vmem] * (2 + COLUMNS),
        out_shape=[jax.ShapeDtypeStruct(own.shape, jnp.bfloat16)] * 3,
        compiler_params=pltpu.CompilerParams(vmem_limit_bytes=8 << 20),
        name="row_sum",
    )(spot, own, one, two, *packs)


def adam_kernel(got_ref, pd, md, vd, pu, mu, vu, keep_ref, opd, omd, ovd, opu, omu, ovu):
    down_rows = pd.shape[0]
    total = jnp.sum(got_ref[...].astype(jnp.float32), axis=0)
    grads = (total[:down_rows], total[down_rows:] * keep_ref[0, 0])
    for grad, p, m, v, op, om, ov in (
        (grads[0], pd, md, vd, opd, omd, ovd),
        (grads[1], pu, mu, vu, opu, omu, ovu),
    ):
        first = beta_one * m[...] + (1.0 - beta_one) * grad
        second = beta_two * v[...] + (1.0 - beta_two) * grad * grad
        op[...] = p[...] - learn_rate * first / (jnp.sqrt(second) + adam_epsilon)
        om[...] = first
        ov[...] = second


def on_device(
    frozen_queries,
    key_value_rows,
    output_gradient,
    inputs,
    adapter_down,
    down_first_moment,
    down_second_moment,
    adapter_up,
    up_first_moment,
    up_second_moment,
    rank_keep_mask,
    group_length,
    group_shift,
):
    tokens = frozen_queries.shape[0]
    width = frozen_queries.shape[1]
    model = inputs.shape[1]
    ctx = lax.axis_size("ctx")
    head_count = lax.axis_size("head")
    ctx_place = lax.axis_index("ctx")
    head_place = lax.axis_index("head")
    core = head_place % CORES
    kv_head = head_place // CORES
    key_width = KVH * HEAD_SIZE
    ranks = rank_keep_mask.shape[1]

    column = ctx_place % COLUMNS
    spot = jnp.concatenate([core.reshape(1), column.reshape(1)]).astype(jnp.int32)
    own_k = lax.dynamic_slice_in_dim(key_value_rows, kv_head * HEAD_SIZE, HEAD_SIZE, 1)
    own_v = lax.dynamic_slice_in_dim(key_value_rows, key_width + kv_head * HEAD_SIZE, HEAD_SIZE, 1)
    mine = lax.dynamic_slice_in_dim(
        key_value_rows, core * key_width + kv_head * HEAD_SIZE, HEAD_SIZE, 1
    )
    swap = [(h, h ^ 1) for h in range(head_count)]

    def along(piece, step):
        return lax.ppermute(piece, "ctx", [(i, (i + step) % ctx) for i in range(ctx)])

    def across(piece, step):
        pairs = [(i, i // COLUMNS * COLUMNS + (i + step) % COLUMNS) for i in range(ctx)]
        return lax.ppermute(piece, "ctx", pairs)

    one, two = along(mine, COLUMNS), along(mine, 2 * COLUMNS)

    down_rows, up_rows = model // 128, width // 128
    row = jnp.concatenate([adapter_down.reshape(down_rows, 128), adapter_up.reshape(up_rows, 128)], 0)
    row = row.astype(jnp.bfloat16)
    gathered = lax.all_to_all(
        jnp.broadcast_to(row[None], (ctx,) + row.shape), "ctx", split_axis=0, concat_axis=0
    )
    packs = pack(spot, mine, one, two)
    direct = [one, two] + [across(p, n + 1) for n, p in enumerate(packs)]
    swapped = [lax.ppermute(piece, "head", swap) for piece in direct]

    down = gathered[:, :down_rows].reshape(ranks, model)
    up = gathered[:, down_rows:].reshape(ranks, width)

    part = dot32(down, inputs, NT).astype(jnp.bfloat16)
    others = [[(h, h ^ k) for h in range(head_count)] for k in range(1, head_count)]
    parts = [part] + [lax.ppermute(part, "head", pairs) for pairs in others]

    length = group_length[kv_head]
    within = jnp.arange(tokens, dtype=jnp.int32)
    rolled = (ctx_place * tokens + within - group_shift[kv_head]) % (tokens * ctx)
    low = (within - rolled % length).reshape(1, tokens)
    keep_masks = rank_keep_mask.astype(jnp.float32)[:, :, None]
    out, query_gradient, low_rank_part, grad_up_part, queries, weights, grad_scores = attention(
        spot,
        frozen_queries,
        output_gradient,
        up,
        [
            rank_keep_mask,
            low,
            own_k,
            own_v,
            *direct,
            *swapped,
            *parts,
        ],
    )

    low_parts = [low_rank_part] + [lax.ppermute(low_rank_part, "head", pairs) for pairs in others]
    send = kv_half(spot, weights, grad_scores, output_gradient, queries, keep=False)
    got = lax.ppermute(send, "head", swap)
    keep = kv_half(spot, weights, grad_scores, output_gradient, queries, keep=True)
    own_sum, one_sum, two_sum, *packs = pair_sum(keep, got, tokens)
    low_parts, grad_up_part, packs = lax.optimization_barrier((low_parts, grad_up_part, packs))
    low_total = sum(p.astype(jnp.float32) for p in low_parts)
    low_rank = (low_total * keep_masks[0] * adapter_scale).astype(jnp.bfloat16)
    grad_down_part = dot32(low_rank, inputs, NN).astype(jnp.bfloat16)
    packed = jnp.concatenate(
        [
            grad_down_part.reshape(ranks, down_rows, 128),
            grad_up_part.reshape(ranks, up_rows, 128),
        ],
        1,
    )
    received = lax.all_to_all(packed, "ctx", split_axis=0, concat_axis=0)

    packs = [across(p, -(n + 1)) for n, p in enumerate(packs)]
    own_sum, one_sum, two_sum = row_sum(spot, own_sum, one_sum, two_sum, packs)

    def home(piece, back):
        pairs = [
            (
                i * head_count + h,
                (i - back) % ctx * head_count + (h % CORES) * CORES + h // CORES,
            )
            for i in range(ctx)
            for h in range(head_count)
        ]
        return lax.ppermute(piece, ("ctx", "head"), pairs).astype(jnp.float32)

    kv_grad = home(own_sum, 0) + home(one_sum, COLUMNS) + home(two_sum, 2 * COLUMNS)

    keep_row = lax.dynamic_slice_in_dim(keep_masks[1], ctx_place, 1, 0)
    small = [
        a.reshape(-1, 128)
        for a in (
            adapter_down,
            down_first_moment,
            down_second_moment,
            adapter_up,
            up_first_moment,
            up_second_moment,
        )
    ]
    news = pl.pallas_call(
        adam_kernel,
        out_shape=[jax.ShapeDtypeStruct(a.shape, jnp.float32) for a in small],
        compiler_params=pltpu.CompilerParams(vmem_limit_bytes=8 << 20),
        name="adam",
    )(received, *small, keep_row)
    news = [n.reshape(1, -1) for n in news]
    return (out, query_gradient, kv_grad, *news)


def solution(mesh):
    both = P("ctx", "head")
    return jax.shard_map(
        on_device,
        mesh=mesh,
        in_specs=(both, P("ctx", None)) + (both,) * 8 + (P(), P(), P()),
        out_specs=(both,) * 9,
        check_vma=False,
    )
```

```python
import functools
import math

import jax
import jax.numpy as jnp
from jax import lax
from jax.experimental import pallas as pl
from jax.experimental.pallas import tpu as pltpu
from jax.sharding import PartitionSpec as P


HEAD_SIZE = 128
KVH = 2
REACH = 8
CORES = 2
COLUMNS = 4

adapter_scale = 0.25
beta_one = 0.9
beta_two = 0.999
learn_rate = 0.01
adam_epsilon = 1e-08


NN = (((1,), (0,)), ((), ()))
NT = (((1,), (1,)), ((), ()))


def dot32(a, b, dims):
    return lax.dot_general(a, b, dims, preferred_element_type=jnp.float32)


def distance(slot, column):
    if slot < 3:
        return (0, COLUMNS, 2 * COLUMNS)[slot]
    step, late = divmod(slot - 1, 2)
    near = column >= step
    return jnp.where(near, step + (0 if late else COLUMNS), step + (COLUMNS if late else 0))


def pack_kernel(spot_ref, own_ref, one_ref, two_ref, fq_ref, go_ref, mask_ref, *outs):
    column = spot_ref[1]
    packs, (fq_out, go_out, mask_out) = outs[: COLUMNS - 1], outs[COLUMNS - 1 :]
    for n, out in enumerate(packs):
        step = n + 1
        out[0] = one_ref[...]

        @pl.when(column + step < COLUMNS)
        def _():
            out[1] = own_ref[...]

        @pl.when(column + step >= COLUMNS)
        def _():
            out[1] = two_ref[...]

    for h in range(fq_out.shape[0]):
        lanes = pl.ds(h * HEAD_SIZE, HEAD_SIZE)
        fq_out[h] = fq_ref[:, lanes]
        go_out[h] = go_ref[:, lanes]
    mask_out[...] = mask_ref[...]


def pack(spot, own, one, two, fq, go, masks):
    tokens, width = fq.shape
    vmem = pl.BlockSpec(memory_space=pltpu.VMEM)
    by_head = jax.ShapeDtypeStruct((width // HEAD_SIZE, tokens, HEAD_SIZE), jnp.bfloat16)
    *packs, fq, go, masks = pl.pallas_call(
        pack_kernel,
        in_specs=[pl.BlockSpec(memory_space=pltpu.SMEM)] + [vmem] * 6,
        out_shape=[jax.ShapeDtypeStruct((2,) + own.shape, own.dtype)] * (COLUMNS - 1)
        + [by_head, by_head, jax.ShapeDtypeStruct(masks.shape, masks.dtype)],
        compiler_params=pltpu.CompilerParams(vmem_limit_bytes=8 << 20),
        name="pack",
    )(spot, own, one, two, fq, go, masks)
    return packs, fq, go, masks


def column_of(row):
    n = row.shape[1]
    eye = lax.broadcasted_iota(jnp.int32, (n, n), 0) == lax.broadcasted_iota(jnp.int32, (n, n), 1)
    return jnp.sum(jnp.where(eye, jnp.broadcast_to(row, (n, n)), 0.0), axis=1, keepdims=True)


def fold(combine, start, x):
    for r in range(0, x.shape[0], 8):
        start = combine(start, x[r : r + 8])
    return start


def attention_kernel(*refs, tokens, heads, score_scale):
    tiles = REACH + 1
    (spot_ref, fq_ref, go_ref, up_ref, mask_ref, low_ref, own_k_ref, own_v_ref) = refs[:8]
    direct, swapped = refs[8:13], refs[13:18]
    parts = refs[18:22]
    out_ref, gq_ref, low_rank_ref, grad_up_ref, q_ref, w_ref, gs_ref = refs[22:29]
    (k_s, v_s, kt_s, vt_s, place_s, s_s, gw_s, a_s, acc_s, lr_s) = refs[29:]
    core = spot_ref[0]
    column = spot_ref[1]
    exponent = score_scale * math.log2(math.e)

    def rows(d):
        return pl.ds(d * tokens, tokens)

    k_s[rows(0), :] = own_k_ref[...]
    v_s[rows(0), :] = own_v_ref[...]

    def fill(store, pieces):
        store[rows(1), :] = pieces[0][...]
        store[rows(2), :] = pieces[1][...]
        for n in range(1, COLUMNS):
            store[rows(2 * n + 1), :] = pieces[n + 1][0]
            store[rows(2 * n + 2), :] = pieces[n + 1][1]

    @pl.when(core == 0)
    def _():
        fill(k_s, direct)
        fill(v_s, swapped)

    @pl.when(core != 0)
    def _():
        fill(k_s, swapped)
        fill(v_s, direct)

    low = low_ref[...]
    place_s[...] = lax.broadcasted_iota(jnp.int32, (tokens, tokens), 0)
    lr_s[...] = jnp.zeros_like(lr_s)
    masks = mask_ref[...].astype(jnp.float32)
    keep0, keep1 = column_of(masks[0:1]), column_of(masks[1:2])
    total = (parts[0][...].astype(jnp.float32) + parts[1][...].astype(jnp.float32)) + (
        parts[2][...].astype(jnp.float32) + parts[3][...].astype(jnp.float32)
    )
    mpt = (total * keep0).astype(jnp.bfloat16)
    mp = mpt.astype(jnp.float32).T.astype(jnp.bfloat16)

    def lanes(head):
        return pl.ds(pl.multiple_of(head * HEAD_SIZE, HEAD_SIZE), HEAD_SIZE)

    def up_of(head):
        return (up_ref[:, lanes(head)].astype(jnp.float32) * keep1).astype(jnp.bfloat16)

    def make_query(head):
        q_ref[head] = (
            fq_ref[head].astype(jnp.float32) + adapter_scale * dot32(mp, up_of(head), NN)
        ).astype(jnp.bfloat16)

    def products(head, slot, d, top):
        s = dot32(k_s[rows(d), :], q_ref[head], NT)
        allowed = place_s[...] >= low + distance(d, column) * tokens
        if d == 0:
            allowed = allowed & (place_s[...] <= lax.broadcasted_iota(jnp.int32, s.shape, 1))
        s = jnp.where(allowed, s, -1e30)
        s_s[slot, rows(d), :] = s
        gw_s[slot, rows(d), :] = dot32(v_s[rows(d), :], go_ref[head], NT)
        if isinstance(head, int):
            kt_s[:, rows(d)] = k_s[rows(d), :].T
            vt_s[:, rows(d)] = v_s[rows(d), :].T
        return fold(jnp.maximum, top, s)

    lowest = jnp.full((8, tokens), -1e30, jnp.float32)
    zero = jnp.zeros((8, tokens), jnp.float32)
    make_query(0)
    top = lowest
    for d in range(tiles):
        top = products(0, 0, d, top)

    def one_head(head, top, last):
        slot = lax.rem(head, 2)
        top = jnp.max(top, axis=0, keepdims=True)
        if not last:
            make_query(head + 1)

        total, next_top = zero, lowest
        for d in range(tiles):
            p = jnp.exp2((s_s[slot, rows(d), :] - top) * exponent)
            a_s[slot, rows(d), :] = p
            total = fold(jnp.add, total, p)
            if not last:
                next_top = products(head + 1, 1 - slot, d, next_top)
        inverse = 1.0 / jnp.sum(total, axis=0, keepdims=True)
        acc_s[...] = jnp.zeros_like(acc_s)

        dots = zero
        for d in range(tiles):
            w = a_s[slot, rows(d), :] * inverse
            w_half = w.astype(jnp.bfloat16)
            w_ref[head, rows(d), :] = w_half
            a = w * gw_s[slot, rows(d), :]
            gw_s[slot, rows(d), :] = a
            acc_s[...] += dot32(vt_s[:, rows(d)], w_half, NN)
            dots = fold(jnp.add, dots, a)
        out_ref[:, lanes(head)] = acc_s[...].T.astype(jnp.bfloat16)
        dots = jnp.sum(dots, axis=0, keepdims=True) * inverse
        acc_s[...] = jnp.zeros_like(acc_s)

        for d in range(tiles):
            gs = (gw_s[slot, rows(d), :] - a_s[slot, rows(d), :] * dots).astype(jnp.bfloat16)
            gs_ref[head, rows(d), :] = gs
            acc_s[...] += dot32(kt_s[:, rows(d)], gs, NN)
        gq_t = (score_scale * acc_s[...]).astype(jnp.bfloat16)
        gq = (gq_t.astype(jnp.float32).T).astype(jnp.bfloat16)
        gq_ref[:, lanes(head)] = gq
        lr_s[...] += dot32(up_of(head), gq_t, NN)
        grad_up_ref[:, lanes(head)] = (adapter_scale * dot32(mpt, gq, NN)).astype(jnp.bfloat16)
        return next_top

    top = lax.fori_loop(0, heads - 1, lambda h, t: one_head(h, t, False), top)
    one_head(heads - 1, top, True)
    low_rank_ref[...] = lr_s[...].astype(jnp.bfloat16)


def attention(spot, fq, go, up, rest):
    heads, tokens, _ = fq.shape
    ranks, width = up.shape
    span = (REACH + 1) * tokens
    vmem = pl.BlockSpec(memory_space=pltpu.VMEM)
    return pl.pallas_call(
        functools.partial(
            attention_kernel, tokens=tokens, heads=heads, score_scale=1.0 / math.sqrt(HEAD_SIZE)
        ),
        in_specs=[pl.BlockSpec(memory_space=pltpu.SMEM)] + [vmem] * (3 + len(rest)),
        out_specs=[vmem] * 7,
        scratch_shapes=[
            pltpu.VMEM((span, HEAD_SIZE), jnp.bfloat16),
            pltpu.VMEM((span, HEAD_SIZE), jnp.bfloat16),
            pltpu.VMEM((HEAD_SIZE, span), jnp.bfloat16),
            pltpu.VMEM((HEAD_SIZE, span), jnp.bfloat16),
            pltpu.VMEM((tokens, tokens), jnp.int32),
            pltpu.VMEM((2, span, tokens), jnp.float32),
            pltpu.VMEM((2, span, tokens), jnp.float32),
            pltpu.VMEM((2, span, tokens), jnp.float32),
            pltpu.VMEM((HEAD_SIZE, tokens), jnp.float32),
            pltpu.VMEM((ranks, tokens), jnp.float32),
        ],
        out_shape=[
            jax.ShapeDtypeStruct((tokens, width), jnp.bfloat16),
            jax.ShapeDtypeStruct((tokens, width), jnp.bfloat16),
            jax.ShapeDtypeStruct((ranks, tokens), jnp.bfloat16),
            jax.ShapeDtypeStruct((ranks, width), jnp.bfloat16),
            jax.ShapeDtypeStruct((heads, tokens, HEAD_SIZE), jnp.bfloat16),
            jax.ShapeDtypeStruct((heads, span, tokens), jnp.bfloat16),
            jax.ShapeDtypeStruct((heads, span, tokens), jnp.bfloat16),
        ],
        compiler_params=pltpu.CompilerParams(vmem_limit_bytes=24 << 20),
        cost_estimate=pl.CostEstimate(
            flops=8 * heads * tokens * span * HEAD_SIZE,
            bytes_accessed=8 << 20,
            transcendentals=heads * tokens * span,
        ),
        name="attention",
    )(spot, fq, go, up, *rest)


def kv_half_kernel(spot_ref, w_ref, gs_ref, go_ref, q_ref, half_ref, *, keep, score_scale):
    heads, span, tokens = w_ref.shape
    values = (spot_ref[0] == 0) != keep

    def product(left_ref, right_ref, scale):
        right = jnp.concatenate([right_ref[h] for h in range(heads)], 0)
        for d in range(span // tokens):
            rows = pl.ds(d * tokens, tokens)
            left = jnp.concatenate([left_ref[h, rows, :] for h in range(heads)], 1)
            half_ref[rows, :] = (scale * dot32(left, right, NN)).astype(half_ref.dtype)

    @pl.when(values)
    def _():
        product(w_ref, go_ref, 1.0)

    @pl.when(jnp.logical_not(values))
    def _():
        product(gs_ref, q_ref, score_scale)


def kv_half(spot, weights, grad_scores, go, queries, keep):
    span = weights.shape[1]
    vmem = pl.BlockSpec(memory_space=pltpu.VMEM)
    return pl.pallas_call(
        functools.partial(kv_half_kernel, keep=keep, score_scale=1.0 / math.sqrt(HEAD_SIZE)),
        in_specs=[pl.BlockSpec(memory_space=pltpu.SMEM)] + [vmem] * 4,
        out_specs=vmem,
        out_shape=jax.ShapeDtypeStruct((span, HEAD_SIZE), jnp.float32 if keep else jnp.bfloat16),
        compiler_params=pltpu.CompilerParams(vmem_limit_bytes=6 << 20),
        cost_estimate=pl.CostEstimate(
            flops=2 * span * queries.size, bytes_accessed=2 << 20, transcendentals=0
        ),
        name="kv_keep" if keep else "kv_send",
    )(spot, weights, grad_scores, go, queries)


def pair_sum_kernel(keep_ref, got_ref, own_ref, one_ref, two_ref, *packs):
    tokens = own_ref.shape[0]

    def total(d):
        rows = pl.ds(d * tokens, tokens)
        return keep_ref[rows, :] + got_ref[rows, :].astype(jnp.float32)

    own_ref[...] = total(0)
    one_ref[...] = total(1)
    two_ref[...] = total(2)
    for n, pack_ref in enumerate(packs):
        pack_ref[0] = total(2 * n + 3).astype(jnp.bfloat16)
        pack_ref[1] = total(2 * n + 4).astype(jnp.bfloat16)


def pair_sum(keep, got, tokens):
    tile = (tokens, HEAD_SIZE)
    return pl.pallas_call(
        pair_sum_kernel,
        out_shape=[jax.ShapeDtypeStruct(tile, jnp.float32)] * 3
        + [jax.ShapeDtypeStruct((2,) + tile, jnp.bfloat16)] * (COLUMNS - 1),
        compiler_params=pltpu.CompilerParams(vmem_limit_bytes=12 << 20),
        name="pair_sum",
    )(keep, got)


def row_sum_kernel(spot_ref, own_ref, one_ref, two_ref, *rest):
    column = spot_ref[1]
    packs, (own_out, one_out, two_out) = rest[: COLUMNS - 1], rest[COLUMNS - 1 :]
    own, one, two = own_ref[...], one_ref[...], two_ref[...]
    for n, pack_ref in enumerate(packs):
        one = one + pack_ref[0].astype(jnp.float32)
        piece = pack_ref[1].astype(jnp.float32)
        near = jnp.full(piece.shape, n + 1, jnp.int32) + column < COLUMNS
        own = own + jnp.where(near, piece, 0.0)
        two = two + jnp.where(near, 0.0, piece)
    own_out[...] = own.astype(jnp.bfloat16)
    one_out[...] = one.astype(jnp.bfloat16)
    two_out[...] = two.astype(jnp.bfloat16)


def row_sum(spot, own, one, two, packs):
    vmem = pl.BlockSpec(memory_space=pltpu.VMEM)
    return pl.pallas_call(
        row_sum_kernel,
        in_specs=[pl.BlockSpec(memory_space=pltpu.SMEM)] + [vmem] * (2 + COLUMNS),
        out_shape=[jax.ShapeDtypeStruct(own.shape, jnp.bfloat16)] * 3,
        compiler_params=pltpu.CompilerParams(vmem_limit_bytes=8 << 20),
        name="row_sum",
    )(spot, own, one, two, *packs)


def spread_kernel(down_ref, up_ref, out_ref):
    row = jnp.concatenate([down_ref[...], up_ref[...]], 0).astype(jnp.bfloat16)
    for n in range(out_ref.shape[0]):
        out_ref[n] = row


def spread(down, up, copies):
    return pl.pallas_call(
        spread_kernel,
        out_shape=jax.ShapeDtypeStruct((copies, down.shape[0] + up.shape[0], 128), jnp.bfloat16),
        compiler_params=pltpu.CompilerParams(vmem_limit_bytes=4 << 20),
        name="spread",
    )(down, up)


def adam_kernel(got_ref, pd, md, vd, pu, mu, vu, keep_ref, opd, omd, ovd, opu, omu, ovu):
    down_rows = pd.shape[0]
    total = jnp.sum(got_ref[...].astype(jnp.float32), axis=0)
    grads = (total[:down_rows], total[down_rows:] * keep_ref[0, 0])
    for grad, p, m, v, op, om, ov in (
        (grads[0], pd, md, vd, opd, omd, ovd),
        (grads[1], pu, mu, vu, opu, omu, ovu),
    ):
        first = beta_one * m[...] + (1.0 - beta_one) * grad
        second = beta_two * v[...] + (1.0 - beta_two) * grad * grad
        op[...] = p[...] - learn_rate * first / (jnp.sqrt(second) + adam_epsilon)
        om[...] = first
        ov[...] = second


def on_device(
    frozen_queries,
    key_value_rows,
    output_gradient,
    inputs,
    adapter_down,
    down_first_moment,
    down_second_moment,
    adapter_up,
    up_first_moment,
    up_second_moment,
    rank_keep_mask,
    group_length,
    group_shift,
):
    tokens = frozen_queries.shape[0]
    width = frozen_queries.shape[1]
    model = inputs.shape[1]
    ctx = lax.axis_size("ctx")
    head_count = lax.axis_size("head")
    ctx_place = lax.axis_index("ctx")
    head_place = lax.axis_index("head")
    core = head_place % CORES
    kv_head = head_place // CORES
    key_width = KVH * HEAD_SIZE
    ranks = rank_keep_mask.shape[1]

    column = ctx_place % COLUMNS
    spot = jnp.concatenate([core.reshape(1), column.reshape(1)]).astype(jnp.int32)
    own_k = lax.dynamic_slice_in_dim(key_value_rows, kv_head * HEAD_SIZE, HEAD_SIZE, 1)
    own_v = lax.dynamic_slice_in_dim(key_value_rows, key_width + kv_head * HEAD_SIZE, HEAD_SIZE, 1)
    mine = lax.dynamic_slice_in_dim(
        key_value_rows, core * key_width + kv_head * HEAD_SIZE, HEAD_SIZE, 1
    )
    swap = [(h, h ^ 1) for h in range(head_count)]

    def along(piece, step):
        return lax.ppermute(piece, "ctx", [(i, (i + step) % ctx) for i in range(ctx)])

    def across(piece, step):
        pairs = [(i, i // COLUMNS * COLUMNS + (i + step) % COLUMNS) for i in range(ctx)]
        return lax.ppermute(piece, "ctx", pairs)

    one, two = along(mine, COLUMNS), along(mine, 2 * COLUMNS)

    down_rows, up_rows = model // 128, width // 128
    row = spread(adapter_down.reshape(down_rows, 128), adapter_up.reshape(up_rows, 128), ctx)
    gathered = lax.all_to_all(row, "ctx", split_axis=0, concat_axis=0)
    packs, queries_in, grads_in, masks_in = pack(
        spot, mine, one, two, frozen_queries, output_gradient, rank_keep_mask
    )
    direct = [one, two] + [across(p, n + 1) for n, p in enumerate(packs)]
    swapped = [lax.ppermute(piece, "head", swap) for piece in direct]

    down = gathered[:, :down_rows].reshape(ranks, model)
    up = gathered[:, down_rows:].reshape(ranks, width)

    part = dot32(down, inputs, NT).astype(jnp.bfloat16)
    others = [[(h, h ^ k) for h in range(head_count)] for k in range(1, head_count)]
    parts = [part] + [lax.ppermute(part, "head", pairs) for pairs in others]

    length = group_length[kv_head]
    within = jnp.arange(tokens, dtype=jnp.int32)
    rolled = (ctx_place * tokens + within - group_shift[kv_head]) % (tokens * ctx)
    low = (within - rolled % length).reshape(1, tokens)
    keep_masks = rank_keep_mask.astype(jnp.float32)[:, :, None]
    out, query_gradient, low_rank_part, grad_up_part, queries, weights, grad_scores = attention(
        spot,
        queries_in,
        grads_in,
        up,
        [
            masks_in,
            low,
            own_k,
            own_v,
            *direct,
            *swapped,
            *parts,
        ],
    )

    low_parts = [low_rank_part] + [lax.ppermute(low_rank_part, "head", pairs) for pairs in others]
    send = kv_half(spot, weights, grad_scores, grads_in, queries, keep=False)
    got = lax.ppermute(send, "head", swap)
    keep = kv_half(spot, weights, grad_scores, grads_in, queries, keep=True)
    own_sum, one_sum, two_sum, *packs = pair_sum(keep, got, tokens)
    low_parts, grad_up_part, packs = lax.optimization_barrier((low_parts, grad_up_part, packs))
    low_total = sum(p.astype(jnp.float32) for p in low_parts)
    low_rank = (low_total * keep_masks[0] * adapter_scale).astype(jnp.bfloat16)
    grad_down_part = dot32(low_rank, inputs, NN).astype(jnp.bfloat16)
    packed = jnp.concatenate(
        [
            grad_down_part.reshape(ranks, down_rows, 128),
            grad_up_part.reshape(ranks, up_rows, 128),
        ],
        1,
    )
    received = lax.all_to_all(packed, "ctx", split_axis=0, concat_axis=0)

    packs = [across(p, -(n + 1)) for n, p in enumerate(packs)]
    own_sum, one_sum, two_sum = row_sum(spot, own_sum, one_sum, two_sum, packs)

    def home(piece, back):
        pairs = [
            (
                i * head_count + h,
                (i - back) % ctx * head_count + (h % CORES) * CORES + h // CORES,
            )
            for i in range(ctx)
            for h in range(head_count)
        ]
        return lax.ppermute(piece, ("ctx", "head"), pairs).astype(jnp.float32)

    kv_grad = home(own_sum, 0) + home(one_sum, COLUMNS) + home(two_sum, 2 * COLUMNS)

    keep_row = lax.dynamic_slice_in_dim(keep_masks[1], ctx_place, 1, 0)
    small = [
        a.reshape(-1, 128)
        for a in (
            adapter_down,
            down_first_moment,
            down_second_moment,
            adapter_up,
            up_first_moment,
            up_second_moment,
        )
    ]
    news = pl.pallas_call(
        adam_kernel,
        out_shape=[jax.ShapeDtypeStruct(a.shape, jnp.float32) for a in small],
        compiler_params=pltpu.CompilerParams(vmem_limit_bytes=8 << 20),
        name="adam",
    )(received, *small, keep_row)
    news = [n.reshape(1, -1) for n in news]
    return (out, query_gradient, kv_grad, *news)


def solution(mesh):
    both = P("ctx", "head")
    return jax.shard_map(
        on_device,
        mesh=mesh,
        in_specs=(both, P("ctx", None)) + (both,) * 8 + (P(), P(), P()),
        out_specs=(both,) * 9,
        check_vma=False,
    )
```

```python
import functools
import math

import jax
import jax.numpy as jnp
from jax import lax
from jax.experimental import pallas as pl
from jax.experimental.pallas import tpu as pltpu
from jax.sharding import PartitionSpec as P


HEAD_SIZE = 128
KVH = 2
REACH = 8
CORES = 2
COLUMNS = 4

adapter_scale = 0.25
beta_one = 0.9
beta_two = 0.999
learn_rate = 0.01
adam_epsilon = 1e-08


NN = (((1,), (0,)), ((), ()))
NT = (((1,), (1,)), ((), ()))


def dot32(a, b, dims):
    return lax.dot_general(a, b, dims, preferred_element_type=jnp.float32)


def distance(slot, column):
    if slot < 3:
        return (0, COLUMNS, 2 * COLUMNS)[slot]
    step, late = divmod(slot - 1, 2)
    near = column >= step
    return jnp.where(near, step + (0 if late else COLUMNS), step + (COLUMNS if late else 0))


def pack_kernel(spot_ref, own_ref, one_ref, two_ref, *outs):
    column = spot_ref[1]
    for n, out in enumerate(outs):
        step = n + 1
        out[0] = one_ref[...]

        @pl.when(column + step < COLUMNS)
        def _():
            out[1] = own_ref[...]

        @pl.when(column + step >= COLUMNS)
        def _():
            out[1] = two_ref[...]


def pack(spot, own, one, two):
    vmem = pl.BlockSpec(memory_space=pltpu.VMEM)
    return pl.pallas_call(
        pack_kernel,
        in_specs=[pl.BlockSpec(memory_space=pltpu.SMEM)] + [vmem] * 3,
        out_shape=[jax.ShapeDtypeStruct((2,) + own.shape, own.dtype)] * (COLUMNS - 1),
        compiler_params=pltpu.CompilerParams(vmem_limit_bytes=8 << 20),
        name="pack",
    )(spot, own, one, two)


def stage_kernel(fq_ref, go_ref, mask_ref, fq_out, go_out, mask_out):
    for h in range(fq_out.shape[0]):
        lanes = pl.ds(h * HEAD_SIZE, HEAD_SIZE)
        fq_out[h] = fq_ref[:, lanes]
        go_out[h] = go_ref[:, lanes]
    mask_out[...] = mask_ref[...]


def stage(fq, go, masks):
    tokens, width = fq.shape
    by_head = jax.ShapeDtypeStruct((width // HEAD_SIZE, tokens, HEAD_SIZE), jnp.bfloat16)
    return pl.pallas_call(
        stage_kernel,
        out_shape=[by_head, by_head, jax.ShapeDtypeStruct(masks.shape, masks.dtype)],
        compiler_params=pltpu.CompilerParams(vmem_limit_bytes=8 << 20),
        name="stage",
    )(fq, go, masks)


def column_of(row):
    n = row.shape[1]
    eye = lax.broadcasted_iota(jnp.int32, (n, n), 0) == lax.broadcasted_iota(jnp.int32, (n, n), 1)
    return jnp.sum(jnp.where(eye, jnp.broadcast_to(row, (n, n)), 0.0), axis=1, keepdims=True)


def fold(combine, start, x):
    for r in range(0, x.shape[0], 8):
        start = combine(start, x[r : r + 8])
    return start


def attention_kernel(*refs, tokens, heads, score_scale):
    tiles = REACH + 1
    (spot_ref, fq_ref, go_ref, up_ref, mask_ref, low_ref, own_k_ref, own_v_ref) = refs[:8]
    direct, swapped = refs[8:13], refs[13:18]
    parts = refs[18:22]
    out_ref, gq_ref, low_rank_ref, grad_up_ref, q_ref, w_ref, gs_ref = refs[22:29]
    (k_s, v_s, kt_s, vt_s, place_s, s_s, gw_s, a_s, acc_s, lr_s) = refs[29:]
    core = spot_ref[0]
    column = spot_ref[1]
    exponent = score_scale * math.log2(math.e)

    def rows(d):
        return pl.ds(d * tokens, tokens)

    k_s[rows(0), :] = own_k_ref[...]
    v_s[rows(0), :] = own_v_ref[...]

    def fill(store, pieces):
        store[rows(1), :] = pieces[0][...]
        store[rows(2), :] = pieces[1][...]
        for n in range(1, COLUMNS):
            store[rows(2 * n + 1), :] = pieces[n + 1][0]
            store[rows(2 * n + 2), :] = pieces[n + 1][1]

    @pl.when(core == 0)
    def _():
        fill(k_s, direct)
        fill(v_s, swapped)

    @pl.when(core != 0)
    def _():
        fill(k_s, swapped)
        fill(v_s, direct)

    low = low_ref[...]
    place_s[...] = lax.broadcasted_iota(jnp.int32, (tokens, tokens), 0)
    lr_s[...] = jnp.zeros_like(lr_s)
    masks = mask_ref[...].astype(jnp.float32)
    keep0, keep1 = column_of(masks[0:1]), column_of(masks[1:2])
    total = (parts[0][...].astype(jnp.float32) + parts[1][...].astype(jnp.float32)) + (
        parts[2][...].astype(jnp.float32) + parts[3][...].astype(jnp.float32)
    )
    mpt = (total * keep0).astype(jnp.bfloat16)
    mp = mpt.astype(jnp.float32).T.astype(jnp.bfloat16)

    def lanes(head):
        return pl.ds(pl.multiple_of(head * HEAD_SIZE, HEAD_SIZE), HEAD_SIZE)

    def up_of(head):
        return (up_ref[:, lanes(head)].astype(jnp.float32) * keep1).astype(jnp.bfloat16)

    def make_query(head):
        q_ref[head] = (
            fq_ref[head].astype(jnp.float32) + adapter_scale * dot32(mp, up_of(head), NN)
        ).astype(jnp.bfloat16)

    def scores(head, slot, d, top):
        s = dot32(k_s[rows(d), :], q_ref[head], NT)
        allowed = place_s[...] >= low + distance(d, column) * tokens
        if d == 0:
            allowed = allowed & (place_s[...] <= lax.broadcasted_iota(jnp.int32, s.shape, 1))
        s = jnp.where(allowed, s, -1e30)
        s_s[slot, rows(d), :] = s
        return fold(jnp.maximum, top, s)

    lowest = jnp.full((8, tokens), -1e30, jnp.float32)
    zero = jnp.zeros((8, tokens), jnp.float32)
    make_query(0)
    top = lowest
    for d in range(tiles):
        top = scores(0, 0, d, top)
        kt_s[:, rows(d)] = k_s[rows(d), :].T
        vt_s[:, rows(d)] = v_s[rows(d), :].T

    def one_head(head, top, last):
        slot = lax.rem(head, 2)
        top = jnp.max(top, axis=0, keepdims=True)
        if not last:
            make_query(head + 1)

        total, next_top = zero, lowest
        for d in range(tiles):
            p = jnp.exp2((s_s[slot, rows(d), :] - top) * exponent)
            a_s[slot, rows(d), :] = p
            total = fold(jnp.add, total, p)
            gw_s[slot, rows(d), :] = dot32(v_s[rows(d), :], go_ref[head], NT)
        inverse = 1.0 / jnp.sum(total, axis=0, keepdims=True)
        acc_s[...] = jnp.zeros_like(acc_s)

        dots = zero
        for d in range(tiles):
            w = a_s[slot, rows(d), :] * inverse
            w_half = w.astype(jnp.bfloat16)
            w_ref[head, rows(d), :] = w_half
            a = w * gw_s[slot, rows(d), :]
            gw_s[slot, rows(d), :] = a
            acc_s[...] += dot32(vt_s[:, rows(d)], w_half, NN)
            dots = fold(jnp.add, dots, a)
            if not last:
                next_top = scores(head + 1, 1 - slot, d, next_top)
        out_ref[:, lanes(head)] = acc_s[...].T.astype(jnp.bfloat16)
        dots = jnp.sum(dots, axis=0, keepdims=True) * inverse
        acc_s[...] = jnp.zeros_like(acc_s)

        for d in range(tiles):
            gs = (gw_s[slot, rows(d), :] - a_s[slot, rows(d), :] * dots).astype(jnp.bfloat16)
            gs_ref[head, rows(d), :] = gs
            acc_s[...] += dot32(kt_s[:, rows(d)], gs, NN)
        gq_t = (score_scale * acc_s[...]).astype(jnp.bfloat16)
        gq = (gq_t.astype(jnp.float32).T).astype(jnp.bfloat16)
        gq_ref[:, lanes(head)] = gq
        lr_s[...] += dot32(up_of(head), gq_t, NN)
        grad_up_ref[:, lanes(head)] = (adapter_scale * dot32(mpt, gq, NN)).astype(jnp.bfloat16)
        return next_top

    top = lax.fori_loop(0, heads - 1, lambda h, t: one_head(h, t, False), top)
    one_head(heads - 1, top, True)
    low_rank_ref[...] = lr_s[...].astype(jnp.bfloat16)


def attention(spot, fq, go, up, rest):
    heads, tokens, _ = fq.shape
    ranks, width = up.shape
    span = (REACH + 1) * tokens
    vmem = pl.BlockSpec(memory_space=pltpu.VMEM)
    return pl.pallas_call(
        functools.partial(
            attention_kernel, tokens=tokens, heads=heads, score_scale=1.0 / math.sqrt(HEAD_SIZE)
        ),
        in_specs=[pl.BlockSpec(memory_space=pltpu.SMEM)] + [vmem] * (3 + len(rest)),
        out_specs=[vmem] * 7,
        scratch_shapes=[
            pltpu.VMEM((span, HEAD_SIZE), jnp.bfloat16),
            pltpu.VMEM((span, HEAD_SIZE), jnp.bfloat16),
            pltpu.VMEM((HEAD_SIZE, span), jnp.bfloat16),
            pltpu.VMEM((HEAD_SIZE, span), jnp.bfloat16),
            pltpu.VMEM((tokens, tokens), jnp.int32),
            pltpu.VMEM((2, span, tokens), jnp.float32),
            pltpu.VMEM((2, span, tokens), jnp.float32),
            pltpu.VMEM((2, span, tokens), jnp.float32),
            pltpu.VMEM((HEAD_SIZE, tokens), jnp.float32),
            pltpu.VMEM((ranks, tokens), jnp.float32),
        ],
        out_shape=[
            jax.ShapeDtypeStruct((tokens, width), jnp.bfloat16),
            jax.ShapeDtypeStruct((tokens, width), jnp.bfloat16),
            jax.ShapeDtypeStruct((ranks, tokens), jnp.bfloat16),
            jax.ShapeDtypeStruct((ranks, width), jnp.bfloat16),
            jax.ShapeDtypeStruct((heads, tokens, HEAD_SIZE), jnp.bfloat16),
            jax.ShapeDtypeStruct((heads, span, tokens), jnp.bfloat16),
            jax.ShapeDtypeStruct((heads, span, tokens), jnp.bfloat16),
        ],
        compiler_params=pltpu.CompilerParams(vmem_limit_bytes=24 << 20),
        cost_estimate=pl.CostEstimate(
            flops=8 * heads * tokens * span * HEAD_SIZE,
            bytes_accessed=8 << 20,
            transcendentals=heads * tokens * span,
        ),
        name="attention",
    )(spot, fq, go, up, *rest)


def kv_half_kernel(spot_ref, w_ref, gs_ref, go_ref, q_ref, half_ref, *, keep, score_scale):
    heads, span, tokens = w_ref.shape
    values = (spot_ref[0] == 0) != keep

    def product(left_ref, right_ref, scale):
        right = jnp.concatenate([right_ref[h] for h in range(heads)], 0)
        for d in range(span // tokens):
            rows = pl.ds(d * tokens, tokens)
            left = jnp.concatenate([left_ref[h, rows, :] for h in range(heads)], 1)
            half_ref[rows, :] = (scale * dot32(left, right, NN)).astype(half_ref.dtype)

    @pl.when(values)
    def _():
        product(w_ref, go_ref, 1.0)

    @pl.when(jnp.logical_not(values))
    def _():
        product(gs_ref, q_ref, score_scale)


def kv_half(spot, weights, grad_scores, go, queries, keep):
    span = weights.shape[1]
    vmem = pl.BlockSpec(memory_space=pltpu.VMEM)
    return pl.pallas_call(
        functools.partial(kv_half_kernel, keep=keep, score_scale=1.0 / math.sqrt(HEAD_SIZE)),
        in_specs=[pl.BlockSpec(memory_space=pltpu.SMEM)] + [vmem] * 4,
        out_specs=vmem,
        out_shape=jax.ShapeDtypeStruct((span, HEAD_SIZE), jnp.float32 if keep else jnp.bfloat16),
        compiler_params=pltpu.CompilerParams(vmem_limit_bytes=6 << 20),
        cost_estimate=pl.CostEstimate(
            flops=2 * span * queries.size, bytes_accessed=2 << 20, transcendentals=0
        ),
        name="kv_keep" if keep else "kv_send",
    )(spot, weights, grad_scores, go, queries)


def pair_sum_kernel(keep_ref, got_ref, own_ref, one_ref, two_ref, *packs):
    tokens = own_ref.shape[0]

    def total(d):
        rows = pl.ds(d * tokens, tokens)
        return keep_ref[rows, :] + got_ref[rows, :].astype(jnp.float32)

    own_ref[...] = total(0)
    one_ref[...] = total(1)
    two_ref[...] = total(2)
    for n, pack_ref in enumerate(packs):
        pack_ref[0] = total(2 * n + 3).astype(jnp.bfloat16)
        pack_ref[1] = total(2 * n + 4).astype(jnp.bfloat16)


def pair_sum(keep, got, tokens):
    tile = (tokens, HEAD_SIZE)
    return pl.pallas_call(
        pair_sum_kernel,
        out_shape=[jax.ShapeDtypeStruct(tile, jnp.float32)] * 3
        + [jax.ShapeDtypeStruct((2,) + tile, jnp.bfloat16)] * (COLUMNS - 1),
        compiler_params=pltpu.CompilerParams(vmem_limit_bytes=12 << 20),
        name="pair_sum",
    )(keep, got)


def row_sum_kernel(spot_ref, own_ref, one_ref, two_ref, *rest):
    column = spot_ref[1]
    packs, (own_out, one_out, two_out) = rest[: COLUMNS - 1], rest[COLUMNS - 1 :]
    own, one, two = own_ref[...], one_ref[...], two_ref[...]
    for n, pack_ref in enumerate(packs):
        one = one + pack_ref[0].astype(jnp.float32)
        piece = pack_ref[1].astype(jnp.float32)
        near = jnp.full(piece.shape, n + 1, jnp.int32) + column < COLUMNS
        own = own + jnp.where(near, piece, 0.0)
        two = two + jnp.where(near, 0.0, piece)
    own_out[...] = own.astype(jnp.bfloat16)
    one_out[...] = one.astype(jnp.bfloat16)
    two_out[...] = two.astype(jnp.bfloat16)


def row_sum(spot, own, one, two, packs):
    vmem = pl.BlockSpec(memory_space=pltpu.VMEM)
    return pl.pallas_call(
        row_sum_kernel,
        in_specs=[pl.BlockSpec(memory_space=pltpu.SMEM)] + [vmem] * (2 + COLUMNS),
        out_shape=[jax.ShapeDtypeStruct(own.shape, jnp.bfloat16)] * 3,
        compiler_params=pltpu.CompilerParams(vmem_limit_bytes=8 << 20),
        name="row_sum",
    )(spot, own, one, two, *packs)


def spread_kernel(down_ref, up_ref, out_ref, down_s, up_s, sems):
    loads = [
        pltpu.make_async_copy(down_ref, down_s, sems.at[0]),
        pltpu.make_async_copy(up_ref, up_s, sems.at[1]),
    ]
    for load in loads:
        load.start()
    for load in loads:
        load.wait()
    row = jnp.concatenate([down_s[...], up_s[...]], 0).astype(jnp.bfloat16)
    for n in range(out_ref.shape[0]):
        out_ref[n] = row


def spread(down, up, copies):
    return pl.pallas_call(
        spread_kernel,
        in_specs=[pl.BlockSpec(memory_space=pl.ANY)] * 2,
        scratch_shapes=[
            pltpu.VMEM(down.shape, down.dtype),
            pltpu.VMEM(up.shape, up.dtype),
            pltpu.SemaphoreType.DMA((2,)),
        ],
        out_shape=jax.ShapeDtypeStruct((copies, down.shape[0] + up.shape[0], 128), jnp.bfloat16),
        compiler_params=pltpu.CompilerParams(vmem_limit_bytes=63 << 20),
        name="spread",
    )(down, up)


def adam_kernel(got_ref, pd, md, vd, pu, mu, vu, keep_ref, opd, omd, ovd, opu, omu, ovu):
    down_rows = pd.shape[0]
    total = jnp.sum(got_ref[...].astype(jnp.float32), axis=0)
    grads = (total[:down_rows], total[down_rows:] * keep_ref[0, 0])
    for grad, p, m, v, op, om, ov in (
        (grads[0], pd, md, vd, opd, omd, ovd),
        (grads[1], pu, mu, vu, opu, omu, ovu),
    ):
        first = beta_one * m[...] + (1.0 - beta_one) * grad
        second = beta_two * v[...] + (1.0 - beta_two) * grad * grad
        op[...] = p[...] - learn_rate * first / (jnp.sqrt(second) + adam_epsilon)
        om[...] = first
        ov[...] = second


def on_device(
    frozen_queries,
    key_value_rows,
    output_gradient,
    inputs,
    adapter_down,
    down_first_moment,
    down_second_moment,
    adapter_up,
    up_first_moment,
    up_second_moment,
    rank_keep_mask,
    group_length,
    group_shift,
):
    tokens = frozen_queries.shape[0]
    width = frozen_queries.shape[1]
    model = inputs.shape[1]
    ctx = lax.axis_size("ctx")
    head_count = lax.axis_size("head")
    ctx_place = lax.axis_index("ctx")
    head_place = lax.axis_index("head")
    core = head_place % CORES
    kv_head = head_place // CORES
    key_width = KVH * HEAD_SIZE
    ranks = rank_keep_mask.shape[1]

    column = ctx_place % COLUMNS
    spot = jnp.concatenate([core.reshape(1), column.reshape(1)]).astype(jnp.int32)
    own_k = lax.dynamic_slice_in_dim(key_value_rows, kv_head * HEAD_SIZE, HEAD_SIZE, 1)
    own_v = lax.dynamic_slice_in_dim(key_value_rows, key_width + kv_head * HEAD_SIZE, HEAD_SIZE, 1)
    mine = lax.dynamic_slice_in_dim(
        key_value_rows, core * key_width + kv_head * HEAD_SIZE, HEAD_SIZE, 1
    )
    swap = [(h, h ^ 1) for h in range(head_count)]

    def along(piece, step):
        return lax.ppermute(piece, "ctx", [(i, (i + step) % ctx) for i in range(ctx)])

    def across(piece, step):
        pairs = [(i, i // COLUMNS * COLUMNS + (i + step) % COLUMNS) for i in range(ctx)]
        return lax.ppermute(piece, "ctx", pairs)

    one, two = along(mine, COLUMNS), along(mine, 2 * COLUMNS)

    down_rows, up_rows = model // 128, width // 128
    row = spread(adapter_down.reshape(down_rows, 128), adapter_up.reshape(up_rows, 128), ctx)
    gathered = lax.all_to_all(row, "ctx", split_axis=0, concat_axis=0)
    packs = pack(spot, mine, one, two)
    direct = [one, two] + [across(p, n + 1) for n, p in enumerate(packs)]
    queries_in, grads_in, masks_in = stage(frozen_queries, output_gradient, rank_keep_mask)
    swapped = [lax.ppermute(piece, "head", swap) for piece in direct]

    down = gathered[:, :down_rows].reshape(ranks, model)
    up = gathered[:, down_rows:].reshape(ranks, width)

    part = dot32(down, inputs, NT).astype(jnp.bfloat16)
    others = [[(h, h ^ k) for h in range(head_count)] for k in range(1, head_count)]
    parts = [part] + [lax.ppermute(part, "head", pairs) for pairs in others]

    length = jnp.where(kv_head == 0, group_length[0:1], group_length[1:2])
    shift = jnp.where(kv_head == 0, group_shift[0:1], group_shift[1:2])
    within = jnp.arange(tokens, dtype=jnp.int32)
    rolled = (ctx_place * tokens + within - shift) % (tokens * ctx)
    low = (within - rolled % length).reshape(1, tokens)
    keep_masks = rank_keep_mask.astype(jnp.float32)[:, :, None]
    out, query_gradient, low_rank_part, grad_up_part, queries, weights, grad_scores = attention(
        spot,
        queries_in,
        grads_in,
        up,
        [
            masks_in,
            low,
            own_k,
            own_v,
            *direct,
            *swapped,
            *parts,
        ],
    )

    low_parts = [low_rank_part] + [lax.ppermute(low_rank_part, "head", pairs) for pairs in others]
    send = kv_half(spot, weights, grad_scores, grads_in, queries, keep=False)
    got = lax.ppermute(send, "head", swap)
    keep = kv_half(spot, weights, grad_scores, grads_in, queries, keep=True)
    own_sum, one_sum, two_sum, *packs = pair_sum(keep, got, tokens)
    low_parts, grad_up_part, packs = lax.optimization_barrier((low_parts, grad_up_part, packs))
    low_total = sum(p.astype(jnp.float32) for p in low_parts)
    low_rank = (low_total * keep_masks[0] * adapter_scale).astype(jnp.bfloat16)
    grad_down_part = dot32(low_rank, inputs, NN).astype(jnp.bfloat16)
    packed = jnp.concatenate(
        [
            grad_down_part.reshape(ranks, down_rows, 128),
            grad_up_part.reshape(ranks, up_rows, 128),
        ],
        1,
    )
    received = lax.all_to_all(packed, "ctx", split_axis=0, concat_axis=0)

    packs = [across(p, -(n + 1)) for n, p in enumerate(packs)]
    own_sum, one_sum, two_sum = row_sum(spot, own_sum, one_sum, two_sum, packs)

    def home(piece, back):
        pairs = [
            (
                i * head_count + h,
                (i - back) % ctx * head_count + (h % CORES) * CORES + h // CORES,
            )
            for i in range(ctx)
            for h in range(head_count)
        ]
        return lax.ppermute(piece, ("ctx", "head"), pairs).astype(jnp.float32)

    kv_grad = home(own_sum, 0) + home(one_sum, COLUMNS) + home(two_sum, 2 * COLUMNS)

    keep_row = lax.dynamic_slice_in_dim(keep_masks[1], ctx_place, 1, 0)
    small = [
        a.reshape(-1, 128)
        for a in (
            adapter_down,
            down_first_moment,
            down_second_moment,
            adapter_up,
            up_first_moment,
            up_second_moment,
        )
    ]
    news = pl.pallas_call(
        adam_kernel,
        out_shape=[jax.ShapeDtypeStruct(a.shape, jnp.float32) for a in small],
        compiler_params=pltpu.CompilerParams(vmem_limit_bytes=8 << 20),
        name="adam",
    )(received, *small, keep_row)
    news = [n.reshape(1, -1) for n in news]
    return (out, query_gradient, kv_grad, *news)


def solution(mesh):
    both = P("ctx", "head")
    return jax.shard_map(
        on_device,
        mesh=mesh,
        in_specs=(both, P("ctx", None)) + (both,) * 8 + (P(), P(), P()),
        out_specs=(both,) * 9,
        check_vma=False,
    )
```

```python
import functools
import math

import jax
import jax.numpy as jnp
from jax import lax
from jax.experimental import pallas as pl
from jax.experimental.pallas import tpu as pltpu
from jax.sharding import PartitionSpec as P


HEAD_SIZE = 128
KVH = 2
REACH = 8
CORES = 2
COLUMNS = 4

adapter_scale = 0.25
beta_one = 0.9
beta_two = 0.999
learn_rate = 0.01
adam_epsilon = 1e-08


NN = (((1,), (0,)), ((), ()))
NT = (((1,), (1,)), ((), ()))


def dot32(a, b, dims):
    return lax.dot_general(a, b, dims, preferred_element_type=jnp.float32)


def core_of():
    return lax.rem(lax.axis_index("head"), CORES)


def column_place():
    return lax.rem(lax.axis_index("ctx"), COLUMNS)


def distance(slot, column):
    if slot < 3:
        return (0, COLUMNS, 2 * COLUMNS)[slot]
    step, late = divmod(slot - 1, 2)
    near = column >= step
    return jnp.where(near, step + (0 if late else COLUMNS), step + (COLUMNS if late else 0))


def pack_kernel(own_ref, one_ref, two_ref, *outs):
    column = column_place()
    for n, out in enumerate(outs):
        step = n + 1
        out[0] = one_ref[...]

        @pl.when(column + step < COLUMNS)
        def _():
            out[1] = own_ref[...]

        @pl.when(column + step >= COLUMNS)
        def _():
            out[1] = two_ref[...]


def pack(own, one, two):
    vmem = pl.BlockSpec(memory_space=pltpu.VMEM)
    return pl.pallas_call(
        pack_kernel,
        in_specs=[vmem] * 3,
        out_shape=[jax.ShapeDtypeStruct((2,) + own.shape, own.dtype)] * (COLUMNS - 1),
        compiler_params=pltpu.CompilerParams(vmem_limit_bytes=8 << 20),
        name="pack",
    )(own, one, two)


def stage_kernel(
    length_ref, shift_ref, fq_ref, go_ref, mask_ref, fq_out, go_out, mask_out, low_out, *, seq_total
):
    tokens = fq_ref.shape[0]
    kv_head = lax.axis_index("head") // CORES
    length = length_ref[kv_head]
    first = lax.rem(lax.axis_index("ctx") * tokens - shift_ref[kv_head] + seq_total, seq_total)
    within = lax.broadcasted_iota(jnp.int32, (1, tokens), 1)
    in_group = within + lax.rem(first, length)
    in_group = jnp.where(in_group >= length, in_group - length, in_group)
    rolled = within + first
    low_out[...] = within - jnp.where(rolled >= seq_total, rolled - seq_total, in_group)
    for h in range(fq_out.shape[0]):
        lanes = pl.ds(h * HEAD_SIZE, HEAD_SIZE)
        fq_out[h] = fq_ref[:, lanes]
        go_out[h] = go_ref[:, lanes]
    mask_out[...] = mask_ref[...]


def stage(length, shift, fq, go, masks, seq_total):
    tokens, width = fq.shape
    vmem = pl.BlockSpec(memory_space=pltpu.VMEM)
    by_head = jax.ShapeDtypeStruct((width // HEAD_SIZE, tokens, HEAD_SIZE), jnp.bfloat16)
    return pl.pallas_call(
        functools.partial(stage_kernel, seq_total=seq_total),
        in_specs=[pl.BlockSpec(memory_space=pltpu.SMEM)] * 2 + [vmem] * 3,
        out_shape=[
            by_head,
            by_head,
            jax.ShapeDtypeStruct(masks.shape, masks.dtype),
            jax.ShapeDtypeStruct((1, tokens), jnp.int32),
        ],
        compiler_params=pltpu.CompilerParams(vmem_limit_bytes=8 << 20),
        name="stage",
    )(length, shift, fq, go, masks)


def column_of(row):
    n = row.shape[1]
    eye = lax.broadcasted_iota(jnp.int32, (n, n), 0) == lax.broadcasted_iota(jnp.int32, (n, n), 1)
    return jnp.sum(jnp.where(eye, jnp.broadcast_to(row, (n, n)), 0.0), axis=1, keepdims=True)


def fold(combine, start, x):
    for r in range(0, x.shape[0], 8):
        start = combine(start, x[r : r + 8])
    return start


def attention_kernel(*refs, tokens, heads, score_scale):
    tiles = REACH + 1
    (fq_ref, go_ref, up_ref, low_ref, mask_ref, own_k_ref, own_v_ref) = refs[:7]
    direct, swapped = refs[7:12], refs[12:17]
    parts = refs[17:21]
    out_ref, gq_ref, low_rank_ref, grad_up_ref, q_ref, w_ref, gs_ref = refs[21:28]
    (k_s, v_s, kt_s, vt_s, place_s, s_s, gw_s, a_s, acc_s, lr_s) = refs[28:]
    core = core_of()
    column = column_place()
    exponent = score_scale * math.log2(math.e)

    def rows(d):
        return pl.ds(d * tokens, tokens)

    k_s[rows(0), :] = own_k_ref[...]
    v_s[rows(0), :] = own_v_ref[...]

    def fill(store, pieces):
        store[rows(1), :] = pieces[0][...]
        store[rows(2), :] = pieces[1][...]
        for n in range(1, COLUMNS):
            store[rows(2 * n + 1), :] = pieces[n + 1][0]
            store[rows(2 * n + 2), :] = pieces[n + 1][1]

    @pl.when(core == 0)
    def _():
        fill(k_s, direct)
        fill(v_s, swapped)

    @pl.when(core != 0)
    def _():
        fill(k_s, swapped)
        fill(v_s, direct)

    low = low_ref[...]
    place_s[...] = lax.broadcasted_iota(jnp.int32, (tokens, tokens), 0)
    lr_s[...] = jnp.zeros_like(lr_s)
    masks = mask_ref[...].astype(jnp.float32)
    keep0, keep1 = column_of(masks[0:1]), column_of(masks[1:2])
    total = (parts[0][...].astype(jnp.float32) + parts[1][...].astype(jnp.float32)) + (
        parts[2][...].astype(jnp.float32) + parts[3][...].astype(jnp.float32)
    )
    mpt = (total * keep0).astype(jnp.bfloat16)
    mp = mpt.astype(jnp.float32).T.astype(jnp.bfloat16)

    def lanes(head):
        return pl.ds(pl.multiple_of(head * HEAD_SIZE, HEAD_SIZE), HEAD_SIZE)

    def up_of(head):
        return (up_ref[:, lanes(head)].astype(jnp.float32) * keep1).astype(jnp.bfloat16)

    def make_query(head):
        q_ref[head] = (
            fq_ref[head].astype(jnp.float32) + adapter_scale * dot32(mp, up_of(head), NN)
        ).astype(jnp.bfloat16)

    def scores(head, slot, d, top):
        s = dot32(k_s[rows(d), :], q_ref[head], NT)
        allowed = place_s[...] >= low + distance(d, column) * tokens
        if d == 0:
            allowed = allowed & (place_s[...] <= lax.broadcasted_iota(jnp.int32, s.shape, 1))
        s = jnp.where(allowed, s, -1e30)
        s_s[slot, rows(d), :] = s
        return fold(jnp.maximum, top, s)

    lowest = jnp.full((8, tokens), -1e30, jnp.float32)
    zero = jnp.zeros((8, tokens), jnp.float32)
    make_query(0)
    top = lowest
    for d in range(tiles):
        top = scores(0, 0, d, top)
        kt_s[:, rows(d)] = k_s[rows(d), :].T
        vt_s[:, rows(d)] = v_s[rows(d), :].T

    def one_head(head, top, last):
        slot = lax.rem(head, 2)
        top = jnp.max(top, axis=0, keepdims=True)
        if not last:
            make_query(head + 1)

        total, next_top = zero, lowest
        for d in range(tiles):
            p = jnp.exp2((s_s[slot, rows(d), :] - top) * exponent)
            a_s[slot, rows(d), :] = p
            total = fold(jnp.add, total, p)
            gw_s[slot, rows(d), :] = dot32(v_s[rows(d), :], go_ref[head], NT)
        inverse = 1.0 / jnp.sum(total, axis=0, keepdims=True)
        acc_s[...] = jnp.zeros_like(acc_s)

        dots = zero
        for d in range(tiles):
            w = a_s[slot, rows(d), :] * inverse
            w_half = w.astype(jnp.bfloat16)
            w_ref[head, rows(d), :] = w_half
            a = w * gw_s[slot, rows(d), :]
            gw_s[slot, rows(d), :] = a
            acc_s[...] += dot32(vt_s[:, rows(d)], w_half, NN)
            dots = fold(jnp.add, dots, a)
            if not last:
                next_top = scores(head + 1, 1 - slot, d, next_top)
        out_ref[:, lanes(head)] = acc_s[...].T.astype(jnp.bfloat16)
        dots = jnp.sum(dots, axis=0, keepdims=True) * inverse
        acc_s[...] = jnp.zeros_like(acc_s)

        for d in range(tiles):
            gs = (gw_s[slot, rows(d), :] - a_s[slot, rows(d), :] * dots).astype(jnp.bfloat16)
            gs_ref[head, rows(d), :] = gs
            acc_s[...] += dot32(kt_s[:, rows(d)], gs, NN)
        gq_t = (score_scale * acc_s[...]).astype(jnp.bfloat16)
        gq = (gq_t.astype(jnp.float32).T).astype(jnp.bfloat16)
        gq_ref[:, lanes(head)] = gq
        lr_s[...] += dot32(up_of(head), gq_t, NN)
        grad_up_ref[:, lanes(head)] = (adapter_scale * dot32(mpt, gq, NN)).astype(jnp.bfloat16)
        return next_top

    top = lax.fori_loop(0, heads - 1, lambda h, t: one_head(h, t, False), top)
    one_head(heads - 1, top, True)
    low_rank_ref[...] = lr_s[...].astype(jnp.bfloat16)


def attention(fq, go, up, low, rest):
    heads, tokens, _ = fq.shape
    ranks, width = up.shape
    span = (REACH + 1) * tokens
    vmem = pl.BlockSpec(memory_space=pltpu.VMEM)
    return pl.pallas_call(
        functools.partial(
            attention_kernel,
            tokens=tokens,
            heads=heads,
            score_scale=1.0 / math.sqrt(HEAD_SIZE),
        ),
        in_specs=[vmem] * (4 + len(rest)),
        out_specs=[vmem] * 7,
        scratch_shapes=[
            pltpu.VMEM((span, HEAD_SIZE), jnp.bfloat16),
            pltpu.VMEM((span, HEAD_SIZE), jnp.bfloat16),
            pltpu.VMEM((HEAD_SIZE, span), jnp.bfloat16),
            pltpu.VMEM((HEAD_SIZE, span), jnp.bfloat16),
            pltpu.VMEM((tokens, tokens), jnp.int32),
            pltpu.VMEM((2, span, tokens), jnp.float32),
            pltpu.VMEM((2, span, tokens), jnp.float32),
            pltpu.VMEM((2, span, tokens), jnp.float32),
            pltpu.VMEM((HEAD_SIZE, tokens), jnp.float32),
            pltpu.VMEM((ranks, tokens), jnp.float32),
        ],
        out_shape=[
            jax.ShapeDtypeStruct((tokens, width), jnp.bfloat16),
            jax.ShapeDtypeStruct((tokens, width), jnp.bfloat16),
            jax.ShapeDtypeStruct((ranks, tokens), jnp.bfloat16),
            jax.ShapeDtypeStruct((ranks, width), jnp.bfloat16),
            jax.ShapeDtypeStruct((heads, tokens, HEAD_SIZE), jnp.bfloat16),
            jax.ShapeDtypeStruct((heads, span, tokens), jnp.bfloat16),
            jax.ShapeDtypeStruct((heads, span, tokens), jnp.bfloat16),
        ],
        compiler_params=pltpu.CompilerParams(vmem_limit_bytes=24 << 20),
        cost_estimate=pl.CostEstimate(
            flops=8 * heads * tokens * span * HEAD_SIZE,
            bytes_accessed=8 << 20,
            transcendentals=heads * tokens * span,
        ),
        name="attention",
    )(fq, go, up, low, *rest)


def kv_half_kernel(w_ref, gs_ref, go_ref, q_ref, half_ref, *, keep, score_scale):
    heads, span, tokens = w_ref.shape
    values = (core_of() == 0) != keep

    def product(left_ref, right_ref, scale):
        right = jnp.concatenate([right_ref[h] for h in range(heads)], 0)
        for d in range(span // tokens):
            rows = pl.ds(d * tokens, tokens)
            left = jnp.concatenate([left_ref[h, rows, :] for h in range(heads)], 1)
            half_ref[rows, :] = (scale * dot32(left, right, NN)).astype(half_ref.dtype)

    @pl.when(values)
    def _():
        product(w_ref, go_ref, 1.0)

    @pl.when(jnp.logical_not(values))
    def _():
        product(gs_ref, q_ref, score_scale)


def kv_half(weights, grad_scores, go, queries, keep):
    span = weights.shape[1]
    vmem = pl.BlockSpec(memory_space=pltpu.VMEM)
    return pl.pallas_call(
        functools.partial(kv_half_kernel, keep=keep, score_scale=1.0 / math.sqrt(HEAD_SIZE)),
        in_specs=[vmem] * 4,
        out_specs=vmem,
        out_shape=jax.ShapeDtypeStruct((span, HEAD_SIZE), jnp.float32 if keep else jnp.bfloat16),
        compiler_params=pltpu.CompilerParams(vmem_limit_bytes=6 << 20),
        cost_estimate=pl.CostEstimate(
            flops=2 * span * queries.size, bytes_accessed=2 << 20, transcendentals=0
        ),
        name="kv_keep" if keep else "kv_send",
    )(weights, grad_scores, go, queries)


def pair_sum_kernel(keep_ref, got_ref, own_ref, one_ref, two_ref, *packs):
    tokens = own_ref.shape[0]

    def total(d):
        rows = pl.ds(d * tokens, tokens)
        return keep_ref[rows, :] + got_ref[rows, :].astype(jnp.float32)

    own_ref[...] = total(0)
    one_ref[...] = total(1)
    two_ref[...] = total(2)
    for n, pack_ref in enumerate(packs):
        pack_ref[0] = total(2 * n + 3).astype(jnp.bfloat16)
        pack_ref[1] = total(2 * n + 4).astype(jnp.bfloat16)


def pair_sum(keep, got, tokens):
    tile = (tokens, HEAD_SIZE)
    return pl.pallas_call(
        pair_sum_kernel,
        out_shape=[jax.ShapeDtypeStruct(tile, jnp.float32)] * 3
        + [jax.ShapeDtypeStruct((2,) + tile, jnp.bfloat16)] * (COLUMNS - 1),
        compiler_params=pltpu.CompilerParams(vmem_limit_bytes=12 << 20),
        name="pair_sum",
    )(keep, got)


def row_sum_kernel(own_ref, one_ref, two_ref, *rest):
    column = column_place()
    packs, (own_out, one_out, two_out) = rest[: COLUMNS - 1], rest[COLUMNS - 1 :]
    own, one, two = own_ref[...], one_ref[...], two_ref[...]
    for n, pack_ref in enumerate(packs):
        one = one + pack_ref[0].astype(jnp.float32)
        piece = pack_ref[1].astype(jnp.float32)
        near = jnp.full(piece.shape, n + 1, jnp.int32) + column < COLUMNS
        own = own + jnp.where(near, piece, 0.0)
        two = two + jnp.where(near, 0.0, piece)
    own_out[...] = own.astype(jnp.bfloat16)
    one_out[...] = one.astype(jnp.bfloat16)
    two_out[...] = two.astype(jnp.bfloat16)


def row_sum(own, one, two, packs):
    vmem = pl.BlockSpec(memory_space=pltpu.VMEM)
    return pl.pallas_call(
        row_sum_kernel,
        in_specs=[vmem] * (2 + COLUMNS),
        out_shape=[jax.ShapeDtypeStruct(own.shape, jnp.bfloat16)] * 3,
        compiler_params=pltpu.CompilerParams(vmem_limit_bytes=8 << 20),
        name="row_sum",
    )(own, one, two, *packs)


def spread_kernel(down_ref, up_ref, out_ref):
    row = jnp.concatenate([down_ref[...], up_ref[...]], 0).astype(jnp.bfloat16)
    for n in range(out_ref.shape[0]):
        out_ref[n] = row


def spread(down, up, copies):
    return pl.pallas_call(
        spread_kernel,
        out_shape=jax.ShapeDtypeStruct((copies, down.shape[0] + up.shape[0], 128), jnp.bfloat16),
        compiler_params=pltpu.CompilerParams(vmem_limit_bytes=4 << 20),
        name="spread",
    )(down, up)


def adam_kernel(got_ref, pd, md, vd, pu, mu, vu, keep_ref, opd, omd, ovd, opu, omu, ovu):
    down_rows = pd.shape[0]
    total = jnp.sum(got_ref[...].astype(jnp.float32), axis=0)
    grads = (total[:down_rows], total[down_rows:] * keep_ref[0, 0])
    for grad, p, m, v, op, om, ov in (
        (grads[0], pd, md, vd, opd, omd, ovd),
        (grads[1], pu, mu, vu, opu, omu, ovu),
    ):
        first = beta_one * m[...] + (1.0 - beta_one) * grad
        second = beta_two * v[...] + (1.0 - beta_two) * grad * grad
        op[...] = p[...] - learn_rate * first / (jnp.sqrt(second) + adam_epsilon)
        om[...] = first
        ov[...] = second


def on_device(
    frozen_queries,
    key_value_rows,
    output_gradient,
    inputs,
    adapter_down,
    down_first_moment,
    down_second_moment,
    adapter_up,
    up_first_moment,
    up_second_moment,
    rank_keep_mask,
    group_length,
    group_shift,
):
    tokens = frozen_queries.shape[0]
    width = frozen_queries.shape[1]
    model = inputs.shape[1]
    ctx = lax.axis_size("ctx")
    head_count = lax.axis_size("head")
    ctx_place = lax.axis_index("ctx")
    head_place = lax.axis_index("head")
    core = head_place % CORES
    kv_head = head_place // CORES
    key_width = KVH * HEAD_SIZE
    ranks = rank_keep_mask.shape[1]

    own_k = lax.dynamic_slice_in_dim(key_value_rows, kv_head * HEAD_SIZE, HEAD_SIZE, 1)
    own_v = lax.dynamic_slice_in_dim(key_value_rows, key_width + kv_head * HEAD_SIZE, HEAD_SIZE, 1)
    mine = lax.dynamic_slice_in_dim(
        key_value_rows, core * key_width + kv_head * HEAD_SIZE, HEAD_SIZE, 1
    )
    swap = [(h, h ^ 1) for h in range(head_count)]

    def along(piece, step):
        return lax.ppermute(piece, "ctx", [(i, (i + step) % ctx) for i in range(ctx)])

    def across(piece, step):
        pairs = [(i, i // COLUMNS * COLUMNS + (i + step) % COLUMNS) for i in range(ctx)]
        return lax.ppermute(piece, "ctx", pairs)

    one, two = along(mine, COLUMNS), along(mine, 2 * COLUMNS)

    down_rows, up_rows = model // 128, width // 128
    row = spread(adapter_down.reshape(down_rows, 128), adapter_up.reshape(up_rows, 128), ctx)
    gathered = lax.all_to_all(row, "ctx", split_axis=0, concat_axis=0)
    packs = pack(mine, one, two)
    direct = [one, two] + [across(p, n + 1) for n, p in enumerate(packs)]
    queries_in, grads_in, masks_in, low = stage(
        group_length,
        group_shift,
        frozen_queries,
        output_gradient,
        rank_keep_mask,
        tokens * ctx,
    )
    swapped = [lax.ppermute(piece, "head", swap) for piece in direct]

    down = gathered[:, :down_rows].reshape(ranks, model)
    up = gathered[:, down_rows:].reshape(ranks, width)

    part = dot32(down, inputs, NT).astype(jnp.bfloat16)
    others = [[(h, h ^ k) for h in range(head_count)] for k in range(1, head_count)]
    parts = [part] + [lax.ppermute(part, "head", pairs) for pairs in others]

    keep_masks = rank_keep_mask.astype(jnp.float32)[:, :, None]
    out, query_gradient, low_rank_part, grad_up_part, queries, weights, grad_scores = attention(
        queries_in,
        grads_in,
        up,
        low,
        [
            masks_in,
            own_k,
            own_v,
            *direct,
            *swapped,
            *parts,
        ],
    )

    low_parts = [low_rank_part] + [lax.ppermute(low_rank_part, "head", pairs) for pairs in others]
    send = kv_half(weights, grad_scores, grads_in, queries, keep=False)
    got = lax.ppermute(send, "head", swap)
    keep = kv_half(weights, grad_scores, grads_in, queries, keep=True)
    own_sum, one_sum, two_sum, *packs = pair_sum(keep, got, tokens)
    low_parts, grad_up_part, packs = lax.optimization_barrier((low_parts, grad_up_part, packs))
    low_total = sum(p.astype(jnp.float32) for p in low_parts)
    low_rank = (low_total * keep_masks[0] * adapter_scale).astype(jnp.bfloat16)
    grad_down_part = dot32(low_rank, inputs, NN).astype(jnp.bfloat16)
    packed = jnp.concatenate(
        [
            grad_down_part.reshape(ranks, down_rows, 128),
            grad_up_part.reshape(ranks, up_rows, 128),
        ],
        1,
    )
    received = lax.all_to_all(packed, "ctx", split_axis=0, concat_axis=0)

    packs = [across(p, -(n + 1)) for n, p in enumerate(packs)]
    own_sum, one_sum, two_sum = row_sum(own_sum, one_sum, two_sum, packs)

    def home(piece, back):
        pairs = [
            (
                i * head_count + h,
                (i - back) % ctx * head_count + (h % CORES) * CORES + h // CORES,
            )
            for i in range(ctx)
            for h in range(head_count)
        ]
        return lax.ppermute(piece, ("ctx", "head"), pairs).astype(jnp.float32)

    kv_grad = home(own_sum, 0) + home(one_sum, COLUMNS) + home(two_sum, 2 * COLUMNS)

    keep_row = lax.dynamic_slice_in_dim(keep_masks[1], ctx_place, 1, 0)
    small = [
        a.reshape(-1, 128)
        for a in (
            adapter_down,
            down_first_moment,
            down_second_moment,
            adapter_up,
            up_first_moment,
            up_second_moment,
        )
    ]
    news = pl.pallas_call(
        adam_kernel,
        out_shape=[jax.ShapeDtypeStruct(a.shape, jnp.float32) for a in small],
        compiler_params=pltpu.CompilerParams(vmem_limit_bytes=8 << 20),
        name="adam",
    )(received, *small, keep_row)
    news = [n.reshape(1, -1) for n in news]
    return (out, query_gradient, kv_grad, *news)


def solution(mesh):
    both = P("ctx", "head")
    return jax.shard_map(
        on_device,
        mesh=mesh,
        in_specs=(both, P("ctx", None)) + (both,) * 8 + (P(), P(), P()),
        out_specs=(both,) * 9,
        check_vma=False,
    )
```

```python
import functools
import math

import jax
import jax.numpy as jnp
from jax import lax
from jax.experimental import pallas as pl
from jax.experimental.pallas import tpu as pltpu
from jax.sharding import PartitionSpec as P


HEAD_SIZE = 128
KVH = 2
REACH = 8
CORES = 2
COLUMNS = 4

adapter_scale = 0.25
beta_one = 0.9
beta_two = 0.999
learn_rate = 0.01
adam_epsilon = 1e-08


NN = (((1,), (0,)), ((), ()))
NT = (((1,), (1,)), ((), ()))


def dot32(a, b, dims):
    return lax.dot_general(a, b, dims, preferred_element_type=jnp.float32)


def core_of():
    return lax.rem(lax.axis_index("head"), CORES)


def column_place():
    return lax.rem(lax.axis_index("ctx"), COLUMNS)


def distance(slot, column):
    if slot < 3:
        return (0, COLUMNS, 2 * COLUMNS)[slot]
    step, late = divmod(slot - 1, 2)
    near = column >= step
    return jnp.where(near, step + (0 if late else COLUMNS), step + (COLUMNS if late else 0))


def pack_kernel(own_ref, one_ref, two_ref, *outs):
    column = column_place()
    for n, out in enumerate(outs):
        step = n + 1
        out[0] = one_ref[...]

        @pl.when(column + step < COLUMNS)
        def _():
            out[1] = own_ref[...]

        @pl.when(column + step >= COLUMNS)
        def _():
            out[1] = two_ref[...]


def pack(own, one, two):
    vmem = pl.BlockSpec(memory_space=pltpu.VMEM)
    return pl.pallas_call(
        pack_kernel,
        in_specs=[vmem] * 3,
        out_shape=[jax.ShapeDtypeStruct((2,) + own.shape, own.dtype)] * (COLUMNS - 1),
        compiler_params=pltpu.CompilerParams(vmem_limit_bytes=8 << 20),
        name="pack",
    )(own, one, two)


def stage_kernel(fq_ref, go_ref, fq_out, go_out):
    for h in range(fq_out.shape[0]):
        lanes = pl.ds(h * HEAD_SIZE, HEAD_SIZE)
        fq_out[h] = fq_ref[:, lanes]
        go_out[h] = go_ref[:, lanes]


def stage(fq, go):
    tokens, width = fq.shape
    by_head = jax.ShapeDtypeStruct((width // HEAD_SIZE, tokens, HEAD_SIZE), jnp.bfloat16)
    return pl.pallas_call(
        stage_kernel,
        out_shape=[by_head, by_head],
        compiler_params=pltpu.CompilerParams(vmem_limit_bytes=8 << 20),
        name="stage",
    )(fq, go)


def bounds_kernel(length_ref, shift_ref, mask_ref, mask_out, low_out, *, seq_total):
    tokens = low_out.shape[1]
    kv_head = lax.axis_index("head") // CORES
    length = length_ref[kv_head]
    first = lax.rem(lax.axis_index("ctx") * tokens - shift_ref[kv_head] + seq_total, seq_total)
    within = lax.broadcasted_iota(jnp.int32, (1, tokens), 1)
    in_group = within + lax.rem(first, length)
    in_group = jnp.where(in_group >= length, in_group - length, in_group)
    rolled = within + first
    low_out[...] = within - jnp.where(rolled >= seq_total, rolled - seq_total, in_group)
    mask_out[...] = mask_ref[...]


def bounds(length, shift, masks, tokens, seq_total):
    smem = pl.BlockSpec(memory_space=pltpu.SMEM)
    return pl.pallas_call(
        functools.partial(bounds_kernel, seq_total=seq_total),
        in_specs=[smem, smem, pl.BlockSpec(memory_space=pltpu.VMEM)],
        out_shape=[
            jax.ShapeDtypeStruct(masks.shape, masks.dtype),
            jax.ShapeDtypeStruct((1, tokens), jnp.int32),
        ],
        compiler_params=pltpu.CompilerParams(vmem_limit_bytes=8 << 20),
        name="bounds",
    )(length, shift, masks)


def column_of(row):
    n = row.shape[1]
    eye = lax.broadcasted_iota(jnp.int32, (n, n), 0) == lax.broadcasted_iota(jnp.int32, (n, n), 1)
    return jnp.sum(jnp.where(eye, jnp.broadcast_to(row, (n, n)), 0.0), axis=1, keepdims=True)


def fold(combine, start, x):
    for r in range(0, x.shape[0], 8):
        start = combine(start, x[r : r + 8])
    return start


def attention_kernel(*refs, tokens, heads, score_scale):
    tiles = REACH + 1
    (fq_ref, go_ref, up_ref, low_ref, mask_ref, own_k_ref, own_v_ref) = refs[:7]
    direct, swapped = refs[7:12], refs[12:17]
    parts = refs[17:21]
    out_ref, gq_ref, low_rank_ref, grad_up_ref, q_ref, w_ref, gs_ref = refs[21:28]
    (k_s, v_s, kt_s, vt_s, place_s, s_s, gw_s, a_s, acc_s, lr_s) = refs[28:]
    core = core_of()
    column = column_place()
    exponent = score_scale * math.log2(math.e)

    def rows(d):
        return pl.ds(d * tokens, tokens)

    k_s[rows(0), :] = own_k_ref[...]
    v_s[rows(0), :] = own_v_ref[...]

    def fill(store, pieces):
        store[rows(1), :] = pieces[0][...]
        store[rows(2), :] = pieces[1][...]
        for n in range(1, COLUMNS):
            store[rows(2 * n + 1), :] = pieces[n + 1][0]
            store[rows(2 * n + 2), :] = pieces[n + 1][1]

    @pl.when(core == 0)
    def _():
        fill(k_s, direct)
        fill(v_s, swapped)

    @pl.when(core != 0)
    def _():
        fill(k_s, swapped)
        fill(v_s, direct)

    low = low_ref[...]
    place_s[...] = lax.broadcasted_iota(jnp.int32, (tokens, tokens), 0)
    lr_s[...] = jnp.zeros_like(lr_s)
    masks = mask_ref[...].astype(jnp.float32)
    keep0, keep1 = column_of(masks[0:1]), column_of(masks[1:2])
    total = (parts[0][...].astype(jnp.float32) + parts[1][...].astype(jnp.float32)) + (
        parts[2][...].astype(jnp.float32) + parts[3][...].astype(jnp.float32)
    )
    mpt = (total * keep0).astype(jnp.bfloat16)
    mp = mpt.astype(jnp.float32).T.astype(jnp.bfloat16)

    def lanes(head):
        return pl.ds(pl.multiple_of(head * HEAD_SIZE, HEAD_SIZE), HEAD_SIZE)

    def up_of(head):
        return (up_ref[:, lanes(head)].astype(jnp.float32) * keep1).astype(jnp.bfloat16)

    def make_query(head):
        q_ref[head] = (
            fq_ref[head].astype(jnp.float32) + adapter_scale * dot32(mp, up_of(head), NN)
        ).astype(jnp.bfloat16)

    def scores(head, slot, d, top):
        s = dot32(k_s[rows(d), :], q_ref[head], NT)
        allowed = place_s[...] >= low + distance(d, column) * tokens
        if d == 0:
            allowed = allowed & (place_s[...] <= lax.broadcasted_iota(jnp.int32, s.shape, 1))
        s = jnp.where(allowed, s, -1e30)
        s_s[slot, rows(d), :] = s
        return fold(jnp.maximum, top, s)

    lowest = jnp.full((8, tokens), -1e30, jnp.float32)
    zero = jnp.zeros((8, tokens), jnp.float32)
    make_query(0)
    top = lowest
    for d in range(tiles):
        top = scores(0, 0, d, top)
        kt_s[:, rows(d)] = k_s[rows(d), :].T
        vt_s[:, rows(d)] = v_s[rows(d), :].T

    def one_head(head, top, last):
        slot = lax.rem(head, 2)
        top = jnp.max(top, axis=0, keepdims=True)
        if not last:
            make_query(head + 1)

        total, next_top = zero, lowest
        for d in range(tiles):
            p = jnp.exp2((s_s[slot, rows(d), :] - top) * exponent)
            a_s[slot, rows(d), :] = p
            total = fold(jnp.add, total, p)
            gw_s[slot, rows(d), :] = dot32(v_s[rows(d), :], go_ref[head], NT)
        inverse = 1.0 / jnp.sum(total, axis=0, keepdims=True)
        acc_s[...] = jnp.zeros_like(acc_s)

        dots = zero
        for d in range(tiles):
            w = a_s[slot, rows(d), :] * inverse
            w_half = w.astype(jnp.bfloat16)
            w_ref[head, rows(d), :] = w_half
            a = w * gw_s[slot, rows(d), :]
            gw_s[slot, rows(d), :] = a
            acc_s[...] += dot32(vt_s[:, rows(d)], w_half, NN)
            dots = fold(jnp.add, dots, a)
            if not last:
                next_top = scores(head + 1, 1 - slot, d, next_top)
        out_ref[:, lanes(head)] = acc_s[...].T.astype(jnp.bfloat16)
        dots = jnp.sum(dots, axis=0, keepdims=True) * inverse
        acc_s[...] = jnp.zeros_like(acc_s)

        for d in range(tiles):
            gs = (gw_s[slot, rows(d), :] - a_s[slot, rows(d), :] * dots).astype(jnp.bfloat16)
            gs_ref[head, rows(d), :] = gs
            acc_s[...] += dot32(kt_s[:, rows(d)], gs, NN)
        gq_t = (score_scale * acc_s[...]).astype(jnp.bfloat16)
        gq = (gq_t.astype(jnp.float32).T).astype(jnp.bfloat16)
        gq_ref[:, lanes(head)] = gq
        lr_s[...] += dot32(up_of(head), gq_t, NN)
        grad_up_ref[:, lanes(head)] = (adapter_scale * dot32(mpt, gq, NN)).astype(jnp.bfloat16)
        return next_top

    top = lax.fori_loop(0, heads - 1, lambda h, t: one_head(h, t, False), top)
    one_head(heads - 1, top, True)
    low_rank_ref[...] = lr_s[...].astype(jnp.bfloat16)


def attention(fq, go, up, low, rest):
    heads, tokens, _ = fq.shape
    ranks, width = up.shape
    span = (REACH + 1) * tokens
    vmem = pl.BlockSpec(memory_space=pltpu.VMEM)
    return pl.pallas_call(
        functools.partial(
            attention_kernel,
            tokens=tokens,
            heads=heads,
            score_scale=1.0 / math.sqrt(HEAD_SIZE),
        ),
        in_specs=[vmem] * (4 + len(rest)),
        out_specs=[vmem] * 7,
        scratch_shapes=[
            pltpu.VMEM((span, HEAD_SIZE), jnp.bfloat16),
            pltpu.VMEM((span, HEAD_SIZE), jnp.bfloat16),
            pltpu.VMEM((HEAD_SIZE, span), jnp.bfloat16),
            pltpu.VMEM((HEAD_SIZE, span), jnp.bfloat16),
            pltpu.VMEM((tokens, tokens), jnp.int32),
            pltpu.VMEM((2, span, tokens), jnp.float32),
            pltpu.VMEM((2, span, tokens), jnp.float32),
            pltpu.VMEM((2, span, tokens), jnp.float32),
            pltpu.VMEM((HEAD_SIZE, tokens), jnp.float32),
            pltpu.VMEM((ranks, tokens), jnp.float32),
        ],
        out_shape=[
            jax.ShapeDtypeStruct((tokens, width), jnp.bfloat16),
            jax.ShapeDtypeStruct((tokens, width), jnp.bfloat16),
            jax.ShapeDtypeStruct((ranks, tokens), jnp.bfloat16),
            jax.ShapeDtypeStruct((ranks, width), jnp.bfloat16),
            jax.ShapeDtypeStruct((heads, tokens, HEAD_SIZE), jnp.bfloat16),
            jax.ShapeDtypeStruct((heads, span, tokens), jnp.bfloat16),
            jax.ShapeDtypeStruct((heads, span, tokens), jnp.bfloat16),
        ],
        compiler_params=pltpu.CompilerParams(vmem_limit_bytes=24 << 20),
        cost_estimate=pl.CostEstimate(
            flops=8 * heads * tokens * span * HEAD_SIZE,
            bytes_accessed=8 << 20,
            transcendentals=heads * tokens * span,
        ),
        name="attention",
    )(fq, go, up, low, *rest)


def kv_half_kernel(w_ref, gs_ref, go_ref, q_ref, half_ref, *, keep, score_scale):
    heads, span, tokens = w_ref.shape
    values = (core_of() == 0) != keep

    def product(left_ref, right_ref, scale):
        right = jnp.concatenate([right_ref[h] for h in range(heads)], 0)
        for d in range(span // tokens):
            rows = pl.ds(d * tokens, tokens)
            left = jnp.concatenate([left_ref[h, rows, :] for h in range(heads)], 1)
            half_ref[rows, :] = (scale * dot32(left, right, NN)).astype(half_ref.dtype)

    @pl.when(values)
    def _():
        product(w_ref, go_ref, 1.0)

    @pl.when(jnp.logical_not(values))
    def _():
        product(gs_ref, q_ref, score_scale)


def kv_half(weights, grad_scores, go, queries, keep):
    span = weights.shape[1]
    vmem = pl.BlockSpec(memory_space=pltpu.VMEM)
    return pl.pallas_call(
        functools.partial(kv_half_kernel, keep=keep, score_scale=1.0 / math.sqrt(HEAD_SIZE)),
        in_specs=[vmem] * 4,
        out_specs=vmem,
        out_shape=jax.ShapeDtypeStruct((span, HEAD_SIZE), jnp.float32 if keep else jnp.bfloat16),
        compiler_params=pltpu.CompilerParams(vmem_limit_bytes=6 << 20),
        cost_estimate=pl.CostEstimate(
            flops=2 * span * queries.size, bytes_accessed=2 << 20, transcendentals=0
        ),
        name="kv_keep" if keep else "kv_send",
    )(weights, grad_scores, go, queries)


def pair_sum_kernel(keep_ref, got_ref, own_ref, one_ref, two_ref, *packs):
    tokens = own_ref.shape[0]

    def total(d):
        rows = pl.ds(d * tokens, tokens)
        return keep_ref[rows, :] + got_ref[rows, :].astype(jnp.float32)

    own_ref[...] = total(0)
    one_ref[...] = total(1)
    two_ref[...] = total(2)
    for n, pack_ref in enumerate(packs):
        pack_ref[0] = total(2 * n + 3).astype(jnp.bfloat16)
        pack_ref[1] = total(2 * n + 4).astype(jnp.bfloat16)


def pair_sum(keep, got, tokens):
    tile = (tokens, HEAD_SIZE)
    return pl.pallas_call(
        pair_sum_kernel,
        out_shape=[jax.ShapeDtypeStruct(tile, jnp.float32)] * 3
        + [jax.ShapeDtypeStruct((2,) + tile, jnp.bfloat16)] * (COLUMNS - 1),
        compiler_params=pltpu.CompilerParams(vmem_limit_bytes=12 << 20),
        name="pair_sum",
    )(keep, got)


def row_sum_kernel(own_ref, one_ref, two_ref, *rest):
    column = column_place()
    packs, (own_out, one_out, two_out) = rest[: COLUMNS - 1], rest[COLUMNS - 1 :]
    own, one, two = own_ref[...], one_ref[...], two_ref[...]
    for n, pack_ref in enumerate(packs):
        one = one + pack_ref[0].astype(jnp.float32)
        piece = pack_ref[1].astype(jnp.float32)
        near = jnp.full(piece.shape, n + 1, jnp.int32) + column < COLUMNS
        own = own + jnp.where(near, piece, 0.0)
        two = two + jnp.where(near, 0.0, piece)
    own_out[...] = own.astype(jnp.bfloat16)
    one_out[...] = one.astype(jnp.bfloat16)
    two_out[...] = two.astype(jnp.bfloat16)


def row_sum(own, one, two, packs):
    vmem = pl.BlockSpec(memory_space=pltpu.VMEM)
    return pl.pallas_call(
        row_sum_kernel,
        in_specs=[vmem] * (2 + COLUMNS),
        out_shape=[jax.ShapeDtypeStruct(own.shape, jnp.bfloat16)] * 3,
        compiler_params=pltpu.CompilerParams(vmem_limit_bytes=8 << 20),
        name="row_sum",
    )(own, one, two, *packs)


def spread_kernel(down_ref, up_ref, out_ref):
    row = jnp.concatenate([down_ref[...], up_ref[...]], 0).astype(jnp.bfloat16)
    for n in range(out_ref.shape[0]):
        out_ref[n] = row


def spread(down, up, copies):
    return pl.pallas_call(
        spread_kernel,
        out_shape=jax.ShapeDtypeStruct((copies, down.shape[0] + up.shape[0], 128), jnp.bfloat16),
        compiler_params=pltpu.CompilerParams(vmem_limit_bytes=4 << 20),
        name="spread",
    )(down, up)


def adam_kernel(got_ref, pd, md, vd, pu, mu, vu, keep_ref, opd, omd, ovd, opu, omu, ovu):
    down_rows = pd.shape[0]
    total = jnp.sum(got_ref[...].astype(jnp.float32), axis=0)
    grads = (total[:down_rows], total[down_rows:] * keep_ref[0, 0])
    for grad, p, m, v, op, om, ov in (
        (grads[0], pd, md, vd, opd, omd, ovd),
        (grads[1], pu, mu, vu, opu, omu, ovu),
    ):
        first = beta_one * m[...] + (1.0 - beta_one) * grad
        second = beta_two * v[...] + (1.0 - beta_two) * grad * grad
        op[...] = p[...] - learn_rate * first / (jnp.sqrt(second) + adam_epsilon)
        om[...] = first
        ov[...] = second


def on_device(
    frozen_queries,
    key_value_rows,
    output_gradient,
    inputs,
    adapter_down,
    down_first_moment,
    down_second_moment,
    adapter_up,
    up_first_moment,
    up_second_moment,
    rank_keep_mask,
    group_length,
    group_shift,
):
    tokens = frozen_queries.shape[0]
    width = frozen_queries.shape[1]
    model = inputs.shape[1]
    ctx = lax.axis_size("ctx")
    head_count = lax.axis_size("head")
    ctx_place = lax.axis_index("ctx")
    head_place = lax.axis_index("head")
    core = head_place % CORES
    kv_head = head_place // CORES
    key_width = KVH * HEAD_SIZE
    ranks = rank_keep_mask.shape[1]

    own_k = lax.dynamic_slice_in_dim(key_value_rows, kv_head * HEAD_SIZE, HEAD_SIZE, 1)
    own_v = lax.dynamic_slice_in_dim(key_value_rows, key_width + kv_head * HEAD_SIZE, HEAD_SIZE, 1)
    mine = lax.dynamic_slice_in_dim(
        key_value_rows, core * key_width + kv_head * HEAD_SIZE, HEAD_SIZE, 1
    )
    swap = [(h, h ^ 1) for h in range(head_count)]

    def along(piece, step):
        return lax.ppermute(piece, "ctx", [(i, (i + step) % ctx) for i in range(ctx)])

    def across(piece, step):
        pairs = [(i, i // COLUMNS * COLUMNS + (i + step) % COLUMNS) for i in range(ctx)]
        return lax.ppermute(piece, "ctx", pairs)

    one, two = along(mine, COLUMNS), along(mine, 2 * COLUMNS)

    down_rows, up_rows = model // 128, width // 128
    row = spread(adapter_down.reshape(down_rows, 128), adapter_up.reshape(up_rows, 128), ctx)
    gathered = lax.all_to_all(row, "ctx", split_axis=0, concat_axis=0)
    packs = pack(mine, one, two)
    direct = [one, two] + [across(p, n + 1) for n, p in enumerate(packs)]
    queries_in, grads_in = stage(frozen_queries, output_gradient)
    masks_in, low = bounds(group_length, group_shift, rank_keep_mask, tokens, tokens * ctx)
    swapped = [lax.ppermute(piece, "head", swap) for piece in direct]

    down = gathered[:, :down_rows].reshape(ranks, model)
    up = gathered[:, down_rows:].reshape(ranks, width)

    part = dot32(down, inputs, NT).astype(jnp.bfloat16)
    others = [[(h, h ^ k) for h in range(head_count)] for k in range(1, head_count)]
    parts = [part] + [lax.ppermute(part, "head", pairs) for pairs in others]

    keep_masks = rank_keep_mask.astype(jnp.float32)[:, :, None]
    out, query_gradient, low_rank_part, grad_up_part, queries, weights, grad_scores = attention(
        queries_in,
        grads_in,
        up,
        low,
        [
            masks_in,
            own_k,
            own_v,
            *direct,
            *swapped,
            *parts,
        ],
    )

    low_parts = [low_rank_part] + [lax.ppermute(low_rank_part, "head", pairs) for pairs in others]
    send = kv_half(weights, grad_scores, grads_in, queries, keep=False)
    got = lax.ppermute(send, "head", swap)
    keep = kv_half(weights, grad_scores, grads_in, queries, keep=True)
    own_sum, one_sum, two_sum, *packs = pair_sum(keep, got, tokens)
    low_parts, grad_up_part, packs = lax.optimization_barrier((low_parts, grad_up_part, packs))
    low_total = sum(p.astype(jnp.float32) for p in low_parts)
    low_rank = (low_total * keep_masks[0] * adapter_scale).astype(jnp.bfloat16)
    grad_down_part = dot32(low_rank, inputs, NN).astype(jnp.bfloat16)
    packed = jnp.concatenate(
        [
            grad_down_part.reshape(ranks, down_rows, 128),
            grad_up_part.reshape(ranks, up_rows, 128),
        ],
        1,
    )
    received = lax.all_to_all(packed, "ctx", split_axis=0, concat_axis=0)

    packs = [across(p, -(n + 1)) for n, p in enumerate(packs)]
    own_sum, one_sum, two_sum = row_sum(own_sum, one_sum, two_sum, packs)

    def home(piece, back):
        pairs = [
            (
                i * head_count + h,
                (i - back) % ctx * head_count + (h % CORES) * CORES + h // CORES,
            )
            for i in range(ctx)
            for h in range(head_count)
        ]
        return lax.ppermute(piece, ("ctx", "head"), pairs).astype(jnp.float32)

    kv_grad = home(own_sum, 0) + home(one_sum, COLUMNS) + home(two_sum, 2 * COLUMNS)

    keep_row = lax.dynamic_slice_in_dim(keep_masks[1], ctx_place, 1, 0)
    small = [
        a.reshape(-1, 128)
        for a in (
            adapter_down,
            down_first_moment,
            down_second_moment,
            adapter_up,
            up_first_moment,
            up_second_moment,
        )
    ]
    news = pl.pallas_call(
        adam_kernel,
        out_shape=[jax.ShapeDtypeStruct(a.shape, jnp.float32) for a in small],
        compiler_params=pltpu.CompilerParams(vmem_limit_bytes=8 << 20),
        name="adam",
    )(received, *small, keep_row)
    news = [n.reshape(1, -1) for n in news]
    return (out, query_gradient, kv_grad, *news)


def solution(mesh):
    both = P("ctx", "head")
    return jax.shard_map(
        on_device,
        mesh=mesh,
        in_specs=(both, P("ctx", None)) + (both,) * 8 + (P(), P(), P()),
        out_specs=(both,) * 9,
        check_vma=False,
    )
```

```python
import functools
import math

import jax
import jax.numpy as jnp
from jax import lax
from jax.experimental import pallas as pl
from jax.experimental.pallas import tpu as pltpu
from jax.sharding import PartitionSpec as P


HEAD_SIZE = 128
KVH = 2
REACH = 8
CORES = 2
COLUMNS = 4

adapter_scale = 0.25
beta_one = 0.9
beta_two = 0.999
learn_rate = 0.01
adam_epsilon = 1e-08


NN = (((1,), (0,)), ((), ()))
NT = (((1,), (1,)), ((), ()))


def dot32(a, b, dims):
    return lax.dot_general(a, b, dims, preferred_element_type=jnp.float32)


def core_of():
    return lax.rem(lax.axis_index("head"), CORES)


def column_place():
    return lax.rem(lax.axis_index("ctx"), COLUMNS)


def distance(slot, column):
    if slot < 3:
        return (0, COLUMNS, 2 * COLUMNS)[slot]
    step, late = divmod(slot - 1, 2)
    near = column >= step
    return jnp.where(near, step + (0 if late else COLUMNS), step + (COLUMNS if late else 0))


def pack_kernel(own_ref, one_ref, two_ref, *outs):
    column = column_place()
    for n, out in enumerate(outs):
        step = n + 1
        out[0] = one_ref[...]

        @pl.when(column + step < COLUMNS)
        def _():
            out[1] = own_ref[...]

        @pl.when(column + step >= COLUMNS)
        def _():
            out[1] = two_ref[...]


def pack(own, one, two):
    vmem = pl.BlockSpec(memory_space=pltpu.VMEM)
    return pl.pallas_call(
        pack_kernel,
        in_specs=[vmem] * 3,
        out_shape=[jax.ShapeDtypeStruct((2,) + own.shape, own.dtype)] * (COLUMNS - 1),
        compiler_params=pltpu.CompilerParams(vmem_limit_bytes=8 << 20),
        name="pack",
    )(own, one, two)


def stage_kernel(fq_ref, go_ref, fq_out, go_out):
    for h in range(fq_out.shape[0]):
        lanes = pl.ds(h * HEAD_SIZE, HEAD_SIZE)
        fq_out[h] = fq_ref[:, lanes]
        go_out[h] = go_ref[:, lanes]


def stage(fq, go):
    tokens, width = fq.shape
    by_head = jax.ShapeDtypeStruct((width // HEAD_SIZE, tokens, HEAD_SIZE), jnp.bfloat16)
    return pl.pallas_call(
        stage_kernel,
        out_shape=[by_head, by_head],
        compiler_params=pltpu.CompilerParams(vmem_limit_bytes=8 << 20),
        name="stage",
    )(fq, go)


def bounds_kernel(length_ref, shift_ref, mask_ref, mask_out, low_out, *, seq_total):
    tokens = low_out.shape[1]
    kv_head = lax.axis_index("head") // CORES
    length = length_ref[kv_head]
    first = lax.rem(lax.axis_index("ctx") * tokens - shift_ref[kv_head] + seq_total, seq_total)
    within = lax.broadcasted_iota(jnp.int32, (1, tokens), 1)
    in_group = within + lax.rem(first, length)
    in_group = jnp.where(in_group >= length, in_group - length, in_group)
    rolled = within + first
    low_out[...] = within - jnp.where(rolled >= seq_total, rolled - seq_total, in_group)
    mask_out[...] = mask_ref[...]


def bounds(length, shift, masks, tokens, seq_total):
    smem = pl.BlockSpec(memory_space=pltpu.SMEM)
    return pl.pallas_call(
        functools.partial(bounds_kernel, seq_total=seq_total),
        in_specs=[smem, smem, pl.BlockSpec(memory_space=pltpu.VMEM)],
        out_shape=[
            jax.ShapeDtypeStruct(masks.shape, masks.dtype),
            jax.ShapeDtypeStruct((1, tokens), jnp.int32),
        ],
        compiler_params=pltpu.CompilerParams(vmem_limit_bytes=8 << 20),
        name="bounds",
    )(length, shift, masks)


def column_of(row):
    n = row.shape[1]
    eye = lax.broadcasted_iota(jnp.int32, (n, n), 0) == lax.broadcasted_iota(jnp.int32, (n, n), 1)
    return jnp.sum(jnp.where(eye, jnp.broadcast_to(row, (n, n)), 0.0), axis=1, keepdims=True)


def fold(combine, start, x):
    for r in range(0, x.shape[0], 8):
        start = combine(start, x[r : r + 8])
    return start


def attention_kernel(*refs, tokens, heads, score_scale):
    tiles = REACH + 1
    (fq_ref, go_ref, up_ref, low_ref, mask_ref, own_k_ref, own_v_ref) = refs[:7]
    direct, swapped = refs[7:12], refs[12:17]
    parts = refs[17:21]
    out_ref, gq_ref, low_rank_ref, grad_up_ref, q_ref, w_ref, gs_ref = refs[21:28]
    (k_s, v_s, kt_s, vt_s, place_s, s_s, gw_s, a_s, acc_s, lr_s) = refs[28:]
    core = core_of()
    column = column_place()
    exponent = score_scale * math.log2(math.e)

    def rows(d):
        return pl.ds(d * tokens, tokens)

    k_s[rows(0), :] = own_k_ref[...]
    v_s[rows(0), :] = own_v_ref[...]

    def fill(store, pieces):
        store[rows(1), :] = pieces[0][...]
        store[rows(2), :] = pieces[1][...]
        for n in range(1, COLUMNS):
            store[rows(2 * n + 1), :] = pieces[n + 1][0]
            store[rows(2 * n + 2), :] = pieces[n + 1][1]

    @pl.when(core == 0)
    def _():
        fill(k_s, direct)
        fill(v_s, swapped)

    @pl.when(core != 0)
    def _():
        fill(k_s, swapped)
        fill(v_s, direct)

    low = low_ref[...]
    place_s[...] = lax.broadcasted_iota(jnp.int32, (tokens, tokens), 0)
    lr_s[...] = jnp.zeros_like(lr_s)
    masks = mask_ref[...].astype(jnp.float32)
    keep0, keep1 = column_of(masks[0:1]), column_of(masks[1:2])
    total = (parts[0][...].astype(jnp.float32) + parts[1][...].astype(jnp.float32)) + (
        parts[2][...].astype(jnp.float32) + parts[3][...].astype(jnp.float32)
    )
    mpt = (total * keep0).astype(jnp.bfloat16)
    mp = mpt.astype(jnp.float32).T.astype(jnp.bfloat16)

    def lanes(head):
        return pl.ds(pl.multiple_of(head * HEAD_SIZE, HEAD_SIZE), HEAD_SIZE)

    def up_of(head):
        return (up_ref[:, lanes(head)].astype(jnp.float32) * keep1).astype(jnp.bfloat16)

    def make_query(head):
        q_ref[head] = (
            fq_ref[head].astype(jnp.float32) + adapter_scale * dot32(mp, up_of(head), NN)
        ).astype(jnp.bfloat16)

    def scores(head, slot, d, top):
        s = dot32(k_s[rows(d), :], q_ref[head], NT)
        allowed = place_s[...] >= low + distance(d, column) * tokens
        if d == 0:
            allowed = allowed & (place_s[...] <= lax.broadcasted_iota(jnp.int32, s.shape, 1))
        s = jnp.where(allowed, s, -1e30)
        s_s[slot, rows(d), :] = s
        return fold(jnp.maximum, top, s)

    lowest = jnp.full((8, tokens), -1e30, jnp.float32)
    zero = jnp.zeros((8, tokens), jnp.float32)
    make_query(0)
    top = lowest
    for d in range(tiles):
        top = scores(0, 0, d, top)
        kt_s[:, rows(d)] = k_s[rows(d), :].T
        vt_s[:, rows(d)] = v_s[rows(d), :].T

    def one_head(head, top, last):
        slot = lax.rem(head, 2)
        top = jnp.max(top, axis=0, keepdims=True)
        if not last:
            make_query(head + 1)

        total, next_top = zero, lowest
        for d in range(tiles):
            p = jnp.exp2((s_s[slot, rows(d), :] - top) * exponent)
            a_s[slot, rows(d), :] = p
            total = fold(jnp.add, total, p)
            gw_s[slot, rows(d), :] = dot32(v_s[rows(d), :], go_ref[head], NT)
        inverse = 1.0 / jnp.sum(total, axis=0, keepdims=True)
        acc_s[...] = jnp.zeros_like(acc_s)

        dots = zero
        for d in range(tiles):
            w = a_s[slot, rows(d), :] * inverse
            w_half = w.astype(jnp.bfloat16)
            w_ref[head, rows(d), :] = w_half
            a = w * gw_s[slot, rows(d), :]
            gw_s[slot, rows(d), :] = a
            acc_s[...] += dot32(vt_s[:, rows(d)], w_half, NN)
            dots = fold(jnp.add, dots, a)
            if not last:
                next_top = scores(head + 1, 1 - slot, d, next_top)
        out_ref[:, lanes(head)] = acc_s[...].T.astype(jnp.bfloat16)
        dots = jnp.sum(dots, axis=0, keepdims=True) * inverse
        acc_s[...] = jnp.zeros_like(acc_s)

        for d in range(tiles):
            gs = (gw_s[slot, rows(d), :] - a_s[slot, rows(d), :] * dots).astype(jnp.bfloat16)
            gs_ref[head, rows(d), :] = gs
            acc_s[...] += dot32(kt_s[:, rows(d)], gs, NN)
        gq_t = (score_scale * acc_s[...]).astype(jnp.bfloat16)
        gq = (gq_t.astype(jnp.float32).T).astype(jnp.bfloat16)
        gq_ref[:, lanes(head)] = gq
        lr_s[...] += dot32(up_of(head), gq_t, NN)
        grad_up_ref[:, lanes(head)] = (adapter_scale * dot32(mpt, gq, NN)).astype(jnp.bfloat16)
        return next_top

    top = lax.fori_loop(0, heads - 1, lambda h, t: one_head(h, t, False), top)
    one_head(heads - 1, top, True)
    low_rank_ref[...] = lr_s[...].astype(jnp.bfloat16)


def attention(fq, go, up, low, rest):
    heads, tokens, _ = fq.shape
    ranks, width = up.shape
    span = (REACH + 1) * tokens
    vmem = pl.BlockSpec(memory_space=pltpu.VMEM)
    return pl.pallas_call(
        functools.partial(
            attention_kernel,
            tokens=tokens,
            heads=heads,
            score_scale=1.0 / math.sqrt(HEAD_SIZE),
        ),
        in_specs=[vmem] * (4 + len(rest)),
        out_specs=[vmem] * 7,
        scratch_shapes=[
            pltpu.VMEM((span, HEAD_SIZE), jnp.bfloat16),
            pltpu.VMEM((span, HEAD_SIZE), jnp.bfloat16),
            pltpu.VMEM((HEAD_SIZE, span), jnp.bfloat16),
            pltpu.VMEM((HEAD_SIZE, span), jnp.bfloat16),
            pltpu.VMEM((tokens, tokens), jnp.int32),
            pltpu.VMEM((2, span, tokens), jnp.float32),
            pltpu.VMEM((2, span, tokens), jnp.float32),
            pltpu.VMEM((2, span, tokens), jnp.float32),
            pltpu.VMEM((HEAD_SIZE, tokens), jnp.float32),
            pltpu.VMEM((ranks, tokens), jnp.float32),
        ],
        out_shape=[
            jax.ShapeDtypeStruct((tokens, width), jnp.bfloat16),
            jax.ShapeDtypeStruct((tokens, width), jnp.bfloat16),
            jax.ShapeDtypeStruct((ranks, tokens), jnp.bfloat16),
            jax.ShapeDtypeStruct((ranks, width), jnp.bfloat16),
            jax.ShapeDtypeStruct((heads, tokens, HEAD_SIZE), jnp.bfloat16),
            jax.ShapeDtypeStruct((heads, span, tokens), jnp.bfloat16),
            jax.ShapeDtypeStruct((heads, span, tokens), jnp.bfloat16),
        ],
        compiler_params=pltpu.CompilerParams(vmem_limit_bytes=24 << 20),
        cost_estimate=pl.CostEstimate(
            flops=8 * heads * tokens * span * HEAD_SIZE,
            bytes_accessed=8 << 20,
            transcendentals=heads * tokens * span,
        ),
        name="attention",
    )(fq, go, up, low, *rest)


def kv_half_kernel(w_ref, gs_ref, go_ref, q_ref, half_ref, *, keep, score_scale):
    heads, span, tokens = w_ref.shape
    values = (core_of() == 0) != keep

    def product(left_ref, right_ref, scale):
        right = jnp.concatenate([right_ref[h] for h in range(heads)], 0)
        for d in range(span // tokens):
            rows = pl.ds(d * tokens, tokens)
            left = jnp.concatenate([left_ref[h, rows, :] for h in range(heads)], 1)
            half_ref[rows, :] = (scale * dot32(left, right, NN)).astype(half_ref.dtype)

    @pl.when(values)
    def _():
        product(w_ref, go_ref, 1.0)

    @pl.when(jnp.logical_not(values))
    def _():
        product(gs_ref, q_ref, score_scale)


def kv_half(weights, grad_scores, go, queries, keep):
    span = weights.shape[1]
    vmem = pl.BlockSpec(memory_space=pltpu.VMEM)
    return pl.pallas_call(
        functools.partial(kv_half_kernel, keep=keep, score_scale=1.0 / math.sqrt(HEAD_SIZE)),
        in_specs=[vmem] * 4,
        out_specs=vmem,
        out_shape=jax.ShapeDtypeStruct((span, HEAD_SIZE), jnp.float32 if keep else jnp.bfloat16),
        compiler_params=pltpu.CompilerParams(vmem_limit_bytes=6 << 20),
        cost_estimate=pl.CostEstimate(
            flops=2 * span * queries.size, bytes_accessed=2 << 20, transcendentals=0
        ),
        name="kv_keep" if keep else "kv_send",
    )(weights, grad_scores, go, queries)


def pair_sum_kernel(keep_ref, got_ref, own_ref, one_ref, two_ref, *packs):
    tokens = own_ref.shape[0]

    def total(d):
        rows = pl.ds(d * tokens, tokens)
        return keep_ref[rows, :] + got_ref[rows, :].astype(jnp.float32)

    own_ref[...] = total(0)
    one_ref[...] = total(1)
    two_ref[...] = total(2)
    for n, pack_ref in enumerate(packs):
        pack_ref[0] = total(2 * n + 3).astype(jnp.bfloat16)
        pack_ref[1] = total(2 * n + 4).astype(jnp.bfloat16)


def pair_sum(keep, got, tokens):
    tile = (tokens, HEAD_SIZE)
    return pl.pallas_call(
        pair_sum_kernel,
        out_shape=[jax.ShapeDtypeStruct(tile, jnp.float32)] * 3
        + [jax.ShapeDtypeStruct((2,) + tile, jnp.bfloat16)] * (COLUMNS - 1),
        compiler_params=pltpu.CompilerParams(vmem_limit_bytes=12 << 20),
        name="pair_sum",
    )(keep, got)


def row_sum_kernel(own_ref, one_ref, two_ref, *rest):
    column = column_place()
    packs, (own_out, one_out, two_out) = rest[: COLUMNS - 1], rest[COLUMNS - 1 :]
    own, one, two = own_ref[...], one_ref[...], two_ref[...]
    for n, pack_ref in enumerate(packs):
        one = one + pack_ref[0].astype(jnp.float32)
        piece = pack_ref[1].astype(jnp.float32)
        near = jnp.full(piece.shape, n + 1, jnp.int32) + column < COLUMNS
        own = own + jnp.where(near, piece, 0.0)
        two = two + jnp.where(near, 0.0, piece)
    own_out[...] = own.astype(jnp.bfloat16)
    one_out[...] = one.astype(jnp.bfloat16)
    two_out[...] = two.astype(jnp.bfloat16)


def row_sum(own, one, two, packs):
    vmem = pl.BlockSpec(memory_space=pltpu.VMEM)
    return pl.pallas_call(
        row_sum_kernel,
        in_specs=[vmem] * (2 + COLUMNS),
        out_shape=[jax.ShapeDtypeStruct(own.shape, jnp.bfloat16)] * 3,
        compiler_params=pltpu.CompilerParams(vmem_limit_bytes=8 << 20),
        name="row_sum",
    )(own, one, two, *packs)


def spread_kernel(row_ref, out_ref):
    row = row_ref[...].astype(jnp.bfloat16)
    for n in range(out_ref.shape[0]):
        out_ref[n] = row


def spread(row, copies):
    return pl.pallas_call(
        spread_kernel,
        out_shape=jax.ShapeDtypeStruct((copies,) + row.shape, jnp.bfloat16),
        compiler_params=pltpu.CompilerParams(vmem_limit_bytes=4 << 20),
        name="spread",
    )(row)


def adam_kernel(got_ref, pd, md, vd, pu, mu, vu, keep_ref, opd, omd, ovd, opu, omu, ovu):
    down_rows = pd.shape[0]
    total = jnp.sum(got_ref[...].astype(jnp.float32), axis=0)
    grads = (total[:down_rows], total[down_rows:] * keep_ref[0, 0])
    for grad, p, m, v, op, om, ov in (
        (grads[0], pd, md, vd, opd, omd, ovd),
        (grads[1], pu, mu, vu, opu, omu, ovu),
    ):
        first = beta_one * m[...] + (1.0 - beta_one) * grad
        second = beta_two * v[...] + (1.0 - beta_two) * grad * grad
        op[...] = p[...] - learn_rate * first / (jnp.sqrt(second) + adam_epsilon)
        om[...] = first
        ov[...] = second


def on_device(
    frozen_queries,
    key_value_rows,
    output_gradient,
    inputs,
    adapter_down,
    down_first_moment,
    down_second_moment,
    adapter_up,
    up_first_moment,
    up_second_moment,
    rank_keep_mask,
    group_length,
    group_shift,
):
    tokens = frozen_queries.shape[0]
    width = frozen_queries.shape[1]
    model = inputs.shape[1]
    ctx = lax.axis_size("ctx")
    head_count = lax.axis_size("head")
    ctx_place = lax.axis_index("ctx")
    head_place = lax.axis_index("head")
    core = head_place % CORES
    kv_head = head_place // CORES
    key_width = KVH * HEAD_SIZE
    ranks = rank_keep_mask.shape[1]

    own_k = lax.dynamic_slice_in_dim(key_value_rows, kv_head * HEAD_SIZE, HEAD_SIZE, 1)
    own_v = lax.dynamic_slice_in_dim(key_value_rows, key_width + kv_head * HEAD_SIZE, HEAD_SIZE, 1)
    mine = lax.dynamic_slice_in_dim(
        key_value_rows, core * key_width + kv_head * HEAD_SIZE, HEAD_SIZE, 1
    )
    swap = [(h, h ^ 1) for h in range(head_count)]

    def along(piece, step):
        return lax.ppermute(piece, "ctx", [(i, (i + step) % ctx) for i in range(ctx)])

    def across(piece, step):
        pairs = [(i, i // COLUMNS * COLUMNS + (i + step) % COLUMNS) for i in range(ctx)]
        return lax.ppermute(piece, "ctx", pairs)

    one, two = along(mine, COLUMNS), along(mine, 2 * COLUMNS)

    down_rows, up_rows = model // 128, width // 128
    row = jnp.concatenate(
        [adapter_down.reshape(down_rows, 128), adapter_up.reshape(up_rows, 128)], 0
    )
    row = spread(row, ctx)
    gathered = lax.all_to_all(row, "ctx", split_axis=0, concat_axis=0)
    packs = pack(mine, one, two)
    direct = [one, two] + [across(p, n + 1) for n, p in enumerate(packs)]
    queries_in, grads_in = stage(frozen_queries, output_gradient)
    masks_in, low = bounds(group_length, group_shift, rank_keep_mask, tokens, tokens * ctx)
    swapped = [lax.ppermute(piece, "head", swap) for piece in direct]

    down = gathered[:, :down_rows].reshape(ranks, model)
    up = gathered[:, down_rows:].reshape(ranks, width)

    part = dot32(down, inputs, NT).astype(jnp.bfloat16)
    others = [[(h, h ^ k) for h in range(head_count)] for k in range(1, head_count)]
    parts = [part] + [lax.ppermute(part, "head", pairs) for pairs in others]

    keep_masks = rank_keep_mask.astype(jnp.float32)[:, :, None]
    out, query_gradient, low_rank_part, grad_up_part, queries, weights, grad_scores = attention(
        queries_in,
        grads_in,
        up,
        low,
        [
            masks_in,
            own_k,
            own_v,
            *direct,
            *swapped,
            *parts,
        ],
    )

    low_parts = [low_rank_part] + [lax.ppermute(low_rank_part, "head", pairs) for pairs in others]
    send = kv_half(weights, grad_scores, grads_in, queries, keep=False)
    got = lax.ppermute(send, "head", swap)
    keep = kv_half(weights, grad_scores, grads_in, queries, keep=True)
    own_sum, one_sum, two_sum, *packs = pair_sum(keep, got, tokens)
    low_parts, grad_up_part, packs = lax.optimization_barrier((low_parts, grad_up_part, packs))
    low_total = sum(p.astype(jnp.float32) for p in low_parts)
    low_rank = (low_total * keep_masks[0] * adapter_scale).astype(jnp.bfloat16)
    grad_down_part = dot32(low_rank, inputs, NN).astype(jnp.bfloat16)
    packed = jnp.concatenate(
        [
            grad_down_part.reshape(ranks, down_rows, 128),
            grad_up_part.reshape(ranks, up_rows, 128),
        ],
        1,
    )
    received = lax.all_to_all(packed, "ctx", split_axis=0, concat_axis=0)

    packs = [across(p, -(n + 1)) for n, p in enumerate(packs)]
    own_sum, one_sum, two_sum = row_sum(own_sum, one_sum, two_sum, packs)

    def home(piece, back):
        pairs = [
            (
                i * head_count + h,
                (i - back) % ctx * head_count + (h % CORES) * CORES + h // CORES,
            )
            for i in range(ctx)
            for h in range(head_count)
        ]
        piece = lax.ppermute(piece, ("ctx", "head"), pairs)
        return piece.astype(jnp.float32)

    kv_grad = home(own_sum, 0) + home(one_sum, COLUMNS) + home(two_sum, 2 * COLUMNS)

    keep_row = lax.dynamic_slice_in_dim(keep_masks[1], ctx_place, 1, 0)
    small = [
        a.reshape(-1, 128)
        for a in (
            adapter_down,
            down_first_moment,
            down_second_moment,
            adapter_up,
            up_first_moment,
            up_second_moment,
        )
    ]
    news = pl.pallas_call(
        adam_kernel,
        out_shape=[jax.ShapeDtypeStruct(a.shape, jnp.float32) for a in small],
        compiler_params=pltpu.CompilerParams(vmem_limit_bytes=8 << 20),
        name="adam",
    )(received, *small, keep_row)
    news = [n.reshape(1, -1) for n in news]
    return (out, query_gradient, kv_grad, *news)


def solution(mesh):
    both = P("ctx", "head")
    return jax.shard_map(
        on_device,
        mesh=mesh,
        in_specs=(both, P("ctx", None)) + (both,) * 8 + (P(), P(), P()),
        out_specs=(both,) * 9,
        check_vma=False,
    )
```

```python
import functools
import math

import jax
import jax.numpy as jnp
from jax import lax
from jax.experimental import pallas as pl
from jax.experimental.pallas import tpu as pltpu
from jax.sharding import PartitionSpec as P


HEAD_SIZE = 128
KVH = 2
REACH = 8
CORES = 2
COLUMNS = 4

adapter_scale = 0.25
beta_one = 0.9
beta_two = 0.999
learn_rate = 0.01
adam_epsilon = 1e-08


NN = (((1,), (0,)), ((), ()))
NT = (((1,), (1,)), ((), ()))


def dot32(a, b, dims):
    return lax.dot_general(a, b, dims, preferred_element_type=jnp.float32)


def core_of():
    return lax.rem(lax.axis_index("head"), CORES)


def column_place():
    return lax.rem(lax.axis_index("ctx"), COLUMNS)


def distance(slot, column):
    if slot < 3:
        return (0, COLUMNS, 2 * COLUMNS)[slot]
    step, late = divmod(slot - 1, 2)
    near = column >= step
    return jnp.where(near, step + (0 if late else COLUMNS), step + (COLUMNS if late else 0))


def pack_kernel(own_ref, one_ref, two_ref, *outs):
    column = column_place()
    for n, out in enumerate(outs):
        step = n + 1
        out[0] = one_ref[...]

        @pl.when(column + step < COLUMNS)
        def _():
            out[1] = own_ref[...]

        @pl.when(column + step >= COLUMNS)
        def _():
            out[1] = two_ref[...]


def pack(own, one, two):
    vmem = pl.BlockSpec(memory_space=pltpu.VMEM)
    return pl.pallas_call(
        pack_kernel,
        in_specs=[vmem] * 3,
        out_shape=[jax.ShapeDtypeStruct((2,) + own.shape, own.dtype)] * (COLUMNS - 1),
        compiler_params=pltpu.CompilerParams(vmem_limit_bytes=8 << 20),
        name="pack",
    )(own, one, two)


def stage_kernel(fq_ref, go_ref, fq_out, go_out):
    for h in range(fq_out.shape[0]):
        lanes = pl.ds(h * HEAD_SIZE, HEAD_SIZE)
        fq_out[h] = fq_ref[:, lanes]
        go_out[h] = go_ref[:, lanes]


def stage(fq, go):
    tokens, width = fq.shape
    by_head = jax.ShapeDtypeStruct((width // HEAD_SIZE, tokens, HEAD_SIZE), jnp.bfloat16)
    return pl.pallas_call(
        stage_kernel,
        out_shape=[by_head, by_head],
        compiler_params=pltpu.CompilerParams(vmem_limit_bytes=8 << 20),
        name="stage",
    )(fq, go)


def bounds_kernel(length_ref, shift_ref, mask_ref, mask_out, low_out, *, seq_total):
    tokens = low_out.shape[1]
    kv_head = lax.axis_index("head") // CORES
    length = length_ref[kv_head]
    first = lax.rem(lax.axis_index("ctx") * tokens - shift_ref[kv_head] + seq_total, seq_total)
    within = lax.broadcasted_iota(jnp.int32, (1, tokens), 1)
    in_group = within + lax.rem(first, length)
    in_group = jnp.where(in_group >= length, in_group - length, in_group)
    rolled = within + first
    low_out[...] = within - jnp.where(rolled >= seq_total, rolled - seq_total, in_group)
    mask_out[...] = mask_ref[...]


def bounds(length, shift, masks, tokens, seq_total):
    smem = pl.BlockSpec(memory_space=pltpu.SMEM)
    return pl.pallas_call(
        functools.partial(bounds_kernel, seq_total=seq_total),
        in_specs=[smem, smem, pl.BlockSpec(memory_space=pltpu.VMEM)],
        out_shape=[
            jax.ShapeDtypeStruct(masks.shape, masks.dtype),
            jax.ShapeDtypeStruct((1, tokens), jnp.int32),
        ],
        compiler_params=pltpu.CompilerParams(vmem_limit_bytes=8 << 20),
        name="bounds",
    )(length, shift, masks)


def column_of(row):
    n = row.shape[1]
    eye = lax.broadcasted_iota(jnp.int32, (n, n), 0) == lax.broadcasted_iota(jnp.int32, (n, n), 1)
    return jnp.sum(jnp.where(eye, jnp.broadcast_to(row, (n, n)), 0.0), axis=1, keepdims=True)


def fold(combine, start, x):
    for r in range(0, x.shape[0], 8):
        start = combine(start, x[r : r + 8])
    return start


def attention_kernel(*refs, tokens, heads, score_scale):
    tiles = REACH + 1
    (fq_ref, go_ref, up_ref, low_ref, mask_ref, own_k_ref, own_v_ref) = refs[:7]
    direct, swapped = refs[7:12], refs[12:17]
    parts = refs[17:21]
    out_ref, gq_ref, low_rank_ref, grad_up_ref, q_ref, w_ref, gs_ref = refs[21:28]
    (k_s, v_s, kt_s, vt_s, place_s, s_s, gw_s, a_s, acc_s, lr_s) = refs[28:]
    core = core_of()
    column = column_place()
    exponent = score_scale * math.log2(math.e)

    def rows(d):
        return pl.ds(d * tokens, tokens)

    k_s[rows(0), :] = own_k_ref[...]
    v_s[rows(0), :] = own_v_ref[...]

    def fill(store, pieces):
        store[rows(1), :] = pieces[0][...]
        store[rows(2), :] = pieces[1][...]
        for n in range(1, COLUMNS):
            store[rows(2 * n + 1), :] = pieces[n + 1][0]
            store[rows(2 * n + 2), :] = pieces[n + 1][1]

    @pl.when(core == 0)
    def _():
        fill(k_s, direct)
        fill(v_s, swapped)

    @pl.when(core != 0)
    def _():
        fill(k_s, swapped)
        fill(v_s, direct)

    low = low_ref[...]
    place_s[...] = lax.broadcasted_iota(jnp.int32, (tokens, tokens), 0)
    lr_s[...] = jnp.zeros_like(lr_s)
    masks = mask_ref[...].astype(jnp.float32)
    keep0, keep1 = column_of(masks[0:1]), column_of(masks[1:2])
    total = (parts[0][...].astype(jnp.float32) + parts[1][...].astype(jnp.float32)) + (
        parts[2][...].astype(jnp.float32) + parts[3][...].astype(jnp.float32)
    )
    mpt = (total * keep0).astype(jnp.bfloat16)
    mp = mpt.astype(jnp.float32).T.astype(jnp.bfloat16)

    def lanes(head):
        return pl.ds(pl.multiple_of(head * HEAD_SIZE, HEAD_SIZE), HEAD_SIZE)

    def up_of(head):
        return (up_ref[:, lanes(head)].astype(jnp.float32) * keep1).astype(jnp.bfloat16)

    def make_query(head):
        q_ref[head] = (
            fq_ref[head].astype(jnp.float32) + adapter_scale * dot32(mp, up_of(head), NN)
        ).astype(jnp.bfloat16)

    def scores(head, slot, d, top):
        s = dot32(k_s[rows(d), :], q_ref[head], NT)
        allowed = place_s[...] >= low + distance(d, column) * tokens
        if d == 0:
            allowed = allowed & (place_s[...] <= lax.broadcasted_iota(jnp.int32, s.shape, 1))
        s = jnp.where(allowed, s, -1e30)
        s_s[slot, rows(d), :] = s
        return fold(jnp.maximum, top, s)

    lowest = jnp.full((8, tokens), -1e30, jnp.float32)
    zero = jnp.zeros((8, tokens), jnp.float32)
    make_query(0)
    top = lowest
    for d in range(tiles):
        top = scores(0, 0, d, top)
        kt_s[:, rows(d)] = k_s[rows(d), :].T
        vt_s[:, rows(d)] = v_s[rows(d), :].T

    def one_head(head, top, last):
        slot = lax.rem(head, 2)
        top = jnp.max(top, axis=0, keepdims=True)
        if not last:
            make_query(head + 1)

        total, next_top = zero, lowest
        for d in range(tiles):
            p = jnp.exp2((s_s[slot, rows(d), :] - top) * exponent)
            a_s[slot, rows(d), :] = p
            total = fold(jnp.add, total, p)
            gw_s[slot, rows(d), :] = dot32(v_s[rows(d), :], go_ref[head], NT)
        inverse = 1.0 / jnp.sum(total, axis=0, keepdims=True)
        acc_s[...] = jnp.zeros_like(acc_s)

        dots = zero
        for d in range(tiles):
            w = a_s[slot, rows(d), :] * inverse
            w_half = w.astype(jnp.bfloat16)
            w_ref[head, rows(d), :] = w_half
            a = w * gw_s[slot, rows(d), :]
            gw_s[slot, rows(d), :] = a
            acc_s[...] += dot32(vt_s[:, rows(d)], w_half, NN)
            dots = fold(jnp.add, dots, a)
            if not last:
                next_top = scores(head + 1, 1 - slot, d, next_top)
        out_ref[:, lanes(head)] = acc_s[...].T.astype(jnp.bfloat16)
        dots = jnp.sum(dots, axis=0, keepdims=True) * inverse
        acc_s[...] = jnp.zeros_like(acc_s)

        for d in range(tiles):
            gs = (gw_s[slot, rows(d), :] - a_s[slot, rows(d), :] * dots).astype(jnp.bfloat16)
            gs_ref[head, rows(d), :] = gs
            acc_s[...] += dot32(kt_s[:, rows(d)], gs, NN)
        gq_t = (score_scale * acc_s[...]).astype(jnp.bfloat16)
        gq = (gq_t.astype(jnp.float32).T).astype(jnp.bfloat16)
        gq_ref[:, lanes(head)] = gq
        lr_s[...] += dot32(up_of(head), gq_t, NN)
        grad_up_ref[:, lanes(head)] = (adapter_scale * dot32(mpt, gq, NN)).astype(jnp.bfloat16)
        return next_top

    top = lax.fori_loop(0, heads - 1, lambda h, t: one_head(h, t, False), top)
    one_head(heads - 1, top, True)
    low_rank_ref[...] = lr_s[...].astype(jnp.bfloat16)


def attention(fq, go, up, low, rest):
    heads, tokens, _ = fq.shape
    ranks, width = up.shape
    span = (REACH + 1) * tokens
    vmem = pl.BlockSpec(memory_space=pltpu.VMEM)
    return pl.pallas_call(
        functools.partial(
            attention_kernel,
            tokens=tokens,
            heads=heads,
            score_scale=1.0 / math.sqrt(HEAD_SIZE),
        ),
        in_specs=[vmem] * (4 + len(rest)),
        out_specs=[vmem] * 7,
        scratch_shapes=[
            pltpu.VMEM((span, HEAD_SIZE), jnp.bfloat16),
            pltpu.VMEM((span, HEAD_SIZE), jnp.bfloat16),
            pltpu.VMEM((HEAD_SIZE, span), jnp.bfloat16),
            pltpu.VMEM((HEAD_SIZE, span), jnp.bfloat16),
            pltpu.VMEM((tokens, tokens), jnp.int32),
            pltpu.VMEM((2, span, tokens), jnp.float32),
            pltpu.VMEM((2, span, tokens), jnp.float32),
            pltpu.VMEM((2, span, tokens), jnp.float32),
            pltpu.VMEM((HEAD_SIZE, tokens), jnp.float32),
            pltpu.VMEM((ranks, tokens), jnp.float32),
        ],
        out_shape=[
            jax.ShapeDtypeStruct((tokens, width), jnp.bfloat16),
            jax.ShapeDtypeStruct((tokens, width), jnp.bfloat16),
            jax.ShapeDtypeStruct((ranks, tokens), jnp.bfloat16),
            jax.ShapeDtypeStruct((ranks, width), jnp.bfloat16),
            jax.ShapeDtypeStruct((heads, tokens, HEAD_SIZE), jnp.bfloat16),
            jax.ShapeDtypeStruct((heads, span, tokens), jnp.bfloat16),
            jax.ShapeDtypeStruct((heads, span, tokens), jnp.bfloat16),
        ],
        compiler_params=pltpu.CompilerParams(vmem_limit_bytes=24 << 20),
        cost_estimate=pl.CostEstimate(
            flops=8 * heads * tokens * span * HEAD_SIZE,
            bytes_accessed=8 << 20,
            transcendentals=heads * tokens * span,
        ),
        name="attention",
    )(fq, go, up, low, *rest)


def kv_half_kernel(w_ref, gs_ref, go_ref, q_ref, half_ref, *, keep, score_scale):
    heads, span, tokens = w_ref.shape
    values = (core_of() == 0) != keep

    def product(left_ref, right_ref, scale):
        right = jnp.concatenate([right_ref[h] for h in range(heads)], 0)
        for d in range(span // tokens):
            rows = pl.ds(d * tokens, tokens)
            left = jnp.concatenate([left_ref[h, rows, :] for h in range(heads)], 1)
            half_ref[rows, :] = (scale * dot32(left, right, NN)).astype(half_ref.dtype)

    @pl.when(values)
    def _():
        product(w_ref, go_ref, 1.0)

    @pl.when(jnp.logical_not(values))
    def _():
        product(gs_ref, q_ref, score_scale)


def kv_half(weights, grad_scores, go, queries, keep):
    span = weights.shape[1]
    vmem = pl.BlockSpec(memory_space=pltpu.VMEM)
    return pl.pallas_call(
        functools.partial(kv_half_kernel, keep=keep, score_scale=1.0 / math.sqrt(HEAD_SIZE)),
        in_specs=[vmem] * 4,
        out_specs=vmem,
        out_shape=jax.ShapeDtypeStruct((span, HEAD_SIZE), jnp.float32 if keep else jnp.bfloat16),
        compiler_params=pltpu.CompilerParams(vmem_limit_bytes=6 << 20),
        cost_estimate=pl.CostEstimate(
            flops=2 * span * queries.size, bytes_accessed=2 << 20, transcendentals=0
        ),
        name="kv_keep" if keep else "kv_send",
    )(weights, grad_scores, go, queries)


def pair_sum_kernel(keep_ref, got_ref, own_ref, one_ref, two_ref, *packs):
    tokens = own_ref.shape[0]

    def total(d):
        rows = pl.ds(d * tokens, tokens)
        return keep_ref[rows, :] + got_ref[rows, :].astype(jnp.float32)

    own_ref[...] = total(0)
    one_ref[...] = total(1)
    two_ref[...] = total(2)
    for n, pack_ref in enumerate(packs):
        pack_ref[0] = total(2 * n + 3).astype(jnp.bfloat16)
        pack_ref[1] = total(2 * n + 4).astype(jnp.bfloat16)


def pair_sum(keep, got, tokens):
    tile = (tokens, HEAD_SIZE)
    return pl.pallas_call(
        pair_sum_kernel,
        out_shape=[jax.ShapeDtypeStruct(tile, jnp.float32)] * 3
        + [jax.ShapeDtypeStruct((2,) + tile, jnp.bfloat16)] * (COLUMNS - 1),
        compiler_params=pltpu.CompilerParams(vmem_limit_bytes=12 << 20),
        name="pair_sum",
    )(keep, got)


def row_sum_kernel(own_ref, one_ref, two_ref, *rest):
    column = column_place()
    packs, (own_out, one_out, two_out) = rest[: COLUMNS - 1], rest[COLUMNS - 1 :]
    own, one, two = own_ref[...], one_ref[...], two_ref[...]
    for n, pack_ref in enumerate(packs):
        one = one + pack_ref[0].astype(jnp.float32)
        piece = pack_ref[1].astype(jnp.float32)
        near = jnp.full(piece.shape, n + 1, jnp.int32) + column < COLUMNS
        own = own + jnp.where(near, piece, 0.0)
        two = two + jnp.where(near, 0.0, piece)
    own_out[...] = own.astype(jnp.bfloat16)
    one_out[...] = one.astype(jnp.bfloat16)
    two_out[...] = two.astype(jnp.bfloat16)


def row_sum(own, one, two, packs):
    vmem = pl.BlockSpec(memory_space=pltpu.VMEM)
    return pl.pallas_call(
        row_sum_kernel,
        in_specs=[vmem] * (2 + COLUMNS),
        out_shape=[jax.ShapeDtypeStruct(own.shape, jnp.bfloat16)] * 3,
        compiler_params=pltpu.CompilerParams(vmem_limit_bytes=8 << 20),
        name="row_sum",
    )(own, one, two, *packs)


def spread_kernel(row_ref, out_ref):
    row = row_ref[...].astype(jnp.bfloat16)
    for n in range(out_ref.shape[0]):
        out_ref[n] = row


def spread(row, copies):
    return pl.pallas_call(
        spread_kernel,
        out_shape=jax.ShapeDtypeStruct((copies,) + row.shape, jnp.bfloat16),
        compiler_params=pltpu.CompilerParams(vmem_limit_bytes=4 << 20),
        name="spread",
    )(row)


def adam_kernel(got_ref, pd, md, vd, pu, mu, vu, keep_ref, opd, omd, ovd, opu, omu, ovu):
    down_rows = pd.shape[0]
    total = jnp.sum(got_ref[...].astype(jnp.float32), axis=0)
    grads = (total[:down_rows], total[down_rows:] * keep_ref[0, 0])
    for grad, p, m, v, op, om, ov in (
        (grads[0], pd, md, vd, opd, omd, ovd),
        (grads[1], pu, mu, vu, opu, omu, ovu),
    ):
        first = beta_one * m[...] + (1.0 - beta_one) * grad
        second = beta_two * v[...] + (1.0 - beta_two) * grad * grad
        op[...] = p[...] - learn_rate * first / (jnp.sqrt(second) + adam_epsilon)
        om[...] = first
        ov[...] = second


def on_device(
    frozen_queries,
    key_value_rows,
    output_gradient,
    inputs,
    adapter_down,
    down_first_moment,
    down_second_moment,
    adapter_up,
    up_first_moment,
    up_second_moment,
    rank_keep_mask,
    group_length,
    group_shift,
):
    tokens = frozen_queries.shape[0]
    width = frozen_queries.shape[1]
    model = inputs.shape[1]
    ctx = lax.axis_size("ctx")
    head_count = lax.axis_size("head")
    ctx_place = lax.axis_index("ctx")
    head_place = lax.axis_index("head")
    core = head_place % CORES
    kv_head = head_place // CORES
    key_width = KVH * HEAD_SIZE
    ranks = rank_keep_mask.shape[1]

    own_k = lax.dynamic_slice_in_dim(key_value_rows, kv_head * HEAD_SIZE, HEAD_SIZE, 1)
    own_v = lax.dynamic_slice_in_dim(key_value_rows, key_width + kv_head * HEAD_SIZE, HEAD_SIZE, 1)
    mine = lax.dynamic_slice_in_dim(
        key_value_rows, core * key_width + kv_head * HEAD_SIZE, HEAD_SIZE, 1
    )
    swap = [(h, h ^ 1) for h in range(head_count)]

    def along(piece, step):
        return lax.ppermute(piece, "ctx", [(i, (i + step) % ctx) for i in range(ctx)])

    def across(piece, step):
        pairs = [(i, i // COLUMNS * COLUMNS + (i + step) % COLUMNS) for i in range(ctx)]
        return lax.ppermute(piece, "ctx", pairs)

    one, two = along(mine, COLUMNS), along(mine, 2 * COLUMNS)

    down_rows, up_rows = model // 128, width // 128
    row = jnp.concatenate(
        [adapter_down.reshape(down_rows, 128), adapter_up.reshape(up_rows, 128)], 0
    )
    row = spread(row, ctx)
    gathered = lax.all_to_all(row, "ctx", split_axis=0, concat_axis=0)
    packs = pack(mine, one, two)
    far = across(packs[1], 2)
    direct = [one, two, across(packs[0], 1), far, across(packs[2], 3)]
    queries_in, grads_in = stage(frozen_queries, output_gradient)
    masks_in, low = bounds(group_length, group_shift, rank_keep_mask, tokens, tokens * ctx)
    swapped = [lax.ppermute(piece, "head", swap) for piece in direct]

    down = gathered[:, :down_rows].reshape(ranks, model)
    up = gathered[:, down_rows:].reshape(ranks, width)

    part = dot32(down, inputs, NT).astype(jnp.bfloat16)
    others = [[(h, h ^ k) for h in range(head_count)] for k in range(head_count - 1, 0, -1)]
    parts = [part] + [lax.ppermute(part, "head", pairs) for pairs in others]

    keep_masks = rank_keep_mask.astype(jnp.float32)[:, :, None]
    out, query_gradient, low_rank_part, grad_up_part, queries, weights, grad_scores = attention(
        queries_in,
        grads_in,
        up,
        low,
        [
            masks_in,
            own_k,
            own_v,
            *direct,
            *swapped,
            *parts,
        ],
    )

    low_parts = [low_rank_part] + [lax.ppermute(low_rank_part, "head", pairs) for pairs in others]
    send = kv_half(weights, grad_scores, grads_in, queries, keep=False)
    got = lax.ppermute(send, "head", swap)
    keep = kv_half(weights, grad_scores, grads_in, queries, keep=True)
    own_sum, one_sum, two_sum, *packs = pair_sum(keep, got, tokens)
    low_parts, grad_up_part, packs = lax.optimization_barrier((low_parts, grad_up_part, packs))
    low_total = sum(p.astype(jnp.float32) for p in low_parts)
    low_rank = (low_total * keep_masks[0] * adapter_scale).astype(jnp.bfloat16)
    grad_down_part = dot32(low_rank, inputs, NN).astype(jnp.bfloat16)
    packed = jnp.concatenate(
        [
            grad_down_part.reshape(ranks, down_rows, 128),
            grad_up_part.reshape(ranks, up_rows, 128),
        ],
        1,
    )
    received = lax.all_to_all(packed, "ctx", split_axis=0, concat_axis=0)

    packs = [across(p, -(n + 1)) for n, p in enumerate(packs)]
    own_sum, one_sum, two_sum = row_sum(own_sum, one_sum, two_sum, packs)

    def home(piece, back):
        pairs = [
            (
                i * head_count + h,
                (i - back) % ctx * head_count + (h % CORES) * CORES + h // CORES,
            )
            for i in range(ctx)
            for h in range(head_count)
        ]
        piece = lax.ppermute(piece, ("ctx", "head"), pairs)
        return piece.astype(jnp.float32)

    kv_grad = home(two_sum, 2 * COLUMNS) + home(one_sum, COLUMNS) + home(own_sum, 0)

    keep_row = lax.dynamic_slice_in_dim(keep_masks[1], ctx_place, 1, 0)
    small = [
        a.reshape(-1, 128)
        for a in (
            adapter_down,
            down_first_moment,
            down_second_moment,
            adapter_up,
            up_first_moment,
            up_second_moment,
        )
    ]
    news = pl.pallas_call(
        adam_kernel,
        out_shape=[jax.ShapeDtypeStruct(a.shape, jnp.float32) for a in small],
        compiler_params=pltpu.CompilerParams(vmem_limit_bytes=8 << 20),
        name="adam",
    )(received, *small, keep_row)
    news = [n.reshape(1, -1) for n in news]
    return (out, query_gradient, kv_grad, *news)


def solution(mesh):
    both = P("ctx", "head")
    return jax.shard_map(
        on_device,
        mesh=mesh,
        in_specs=(both, P("ctx", None)) + (both,) * 8 + (P(), P(), P()),
        out_specs=(both,) * 9,
        check_vma=False,
    )
```

```python
import functools
import math

import jax
import jax.numpy as jnp
from jax import lax
from jax.experimental import pallas as pl
from jax.experimental.pallas import tpu as pltpu
from jax.sharding import PartitionSpec as P


HEAD_SIZE = 128
KVH = 2
REACH = 8
CORES = 2
COLUMNS = 4

adapter_scale = 0.25
beta_one = 0.9
beta_two = 0.999
learn_rate = 0.01
adam_epsilon = 1e-08


NN = (((1,), (0,)), ((), ()))
NT = (((1,), (1,)), ((), ()))


def dot32(a, b, dims):
    return lax.dot_general(a, b, dims, preferred_element_type=jnp.float32)


def core_of():
    return lax.rem(lax.axis_index("head"), CORES)


def column_place():
    return lax.rem(lax.axis_index("ctx"), COLUMNS)


def distance(slot, column):
    if slot < 3:
        return (0, COLUMNS, 2 * COLUMNS)[slot]
    step, late = divmod(slot - 1, 2)
    near = column >= step
    return jnp.where(near, step + (0 if late else COLUMNS), step + (COLUMNS if late else 0))


def pack_kernel(own_ref, one_ref, two_ref, *outs):
    column = column_place()
    for n, out in enumerate(outs):
        step = n + 1
        out[0] = one_ref[...]

        @pl.when(column + step < COLUMNS)
        def _():
            out[1] = own_ref[...]

        @pl.when(column + step >= COLUMNS)
        def _():
            out[1] = two_ref[...]


def pack(own, one, two):
    vmem = pl.BlockSpec(memory_space=pltpu.VMEM)
    return pl.pallas_call(
        pack_kernel,
        in_specs=[vmem] * 3,
        out_shape=[jax.ShapeDtypeStruct((2,) + own.shape, own.dtype)] * (COLUMNS - 1),
        compiler_params=pltpu.CompilerParams(vmem_limit_bytes=8 << 20),
        name="pack",
    )(own, one, two)


def stage_kernel(fq_ref, go_ref, fq_out, go_out):
    for h in range(fq_out.shape[0]):
        lanes = pl.ds(h * HEAD_SIZE, HEAD_SIZE)
        fq_out[h] = fq_ref[:, lanes]
        go_out[h] = go_ref[:, lanes]


def stage(fq, go):
    tokens, width = fq.shape
    by_head = jax.ShapeDtypeStruct((width // HEAD_SIZE, tokens, HEAD_SIZE), jnp.bfloat16)
    return pl.pallas_call(
        stage_kernel,
        out_shape=[by_head, by_head],
        compiler_params=pltpu.CompilerParams(vmem_limit_bytes=8 << 20),
        name="stage",
    )(fq, go)


def bounds_kernel(length_ref, shift_ref, mask_ref, mask_out, low_out, *, seq_total):
    tokens = low_out.shape[1]
    kv_head = lax.axis_index("head") // CORES
    length = length_ref[kv_head]
    first = lax.rem(lax.axis_index("ctx") * tokens - shift_ref[kv_head] + seq_total, seq_total)
    within = lax.broadcasted_iota(jnp.int32, (1, tokens), 1)
    in_group = within + lax.rem(first, length)
    in_group = jnp.where(in_group >= length, in_group - length, in_group)
    rolled = within + first
    low_out[...] = within - jnp.where(rolled >= seq_total, rolled - seq_total, in_group)
    mask_out[...] = mask_ref[...]


def bounds(length, shift, masks, tokens, seq_total):
    smem = pl.BlockSpec(memory_space=pltpu.SMEM)
    return pl.pallas_call(
        functools.partial(bounds_kernel, seq_total=seq_total),
        in_specs=[smem, smem, pl.BlockSpec(memory_space=pltpu.VMEM)],
        out_shape=[
            jax.ShapeDtypeStruct(masks.shape, masks.dtype),
            jax.ShapeDtypeStruct((1, tokens), jnp.int32),
        ],
        compiler_params=pltpu.CompilerParams(vmem_limit_bytes=8 << 20),
        name="bounds",
    )(length, shift, masks)


def column_of(row):
    n = row.shape[1]
    eye = lax.broadcasted_iota(jnp.int32, (n, n), 0) == lax.broadcasted_iota(jnp.int32, (n, n), 1)
    return jnp.sum(jnp.where(eye, jnp.broadcast_to(row, (n, n)), 0.0), axis=1, keepdims=True)


def fold(combine, start, x):
    for r in range(0, x.shape[0], 8):
        start = combine(start, x[r : r + 8])
    return start


def attention_kernel(*refs, tokens, heads, score_scale):
    tiles = REACH + 1
    (fq_ref, go_ref, up_ref, low_ref, mask_ref, own_k_ref, own_v_ref) = refs[:7]
    direct, swapped = refs[7:12], refs[12:17]
    parts = refs[17:21]
    out_ref, gq_ref, low_rank_ref, grad_up_ref, q_ref, w_ref, gs_ref = refs[21:28]
    (k_s, v_s, kt_s, vt_s, place_s, s_s, gw_s, a_s, acc_s, lr_s) = refs[28:]
    core = core_of()
    column = column_place()
    exponent = score_scale * math.log2(math.e)

    def rows(d):
        return pl.ds(d * tokens, tokens)

    k_s[rows(0), :] = own_k_ref[...]
    v_s[rows(0), :] = own_v_ref[...]

    def fill(store, pieces):
        store[rows(1), :] = pieces[0][...]
        store[rows(2), :] = pieces[1][...]
        for n in range(1, COLUMNS):
            store[rows(2 * n + 1), :] = pieces[n + 1][0]
            store[rows(2 * n + 2), :] = pieces[n + 1][1]

    @pl.when(core == 0)
    def _():
        fill(k_s, direct)
        fill(v_s, swapped)

    @pl.when(core != 0)
    def _():
        fill(k_s, swapped)
        fill(v_s, direct)

    low = low_ref[...]
    place_s[...] = lax.broadcasted_iota(jnp.int32, (tokens, tokens), 0)
    lr_s[...] = jnp.zeros_like(lr_s)
    masks = mask_ref[...].astype(jnp.float32)
    keep0, keep1 = column_of(masks[0:1]), column_of(masks[1:2])
    total = (parts[0][...].astype(jnp.float32) + parts[1][...].astype(jnp.float32)) + (
        parts[2][...].astype(jnp.float32) + parts[3][...].astype(jnp.float32)
    )
    mpt = (total * keep0).astype(jnp.bfloat16)
    mp = mpt.astype(jnp.float32).T.astype(jnp.bfloat16)

    def lanes(head):
        return pl.ds(pl.multiple_of(head * HEAD_SIZE, HEAD_SIZE), HEAD_SIZE)

    def up_of(head):
        return (up_ref[:, lanes(head)].astype(jnp.float32) * keep1).astype(jnp.bfloat16)

    def make_query(head):
        q_ref[head] = (
            fq_ref[head].astype(jnp.float32) + adapter_scale * dot32(mp, up_of(head), NN)
        ).astype(jnp.bfloat16)

    def scores(head, slot, d, top):
        s = dot32(k_s[rows(d), :], q_ref[head], NT)
        allowed = place_s[...] >= low + distance(d, column) * tokens
        if d == 0:
            allowed = allowed & (place_s[...] <= lax.broadcasted_iota(jnp.int32, s.shape, 1))
        s = jnp.where(allowed, s, -1e30)
        s_s[slot, rows(d), :] = s
        return fold(jnp.maximum, top, s)

    lowest = jnp.full((8, tokens), -1e30, jnp.float32)
    zero = jnp.zeros((8, tokens), jnp.float32)
    make_query(0)
    top = lowest
    for d in range(tiles):
        top = scores(0, 0, d, top)
        kt_s[:, rows(d)] = k_s[rows(d), :].T
        vt_s[:, rows(d)] = v_s[rows(d), :].T

    def one_head(head, top, last):
        slot = lax.rem(head, 2)
        top = jnp.max(top, axis=0, keepdims=True)
        if not last:
            make_query(head + 1)

        total, next_top = zero, lowest
        for d in range(tiles):
            p = jnp.exp2((s_s[slot, rows(d), :] - top) * exponent)
            a_s[slot, rows(d), :] = p
            total = fold(jnp.add, total, p)
            gw_s[slot, rows(d), :] = dot32(v_s[rows(d), :], go_ref[head], NT)
        inverse = 1.0 / jnp.sum(total, axis=0, keepdims=True)
        acc_s[...] = jnp.zeros_like(acc_s)

        dots = zero
        for d in range(tiles):
            w = a_s[slot, rows(d), :] * inverse
            w_half = w.astype(jnp.bfloat16)
            w_ref[head, rows(d), :] = w_half
            a = w * gw_s[slot, rows(d), :]
            gw_s[slot, rows(d), :] = a
            acc_s[...] += dot32(vt_s[:, rows(d)], w_half, NN)
            dots = fold(jnp.add, dots, a)
            if not last:
                next_top = scores(head + 1, 1 - slot, d, next_top)
        out_ref[:, lanes(head)] = acc_s[...].T.astype(jnp.bfloat16)
        dots = jnp.sum(dots, axis=0, keepdims=True) * inverse
        acc_s[...] = jnp.zeros_like(acc_s)

        for d in range(tiles):
            gs = (gw_s[slot, rows(d), :] - a_s[slot, rows(d), :] * dots).astype(jnp.bfloat16)
            gs_ref[head, rows(d), :] = gs
            acc_s[...] += dot32(kt_s[:, rows(d)], gs, NN)
        gq_t = (score_scale * acc_s[...]).astype(jnp.bfloat16)
        gq = (gq_t.astype(jnp.float32).T).astype(jnp.bfloat16)
        gq_ref[:, lanes(head)] = gq
        lr_s[...] += dot32(up_of(head), gq_t, NN)
        grad_up_ref[:, lanes(head)] = (adapter_scale * dot32(mpt, gq, NN)).astype(jnp.bfloat16)
        return next_top

    top = lax.fori_loop(0, heads - 1, lambda h, t: one_head(h, t, False), top)
    one_head(heads - 1, top, True)
    low_rank_ref[...] = lr_s[...].astype(jnp.bfloat16)


def attention(fq, go, up, low, rest):
    heads, tokens, _ = fq.shape
    ranks, width = up.shape
    span = (REACH + 1) * tokens
    vmem = pl.BlockSpec(memory_space=pltpu.VMEM)
    return pl.pallas_call(
        functools.partial(
            attention_kernel,
            tokens=tokens,
            heads=heads,
            score_scale=1.0 / math.sqrt(HEAD_SIZE),
        ),
        in_specs=[vmem] * (4 + len(rest)),
        out_specs=[vmem] * 7,
        scratch_shapes=[
            pltpu.VMEM((span, HEAD_SIZE), jnp.bfloat16),
            pltpu.VMEM((span, HEAD_SIZE), jnp.bfloat16),
            pltpu.VMEM((HEAD_SIZE, span), jnp.bfloat16),
            pltpu.VMEM((HEAD_SIZE, span), jnp.bfloat16),
            pltpu.VMEM((tokens, tokens), jnp.int32),
            pltpu.VMEM((2, span, tokens), jnp.float32),
            pltpu.VMEM((2, span, tokens), jnp.float32),
            pltpu.VMEM((2, span, tokens), jnp.float32),
            pltpu.VMEM((HEAD_SIZE, tokens), jnp.float32),
            pltpu.VMEM((ranks, tokens), jnp.float32),
        ],
        out_shape=[
            jax.ShapeDtypeStruct((tokens, width), jnp.bfloat16),
            jax.ShapeDtypeStruct((tokens, width), jnp.bfloat16),
            jax.ShapeDtypeStruct((ranks, tokens), jnp.bfloat16),
            jax.ShapeDtypeStruct((ranks, width), jnp.bfloat16),
            jax.ShapeDtypeStruct((heads, tokens, HEAD_SIZE), jnp.bfloat16),
            jax.ShapeDtypeStruct((heads, span, tokens), jnp.bfloat16),
            jax.ShapeDtypeStruct((heads, span, tokens), jnp.bfloat16),
        ],
        compiler_params=pltpu.CompilerParams(vmem_limit_bytes=24 << 20),
        cost_estimate=pl.CostEstimate(
            flops=8 * heads * tokens * span * HEAD_SIZE,
            bytes_accessed=8 << 20,
            transcendentals=heads * tokens * span,
        ),
        name="attention",
    )(fq, go, up, low, *rest)


def kv_half_kernel(w_ref, gs_ref, go_ref, q_ref, half_ref, *, keep, score_scale):
    heads, span, tokens = w_ref.shape
    values = (core_of() == 0) != keep

    def product(left_ref, right_ref, scale):
        right = jnp.concatenate([right_ref[h] for h in range(heads)], 0)
        for d in range(span // tokens):
            rows = pl.ds(d * tokens, tokens)
            left = jnp.concatenate([left_ref[h, rows, :] for h in range(heads)], 1)
            half_ref[rows, :] = (scale * dot32(left, right, NN)).astype(half_ref.dtype)

    @pl.when(values)
    def _():
        product(w_ref, go_ref, 1.0)

    @pl.when(jnp.logical_not(values))
    def _():
        product(gs_ref, q_ref, score_scale)


def kv_half(weights, grad_scores, go, queries, keep):
    span = weights.shape[1]
    vmem = pl.BlockSpec(memory_space=pltpu.VMEM)
    return pl.pallas_call(
        functools.partial(kv_half_kernel, keep=keep, score_scale=1.0 / math.sqrt(HEAD_SIZE)),
        in_specs=[vmem] * 4,
        out_specs=vmem,
        out_shape=jax.ShapeDtypeStruct((span, HEAD_SIZE), jnp.float32 if keep else jnp.bfloat16),
        compiler_params=pltpu.CompilerParams(vmem_limit_bytes=6 << 20),
        cost_estimate=pl.CostEstimate(
            flops=2 * span * queries.size, bytes_accessed=2 << 20, transcendentals=0
        ),
        name="kv_keep" if keep else "kv_send",
    )(weights, grad_scores, go, queries)


def pair_sum_kernel(keep_ref, got_ref, own_ref, one_ref, two_ref, *packs):
    tokens = own_ref.shape[0]

    def total(d):
        rows = pl.ds(d * tokens, tokens)
        return keep_ref[rows, :] + got_ref[rows, :].astype(jnp.float32)

    own_ref[...] = total(0)
    one_ref[...] = total(1)
    two_ref[...] = total(2)
    for n, pack_ref in enumerate(packs):
        pack_ref[0] = total(2 * n + 3).astype(jnp.bfloat16)
        pack_ref[1] = total(2 * n + 4).astype(jnp.bfloat16)


def pair_sum(keep, got, tokens):
    tile = (tokens, HEAD_SIZE)
    return pl.pallas_call(
        pair_sum_kernel,
        out_shape=[jax.ShapeDtypeStruct(tile, jnp.float32)] * 3
        + [jax.ShapeDtypeStruct((2,) + tile, jnp.bfloat16)] * (COLUMNS - 1),
        compiler_params=pltpu.CompilerParams(vmem_limit_bytes=12 << 20),
        name="pair_sum",
    )(keep, got)


def row_sum_kernel(own_ref, one_ref, two_ref, *rest):
    column = column_place()
    packs, (own_out, one_out, two_out) = rest[: COLUMNS - 1], rest[COLUMNS - 1 :]
    own, one, two = own_ref[...], one_ref[...], two_ref[...]
    for n, pack_ref in enumerate(packs):
        one = one + pack_ref[0].astype(jnp.float32)
        piece = pack_ref[1].astype(jnp.float32)
        near = jnp.full(piece.shape, n + 1, jnp.int32) + column < COLUMNS
        own = own + jnp.where(near, piece, 0.0)
        two = two + jnp.where(near, 0.0, piece)
    own_out[...] = own.astype(jnp.bfloat16)
    one_out[...] = one.astype(jnp.bfloat16)
    two_out[...] = two.astype(jnp.bfloat16)


def row_sum(own, one, two, packs):
    vmem = pl.BlockSpec(memory_space=pltpu.VMEM)
    return pl.pallas_call(
        row_sum_kernel,
        in_specs=[vmem] * (2 + COLUMNS),
        out_shape=[jax.ShapeDtypeStruct(own.shape, jnp.bfloat16)] * 3,
        compiler_params=pltpu.CompilerParams(vmem_limit_bytes=8 << 20),
        name="row_sum",
    )(own, one, two, *packs)


def spread_kernel(row_ref, out_ref):
    row = row_ref[...].astype(jnp.bfloat16)
    for n in range(out_ref.shape[0]):
        out_ref[n] = row


def spread(row, copies):
    return pl.pallas_call(
        spread_kernel,
        out_shape=jax.ShapeDtypeStruct((copies,) + row.shape, jnp.bfloat16),
        compiler_params=pltpu.CompilerParams(vmem_limit_bytes=4 << 20),
        name="spread",
    )(row)


def adam_kernel(got_ref, pd, md, vd, pu, mu, vu, keep_ref, opd, omd, ovd, opu, omu, ovu):
    groups = pd.shape[0]
    total = jnp.sum(got_ref[...].astype(jnp.float32), axis=0)
    grads = (total[:groups], total[groups:] * keep_ref[0, 0])
    for grad, p, m, v, op, om, ov in (
        (grads[0], pd, md, vd, opd, omd, ovd),
        (grads[1], pu, mu, vu, opu, omu, ovu),
    ):
        first = beta_one * m[...] + (1.0 - beta_one) * grad
        second = beta_two * v[...] + (1.0 - beta_two) * grad * grad
        op[...] = p[...] - learn_rate * first / (jnp.sqrt(second) + adam_epsilon)
        om[...] = first
        ov[...] = second


def on_device(
    frozen_queries,
    key_value_rows,
    output_gradient,
    inputs,
    adapter_down,
    down_first_moment,
    down_second_moment,
    adapter_up,
    up_first_moment,
    up_second_moment,
    rank_keep_mask,
    group_length,
    group_shift,
):
    tokens = frozen_queries.shape[0]
    width = frozen_queries.shape[1]
    model = inputs.shape[1]
    ctx = lax.axis_size("ctx")
    head_count = lax.axis_size("head")
    ctx_place = lax.axis_index("ctx")
    head_place = lax.axis_index("head")
    core = head_place % CORES
    kv_head = head_place // CORES
    key_width = KVH * HEAD_SIZE
    ranks = rank_keep_mask.shape[1]

    own_k = lax.dynamic_slice_in_dim(key_value_rows, kv_head * HEAD_SIZE, HEAD_SIZE, 1)
    own_v = lax.dynamic_slice_in_dim(key_value_rows, key_width + kv_head * HEAD_SIZE, HEAD_SIZE, 1)
    mine = lax.dynamic_slice_in_dim(
        key_value_rows, core * key_width + kv_head * HEAD_SIZE, HEAD_SIZE, 1
    )
    swap = [(h, h ^ 1) for h in range(head_count)]

    def along(piece, step):
        return lax.ppermute(piece, "ctx", [(i, (i + step) % ctx) for i in range(ctx)])

    def across(piece, step):
        pairs = [(i, i // COLUMNS * COLUMNS + (i + step) % COLUMNS) for i in range(ctx)]
        return lax.ppermute(piece, "ctx", pairs)

    one, two = along(mine, COLUMNS), along(mine, 2 * COLUMNS)

    down_rows, up_rows = model // 128, width // 128
    row = jnp.concatenate(
        [adapter_down.reshape(down_rows, 128), adapter_up.reshape(up_rows, 128)], 0
    )
    row = spread(row, ctx)
    gathered = lax.all_to_all(row, "ctx", split_axis=0, concat_axis=0)
    packs = pack(mine, one, two)
    far = across(packs[1], 2)
    direct = [one, two, across(packs[0], 1), far, across(packs[2], 3)]
    queries_in, grads_in = stage(frozen_queries, output_gradient)
    masks_in, low = bounds(group_length, group_shift, rank_keep_mask, tokens, tokens * ctx)
    swapped = [lax.ppermute(piece, "head", swap) for piece in direct]

    down = gathered[:, :down_rows].reshape(ranks, model)
    up = gathered[:, down_rows:].reshape(ranks, width)

    part = dot32(down, inputs, NT).astype(jnp.bfloat16)
    others = [[(h, h ^ k) for h in range(head_count)] for k in range(head_count - 1, 0, -1)]
    parts = [part] + [lax.ppermute(part, "head", pairs) for pairs in others]

    keep_masks = rank_keep_mask.astype(jnp.float32)[:, :, None]
    out, query_gradient, low_rank_part, grad_up_part, queries, weights, grad_scores = attention(
        queries_in,
        grads_in,
        up,
        low,
        [
            masks_in,
            own_k,
            own_v,
            *direct,
            *swapped,
            *parts,
        ],
    )

    low_parts = [low_rank_part] + [lax.ppermute(low_rank_part, "head", pairs) for pairs in others]
    send = kv_half(weights, grad_scores, grads_in, queries, keep=False)
    got = lax.ppermute(send, "head", swap)
    keep = kv_half(weights, grad_scores, grads_in, queries, keep=True)
    own_sum, one_sum, two_sum, *packs = pair_sum(keep, got, tokens)
    low_parts, grad_up_part, packs = lax.optimization_barrier((low_parts, grad_up_part, packs))
    low_total = sum(p.astype(jnp.float32) for p in low_parts)
    low_rank = (low_total * keep_masks[0] * adapter_scale).astype(jnp.bfloat16)
    grad_down_part = dot32(low_rank, inputs, NN).astype(jnp.bfloat16)
    packed = jnp.concatenate(
        [
            grad_down_part.reshape(ranks, down_rows // 4, 4, 128),
            grad_up_part.reshape(ranks, up_rows // 4, 4, 128),
        ],
        1,
    )
    received = lax.all_to_all(packed, "ctx", split_axis=0, concat_axis=0)

    packs = [across(p, -(n + 1)) for n, p in enumerate(packs)]
    own_sum, one_sum, two_sum = row_sum(own_sum, one_sum, two_sum, packs)

    def home(piece, back):
        pairs = [
            (
                i * head_count + h,
                (i - back) % ctx * head_count + (h % CORES) * CORES + h // CORES,
            )
            for i in range(ctx)
            for h in range(head_count)
        ]
        piece = lax.ppermute(piece, ("ctx", "head"), pairs)
        return piece.astype(jnp.float32)

    kv_grad = home(two_sum, 2 * COLUMNS) + home(one_sum, COLUMNS) + home(own_sum, 0)

    keep_row = lax.dynamic_slice_in_dim(keep_masks[1], ctx_place, 1, 0)
    small = [
        a.reshape(-1, 4, 128)
        for a in (
            adapter_down,
            down_first_moment,
            down_second_moment,
            adapter_up,
            up_first_moment,
            up_second_moment,
        )
    ]
    news = pl.pallas_call(
        adam_kernel,
        out_shape=[jax.ShapeDtypeStruct(a.shape, jnp.float32) for a in small],
        compiler_params=pltpu.CompilerParams(vmem_limit_bytes=8 << 20),
        name="adam",
    )(received, *small, keep_row)
    news = [n.reshape(1, -1) for n in news]
    return (out, query_gradient, kv_grad, *news)


def solution(mesh):
    both = P("ctx", "head")
    return jax.shard_map(
        on_device,
        mesh=mesh,
        in_specs=(both, P("ctx", None)) + (both,) * 8 + (P(), P(), P()),
        out_specs=(both,) * 9,
        check_vma=False,
    )
```
